32 devices in a mesh: dp: 16 (over z, y, x), mp: 2 (over core).
Axes of the slice: x: 2, y: 2, z: 4, core: 2. Of those that a mesh axis runs over, the one named last changes fastest.
Arguments:
- pixels: bfloat16 [16, 13, 256, 256], P('dp'), may hold values from -6 to 6
- band_count: int32 [16], P('dp'), may hold values from 1 to 13
- wavelengths: int32 [16, 13], P('dp'), may hold values from 40 to 249
- size_class: int32 [16], P('dp'), may hold values from 0 to 2
- token_keep: int32 [16, 256], P('dp'), may hold values 0 or 1
- hyp_attn: float32 [4, 128, 128], replicated, may hold values from -0.75 to 0.75
- hyp_mlp_in: float32 [128, 2048], replicated, may hold values from -0.5 to 0.5
- hyp_mlp_out: float32 [2048, 128], replicated, may hold values from -0.125 to 0.125
- hyp_gain: float32 [2, 128], replicated, may hold values from 0.5 to 1.5
- hyp_shift: float32 [2, 128], replicated, may hold values from -4 to 4
- bias_token: float32 [128], replicated, may hold values from -6 to 6
- kern_weight: float32 [128, 768, 256], P(None, 'dp'), may hold values from -0.009765625 to 0.009765625
- kern_bias: float32 [768, 256], P('dp'), may hold values from -0.125 to 0.125
- patch_bias_weight: float32 [128, 768], replicated, may hold values from -0.5 to 0.5
- norm_gain: float32 [2, 768], replicated, may hold values from 0.5 to 1.5
- norm_shift: float32 [2, 768], replicated, may hold values from -4 to 4
- attn_in: float32 [3, 768, 768], P(None, 'dp', 'mp'), may hold values from -0.21875 to 0.21875
- attn_in_bias: float32 [2, 768], P(None, 'mp'), may hold values from -4 to 4
- attn_out: float32 [768, 768], P('dp', 'mp'), may hold values from -0.625 to 0.625
- attn_out_bias: float32 [768], replicated, may hold values from -4 to 4
- mlp_in: float32 [768, 3072], P('dp', 'mp'), may hold values from -0.21875 to 0.21875
- mlp_in_bias: float32 [3072], P('mp'), may hold values from -4 to 4
- mlp_out: float32 [768, 3072], P('dp', 'mp'), may hold values from -0.109375 to 0.109375
- mlp_out_bias: float32 [768], replicated, may hold values from -4 to 4
- cotangent: bfloat16 [16, 256, 768], P('dp'), may hold values from -6 to 6
Outputs:
- layer_out: bfloat16 [16, 256, 768], P('dp')
- pixel_grad: bfloat16 [16, 13, 256, 256], P('dp')
- grad_hyp_attn: float32 [4, 128, 128], replicated
- grad_hyp_mlp_in: float32 [128, 2048], replicated
- grad_hyp_mlp_out: float32 [2048, 128], replicated
- grad_hyp_gain: float32 [2, 128], replicated
- grad_hyp_shift: float32 [2, 128], replicated
- grad_bias_token: float32 [128], replicated
- grad_kern_weight: float32 [128, 768, 256], P(None, 'dp')
- grad_kern_bias: float32 [768, 256], P('dp')
- grad_patch_bias_weight: float32 [128, 768], replicated
- grad_norm_gain: float32 [2, 768], replicated
- grad_norm_shift: float32 [2, 768], replicated
- grad_attn_in: float32 [3, 768, 768], P(None, 'dp', 'mp')
- grad_attn_in_bias: float32 [2, 768], P(None, 'mp')
- grad_attn_out: float32 [768, 768], P('dp', 'mp')
- grad_attn_out_bias: float32 [768], replicated
- grad_mlp_in: float32 [768, 3072], P('dp', 'mp')
- grad_mlp_in_bias: float32 [3072], P('mp')
- grad_mlp_out: float32 [768, 3072], P('dp', 'mp')
- grad_mlp_out_bias: float32 [768], replicated
The draws below stay inside these ranges and needn't reach their ends.
Inputs may be any that keep to these rules, and one draw needn't show every extreme that they name: Bands 0 to band_count[s] - 1 of slot s are present.
All inputs are finite; a program needn't handle non-finite values. No bound on the sum of `token_keep` on one device may be relied on, other than what follows from the above.
Results may differ from the reference program's by a relative error of at most 0.013.
Values may be sent and summed in bfloat16 or wider, within the bound.
A program may use at most 192 MiB of HBM per device.

```python
import math
import jax
import jax.numpy as jnp
from jax import lax

D = 768
HEADS = 12
HEAD_DIM = 64
FF = 3072
HYP_WIDTH = 128
HYP_HEADS = 4
HYP_FF = 2048
BANDS = 13
PATCH_PIX = 256
PATCHES = 256
SLOTS = 16


def with_ends(drawn, key, low, largest):
    extent = drawn.shape
    spot = [jax.random.randint(jax.random.fold_in(key, axis), (), 0, extent[axis]) for axis in range(len(extent))]
    drawn = drawn.at[tuple(spot)].set(low)
    longest = extent.index(max(extent))
    spot[longest] = (spot[longest] + 1) % extent[longest]
    return drawn.at[tuple(spot)].set(largest)


def with_spikes(entries, own_key, source, target, shards_of, factor):
    owner, partner = [(jnp.arange(entries.shape[dim]) // (entries.shape[dim] // shards_of)).reshape([-1 if axis == dim else 1 for axis in range(entries.ndim)]) for dim in (source, target)]
    chosen = jax.random.permutation(own_key, shards_of)[partner]
    strong = (owner == chosen) | (owner == (partner + shards_of // 2) % shards_of)
    return jnp.where(strong, factor * entries, entries)


def steps_of(rng, extent, split, least, top_value):
    def one(dim, parts):
        draws = jax.random.uniform(jax.random.fold_in(jax.random.fold_in(rng, 6), dim), (parts,), jnp.float32, least / len(split), top_value / len(split))
        return jnp.repeat(jnp.exp(draws), extent[dim] // parts).reshape((-1,) + (1,) * (len(extent) - dim - 1))

    level = one(*split[0])
    for cut in split[1:]:
        level = level * one(*cut)
    return level


def scatter_about(own_key, dims, scale, limit, cuts=(), kind=jnp.bfloat16):
    gain = steps_of(own_key, dims, cuts, -0.22, 0.18) if cuts else 1.0
    values = jax.random.normal(own_key, dims, jnp.float32) * scale * gain
    return jnp.minimum(jnp.maximum(values, -limit), limit).astype(kind)


def noise_with(stream_key, extent, deviation, limit, cuts, heavy, kind=jnp.bfloat16):
    values = deviation * jax.random.normal(stream_key, extent, jnp.float32)
    if cuts:
        values = values * steps_of(stream_key, extent, cuts, -0.22, 0.18)
    return jnp.clip(with_spikes(values, jax.random.fold_in(stream_key, 3), *heavy), -limit, limit).astype(kind)


def setup_inputs(seed: int = 0) -> dict:
    key_list = jax.random.split(jax.random.key(seed), 26)
    pixels = scatter_about(key_list[0], (SLOTS, BANDS, PATCHES, PATCH_PIX), 1.0, 6.0, ((0, 16),))
    band_count = with_ends(jax.random.randint(key_list[1], (SLOTS,), 1, BANDS + 1), jax.random.fold_in(key_list[1], 1), 1, BANDS).astype(jnp.int32)
    wavelengths = with_ends(jax.random.randint(key_list[2], (SLOTS, BANDS), 40, 250), jax.random.fold_in(key_list[2], 1), 40, 249).astype(jnp.int32)
    size_class = with_ends(jax.random.randint(key_list[3], (SLOTS,), 0, 3), jax.random.fold_in(key_list[3], 1), 0, 2).astype(jnp.int32)
    token_keep = with_ends((jax.random.randint(key_list[4], (SLOTS, PATCHES), 0, 8) < 7).astype(jnp.int32), jax.random.fold_in(key_list[4], 1), 0, 1)
    hyp_attn = scatter_about(key_list[5], (4, HYP_WIDTH, HYP_WIDTH), (HYP_WIDTH // 2) ** -0.5, 0.75, (), jnp.float32)
    hyp_mlp_in = scatter_about(key_list[6], (HYP_WIDTH, HYP_FF), HYP_WIDTH ** -0.5, 0.5, (), jnp.float32)
    hyp_mlp_out = scatter_about(key_list[7], (HYP_FF, HYP_WIDTH), HYP_FF ** -0.5, 0.125, (), jnp.float32)
    hyp_gain = jnp.clip(1.0 + 0.1 * jax.random.normal(key_list[8], (2, HYP_WIDTH), jnp.float32), 0.5, 1.5)
    hyp_shift = scatter_about(key_list[9], (2, HYP_WIDTH), 0.3, 4.0, (), jnp.float32)
    bias_token = scatter_about(key_list[10], (HYP_WIDTH,), 1.0, 6.0, (), jnp.float32)
    kern_weight = scatter_about(key_list[11], (HYP_WIDTH, D, PATCH_PIX), (HYP_WIDTH * BANDS * PATCH_PIX) ** -0.5, 0.009765625, ((1, 16),), jnp.float32)
    kern_bias = scatter_about(key_list[12], (D, PATCH_PIX), (0.5 / (BANDS * PATCH_PIX) ** 0.5), 0.125, ((0, 16),), jnp.float32)
    patch_bias_weight = scatter_about(key_list[13], (HYP_WIDTH, D), HYP_WIDTH ** -0.5, 0.5, (), jnp.float32)
    norm_gain = jnp.clip(1.0 + 0.1 * jax.random.normal(key_list[14], (2, D), jnp.float32), 0.5, 1.5)
    norm_shift = scatter_about(key_list[15], (2, D), 0.3, 4.0, (), jnp.float32)
    attn_in = scatter_about(key_list[16], (3, D, D), D ** -0.5, 0.21875, ((1, 16), (2, 2)), jnp.float32)
    attn_in_bias = scatter_about(key_list[17], (2, D), 0.3, 4.0, ((1, 2),), jnp.float32)
    attn_out = scatter_about(key_list[18], (D, D), (D // 8) ** -0.5, 0.625, ((0, 16), (1, 2)), jnp.float32)
    attn_out_bias = scatter_about(key_list[19], (D,), 0.3, 4.0, (), jnp.float32)
    mlp_in = scatter_about(key_list[20], (D, FF), D ** -0.5, 0.21875, ((0, 16), (1, 2)), jnp.float32)
    mlp_in_bias = scatter_about(key_list[21], (FF,), 0.3, 4.0, ((0, 2),), jnp.float32)
    mlp_out = scatter_about(key_list[22], (D, FF), FF ** -0.5, 0.109375, ((0, 16), (1, 2)), jnp.float32)
    mlp_out_bias = scatter_about(key_list[23], (D,), 0.3, 4.0, (), jnp.float32)
    cotangent = noise_with(key_list[24], (SLOTS, PATCHES, D), 1.0, 6.0, ((0, 16),), (0, 2, 16, 2.0))
    return {"pixels": pixels, "band_count": band_count, "wavelengths": wavelengths, "size_class": size_class, "token_keep": token_keep, "hyp_attn": hyp_attn, "hyp_mlp_in": hyp_mlp_in, "hyp_mlp_out": hyp_mlp_out, "hyp_gain": hyp_gain, "hyp_shift": hyp_shift, "bias_token": bias_token, "kern_weight": kern_weight, "kern_bias": kern_bias, "patch_bias_weight": patch_bias_weight, "norm_gain": norm_gain, "norm_shift": norm_shift, "attn_in": attn_in, "attn_in_bias": attn_in_bias, "attn_out": attn_out, "attn_out_bias": attn_out_bias, "mlp_in": mlp_in, "mlp_in_bias": mlp_in_bias, "mlp_out": mlp_out, "mlp_out_bias": mlp_out_bias, "cotangent": cotangent}


@jax.custom_vjp
def low(v):
    return lax.optimization_barrier(v.astype(jnp.bfloat16)).astype(jnp.float32)

@jax.custom_vjp
def low_back(v):
    return v

def low_keep(v):
    return (low(v), None)

def low_pass(kept, grad):
    return (grad,)

def back_keep(v):
    return (v, None)

def back_low(kept, grad):
    return (low(grad),)
low.defvjp(low_keep, low_pass)
low_back.defvjp(back_keep, back_low)

def exact_einsum(pattern, left_side, right_side):
    return jnp.einsum(pattern, left_side, right_side, precision=lax.Precision.HIGHEST, preferred_element_type=jnp.float32)

def norm_rows(values, gain_row, shift_row, epsilon):
    center = values - lax.optimization_barrier(jnp.mean(values, axis=-1, keepdims=True))
    spread = lax.optimization_barrier(jnp.mean(center * center, axis=-1, keepdims=True))
    return center * lax.rsqrt(spread + epsilon) * gain_row + shift_row

def exact_gelu(values):
    return jax.nn.gelu(values, approximate=False)

def wave_embedding(wavelengths, model_width):
    half_width = model_width // 2
    frequency = 10000.0 ** (-jnp.arange(half_width, dtype=jnp.float32) * 2.0 / model_width)
    angles = wavelengths.astype(jnp.float32)[..., None] * frequency
    return jnp.concatenate([jnp.sin(angles), jnp.cos(angles)], axis=-1)

def hyper_slot(embedding, band_valid, hyp_attn, hyp_mlp_in, hyp_mlp_out, hyp_gain, hyp_shift, bias_token):
    model_width = embedding.shape[-1]
    sequence = jnp.concatenate([embedding, bias_token[None, :]], axis=0)
    keys_valid = jnp.concatenate([band_valid, jnp.ones((1,), dtype=bool)])
    length = sequence.shape[0]
    head_size = model_width // HYP_HEADS
    query_rows = exact_einsum('te,ef->tf', sequence, hyp_attn[0]).reshape(length, HYP_HEADS, head_size)
    key_rows = exact_einsum('te,ef->tf', sequence, hyp_attn[1]).reshape(length, HYP_HEADS, head_size)
    value_rows = exact_einsum('te,ef->tf', sequence, hyp_attn[2]).reshape(length, HYP_HEADS, head_size)
    scores = exact_einsum('qhd,khd->hqk', query_rows, key_rows) * (1.0 / math.sqrt(head_size))
    scores = jnp.where(keys_valid[None, None, :], scores, -1e+30)
    weights = jax.nn.softmax(scores, axis=-1)
    mixed_rows = exact_einsum('hqk,khd->qhd', weights, value_rows).reshape(length, model_width)
    first_rows = norm_rows(sequence + exact_einsum('te,ef->tf', mixed_rows, hyp_attn[3]), hyp_gain[0], hyp_shift[0], 1e-05)
    inner_rows = exact_gelu(exact_einsum('te,ef->tf', first_rows, hyp_mlp_in))
    second_rows = norm_rows(first_rows + exact_einsum('tf,fe->te', inner_rows, hyp_mlp_out), hyp_gain[1], hyp_shift[1], 1e-05)
    return (second_rows[:-1] + embedding, second_rows[-1])

def reference(pixels, band_count, wavelengths, size_class, token_keep, hyp_attn, hyp_mlp_in, hyp_mlp_out, hyp_gain, hyp_shift, bias_token, kern_weight, kern_bias, patch_bias_weight, norm_gain, norm_shift, attn_in, attn_in_bias, attn_out, attn_out_bias, mlp_in, mlp_in_bias, mlp_out, mlp_out_bias, cotangent):
    embedding = wave_embedding(wavelengths, HYP_WIDTH)
    band_valid = jnp.arange(BANDS)[None, :] < band_count[:, None]
    live_rows = jnp.where(size_class == 0, PATCHES * 49 // 256, jnp.where(size_class == 1, PATCHES * 196 // 256, PATCHES))
    position = jnp.arange(PATCHES)
    row_valid = position[None, :] < live_rows[:, None]
    key_valid = row_valid & ((token_keep == 1) | (position[None, :] == 0))
    row_scale = row_valid.astype(jnp.float32)
    band_scale = band_valid.astype(jnp.float32)
    group_size = math.gcd(SLOTS, max(1, 4096 // PATCHES))
    score_scale = 1.0 / math.sqrt(HEAD_DIM)

    def forward(pixels_wide, hyp_attn, hyp_mlp_in, hyp_mlp_out, hyp_gain, hyp_shift, bias_token, kern_weight, kern_bias, patch_bias_weight, norm_gain, norm_shift, attn_in, attn_in_bias, attn_out, attn_out_bias, mlp_in, mlp_in_bias, mlp_out, mlp_out_bias):
        code_vals, tail_rows = jax.vmap(hyper_slot, in_axes=(0, 0, None, None, None, None, None, None))(embedding, band_valid, hyp_attn, hyp_mlp_in, hyp_mlp_out, hyp_gain, hyp_shift, bias_token)
        code_low = low(code_vals)
        patch_bias = exact_einsum('se,ec->sc', tail_rows, patch_bias_weight)
        kern_low = low(kern_weight)
        attn_in_low = low(attn_in)
        attn_out_low = low(attn_out)
        mlp_in_low = low(mlp_in)
        mlp_out_low = low(mlp_out)

        def group_block(inputs):
            group_codes, group_bias, group_pixels, group_bands, group_keys, group_rows = inputs
            count_here = group_codes.shape[0]
            head_shape = (count_here, PATCHES, HEADS, HEAD_DIM)
            kernel = exact_einsum('sbe,ecp->sbcp', group_codes, kern_low) + kern_bias
            kernel = low(low_back(kernel))
            masked = group_pixels * group_bands[:, :, None, None]
            embedded = low_back(exact_einsum('sbtp,sbcp->stc', masked, kernel) + group_bias[:, None, :])
            normed = low(norm_rows(embedded, norm_gain[0], norm_shift[0], 1e-06))
            query_rows = low(low_back(exact_einsum('std,de->ste', normed, attn_in_low[0]) + attn_in_bias[0]))
            key_rows = low(low_back(exact_einsum('std,de->ste', normed, attn_in_low[1])))
            value_rows = low(low_back(exact_einsum('std,de->ste', normed, attn_in_low[2]) + attn_in_bias[1]))
            scores = low_back(exact_einsum('sqhd,skhd->shqk', query_rows.reshape(head_shape), key_rows.reshape(head_shape)) * score_scale)
            scores = jnp.where(group_keys[:, None, None, :], scores, -1e+30)
            prob = jax.nn.softmax(scores, axis=-1)
            context = exact_einsum('shqk,skhd->sqhd', low(prob), value_rows.reshape(head_shape)).reshape(count_here, PATCHES, D)
            context = low(low_back(context))
            attended = low_back(exact_einsum('std,ed->ste', context, attn_out_low) + attn_out_bias)
            middle = embedded + attended
            normed_b = low(norm_rows(middle, norm_gain[1], norm_shift[1], 1e-06))
            pre_act = low_back(exact_einsum('std,df->stf', normed_b, mlp_in_low) + mlp_in_bias)
            activation = low(low_back(exact_gelu(pre_act)))
            branch = low_back(exact_einsum('stf,df->std', activation, mlp_out_low) + mlp_out_bias)
            return (middle + branch) * group_rows[:, :, None]
        saved_block = jax.checkpoint(group_block)

        def scan_step(scan_carry, inputs):
            return (scan_carry, saved_block(inputs))
        stacked = (code_low.reshape(-1, group_size, BANDS, HYP_WIDTH), patch_bias.reshape(-1, group_size, D), pixels_wide.reshape(-1, group_size, BANDS, PATCHES, PATCH_PIX), band_scale.reshape(-1, group_size, BANDS), key_valid.reshape(-1, group_size, PATCHES), row_scale.reshape(-1, group_size, PATCHES))
        outputs = lax.scan(scan_step, jnp.zeros((), jnp.float32), stacked)[1]
        return outputs.reshape(SLOTS, PATCHES, D)
    primals = (pixels.astype(jnp.float32), hyp_attn, hyp_mlp_in, hyp_mlp_out, hyp_gain, hyp_shift, bias_token, kern_weight, kern_bias, patch_bias_weight, norm_gain, norm_shift, attn_in, attn_in_bias, attn_out, attn_out_bias, mlp_in, mlp_in_bias, mlp_out, mlp_out_bias)
    result, backward = jax.vjp(forward, *primals)
    gradients = backward(cotangent.astype(jnp.float32))
    return (result.astype(jnp.bfloat16), gradients[0].astype(jnp.bfloat16), gradients[1], gradients[2], gradients[3], gradients[4], gradients[5], gradients[6], gradients[7], gradients[8], gradients[9], gradients[10], gradients[11], gradients[12], gradients[13], gradients[14], gradients[15], gradients[16], gradients[17], gradients[18], gradients[19])
```

```python
from functools import partial
import math

import jax
import jax.numpy as jnp
from jax import lax
from jax.experimental import pallas as pl
from jax.experimental.pallas import tpu as pltpu
from jax.sharding import PartitionSpec as P

HEAD_DIM = 64
HYP_HEADS = 4
MESH = pl.DeviceIdType.MESH
ANY = pl.BlockSpec(memory_space=pl.ANY)
VMEM = pl.BlockSpec(memory_space=pltpu.VMEM)
BIG_VMEM = 56 * 1024 * 1024

vit_epsilon = 1e-06
hyper_epsilon = 1e-05


def factors_of(n):
    return {16: (4, 2, 2), 128: (4, 8, 4)}.get(n, (n,))


def coords(me, grid):
    out = []
    for size in reversed(grid):
        out.append(lax.rem(me, size))
        me = me // size
    return out[::-1]


def device_at(position, grid, offset):
    index = 0
    for place, size, step in zip(position, grid, offset):
        index = index * size + (lax.rem(place + step, size) if step else place)
    return index


def offsets_in(grid, dims):
    out = [()]
    for dim, size in enumerate(grid):
        out = [o + (i,) for o in out for i in range(size if dim in dims else 1)]
    return out


def along(grid, dim, step):
    return tuple(step if d == dim else 0 for d in range(len(grid)))


def minus(a, b, grid):
    return tuple((i - j) % size for i, j, size in zip(a, b, grid))


def orders_of(grid):
    return [(0, 1, 2), (0, 2, 1)] if len(grid) == 3 else [tuple(range(len(grid)))]


def greet_all(n, me, mp, partner):
    sem = pltpu.get_barrier_semaphore()
    for k in range(1, n):
        pl.semaphore_signal(sem, inc=1, device_id=(lax.rem(me + k, n), mp), device_id_type=MESH)
    if partner:
        pl.semaphore_signal(sem, inc=1, device_id=(me, 1 - mp), device_id_type=MESH)
    pl.semaphore_wait(sem, n if partner else n - 1)


def remote(src, dst, send, recv, device):
    copy = pltpu.make_async_remote_copy(
        src_ref=src, dst_ref=dst, send_sem=send, recv_sem=recv, device_id=device, device_id_type=MESH
    )
    copy.start()
    return copy


def params(collective, limit=None):
    return pltpu.CompilerParams(collective_id=collective, has_side_effects=True, vmem_limit_bytes=limit)


def share_kernel(n, x_ref, o_ref, local, send, recv):
    me, mp = lax.axis_index("dp"), lax.axis_index("mp")
    greet_all(n, me, mp, False)
    own = pltpu.make_async_copy(x_ref, o_ref.at[me], local)
    own.start()
    copies = []
    for k in range(1, n):
        there = (lax.rem(me + k, n), mp)
        copies.append(remote(x_ref, o_ref.at[me], send.at[k - 1], recv.at[k - 1], there))
    own.wait()
    for copy in copies:
        copy.wait()


def share(x, n):
    return pl.pallas_call(
        partial(share_kernel, n),
        out_shape=jax.ShapeDtypeStruct((n,) + x.shape, x.dtype),
        in_specs=[VMEM],
        out_specs=VMEM,
        scratch_shapes=[
            pltpu.SemaphoreType.DMA,
            pltpu.SemaphoreType.DMA((n - 1,)),
            pltpu.SemaphoreType.DMA((n - 1,)),
        ],
        compiler_params=params(0),
        name="share",
    )(x)


def fetch_kernel(n, grid, direct, kern, attn, mlp, kern_o, attn_o, mlp_o, local, a_send, a_recv, g_send, g_recv):
    me, mp = lax.axis_index("dp"), lax.axis_index("mp")
    here = coords(me, grid)
    greet_all(n, me, mp, False)
    bands, rows = kern.shape[0] // n, kern.shape[1]
    orders = orders_of(grid)
    everyone = offsets_in(grid, range(len(grid)))
    index = {o: i for i, o in enumerate(everyone)}

    def kern_slot():
        if direct:
            return kern_o.at[:, pl.ds(pl.multiple_of(rows * me, 16), rows)]
        return kern_o.at[me]

    own = [
        pltpu.make_async_copy(kern.at[pl.ds(bands * me, bands)], kern_slot(), local.at[0]),
        pltpu.make_async_copy(attn, attn_o.at[me], local.at[1]),
        pltpu.make_async_copy(mlp, mlp_o.at[me], local.at[2]),
    ]
    pieces = []
    for src, dst in ((attn, attn_o), (mlp, mlp_o)):
        width = src.shape[1] // len(orders)
        for half, order in enumerate(orders):
            pieces.append((src, dst, pl.ds(half * width, width), order, len(pieces)))
    sends, count, seen = [], [0] * len(pieces), set()

    def send(piece, shard, step):
        src, dst, lanes, _, p = piece
        owner = device_at(here, grid, shard)
        there = device_at(here, grid, step)
        held = dst.at[owner, :, lanes] if any(shard) else src.at[:, lanes]
        slot = index[minus(shard, step, grid)]
        sends.append(
            remote(held, dst.at[owner, :, lanes], g_send.at[p, count[p]], g_recv.at[p, slot], (there, mp))
        )
        count[p] += 1

    def arrive(piece, shard):
        _, dst, lanes, _, p = piece
        if any(shard) and (p, shard) not in seen:
            seen.add((p, shard))
            block = dst.at[device_at(here, grid, shard), :, lanes]
            pltpu.make_async_copy(block, block, g_recv.at[p, index[shard]]).wait()

    def stage(number, piece):
        order = piece[3]
        for shard in sorted(offsets_in(grid, order[:number]), key=sum):
            arrive(piece, shard)
            for k in range(1, grid[order[number]]):
                send(piece, shard, along(grid, order[number], k))

    for piece in pieces:
        stage(0, piece)
    exchange = []
    for i, step in enumerate(sorted(everyone[1:], key=sum, reverse=True)):
        there = device_at(here, grid, step)
        exchange.append(
            remote(kern.at[pl.ds(bands * there, bands)], kern_slot(), a_send.at[i], a_recv.at[i], (there, mp))
        )
    for copy in own:
        copy.start()
    for number in range(1, len(grid)):
        for piece in pieces:
            stage(number, piece)
    for piece in pieces:
        for shard in everyone:
            arrive(piece, shard)
    for copy in sends:
        copy.wait_send()
    for copy in exchange:
        copy.wait()
    for copy in own:
        copy.wait()


def fetch(kern, attn, mlp, n):
    grid = factors_of(n)
    bands, (_, rows, pixels) = kern.shape[0] // n, kern.shape
    direct = rows % 16 == 0
    pieces = 2 * len(orders_of(grid))
    kern_shape = (bands, rows * n, pixels) if direct else (n, bands, rows, pixels)
    kernel, attn_all, mlp_all = pl.pallas_call(
        partial(fetch_kernel, n, grid, direct),
        out_shape=[
            jax.ShapeDtypeStruct(kern_shape, kern.dtype),
            jax.ShapeDtypeStruct((n,) + attn.shape, attn.dtype),
            jax.ShapeDtypeStruct((n,) + mlp.shape, mlp.dtype),
        ],
        in_specs=[ANY] * 3,
        out_specs=[ANY] * 3,
        scratch_shapes=[
            pltpu.SemaphoreType.DMA((3,)),
            pltpu.SemaphoreType.DMA((n - 1,)),
            pltpu.SemaphoreType.DMA((n - 1,)),
            pltpu.SemaphoreType.DMA((pieces, n - 1)),
            pltpu.SemaphoreType.DMA((pieces, n)),
        ],
        compiler_params=params(1),
        name="fetch",
    )(kern, attn, mlp)
    if not direct:
        kernel = kernel.transpose(1, 0, 2, 3).reshape(bands, rows * n, pixels)
    return kernel, attn_all.reshape(n * rows, -1), mlp_all.reshape(n * rows, -1)


def reduce_kernel(
    n, grid, direct, kern, attn, mlp, kern_o, attn_o, mlp_o,
    attn_sum, mlp_sum, attn_in, mlp_in, local, a_send, a_recv, f_send, f_recv, g_send, g_recv,
):
    me, mp = lax.axis_index("dp"), lax.axis_index("mp")
    here = coords(me, grid)
    greet_all(n, me, mp, True)
    rows, pixels = kern_o.shape[2], kern.shape[-1]
    depth = len(grid)
    orders = [order[::-1] for order in orders_of(grid)]
    everyone = offsets_in(grid, range(depth))
    half_lanes = pl.ds(pl.multiple_of(mp * pixels, pixels), pixels)

    def block_for(there):
        if direct:
            return kern.at[:, pl.ds(pl.multiple_of(rows * there, 16), rows)]
        return kern.at[there]

    pieces = []
    for src, acc, inbox, out in ((attn, attn_sum, attn_in, attn_o), (mlp, mlp_sum, mlp_in, mlp_o)):
        width = src.shape[2] // len(orders)
        for half, order in enumerate(orders):
            pieces.append((src, acc, inbox, out, pl.ds(half * width, width), order, len(pieces)))
    slots = {}
    for which, order in enumerate(orders):
        number = 0
        for t in range(depth):
            rest = sorted(offsets_in(grid, order[t + 1 :]), key=sum, reverse=True)
            for shard in rest:
                for k in range(1, grid[order[t]]):
                    slots[which, t, shard, k] = number
                    number += 1
    sends = []

    def send_stage(t, piece):
        src, acc, inbox, _, lanes, order, p = piece
        held = src if t == 0 else acc
        for shard in sorted(offsets_in(grid, order[t + 1 :]), key=sum, reverse=True):
            for k in range(1, grid[order[t]]):
                step = along(grid, order[t], k)
                target = tuple(i + j for i, j in zip(shard, step))
                owner = device_at(here, grid, target)
                slot = slots[p % len(orders), t, shard, grid[order[t]] - k]
                sends.append(
                    remote(
                        held.at[owner, :, lanes], inbox.at[slot, :, lanes],
                        g_send.at[p, slot], g_recv.at[p, slot], (device_at(here, grid, step), mp),
                    )
                )

    def add_stage(t, piece):
        src, acc, inbox, out, lanes, order, p = piece
        held = src if t == 0 else acc
        for shard in sorted(offsets_in(grid, order[t + 1 :]), key=sum, reverse=True):
            owner = device_at(here, grid, shard)
            total = held[owner, :, lanes].astype(jnp.float32)
            for k in range(1, grid[order[t]]):
                slot = slots[p % len(orders), t, shard, k]
                block = inbox.at[slot, :, lanes]
                pltpu.make_async_copy(block, block, g_recv.at[p, slot]).wait()
                total = total + inbox[slot, :, lanes].astype(jnp.float32)
            if t == depth - 1:
                out[:, lanes] = total
            else:
                acc[owner, :, lanes] = total.astype(acc.dtype)

    for piece in pieces:
        send_stage(0, piece)
    exchange = []
    far = sorted(everyone[1:], key=sum, reverse=True)
    for i, step in enumerate(far):
        there = device_at(here, grid, step)
        exchange.append(
            remote(
                block_for(there), kern_o.at[me, :, :, half_lanes], a_send.at[i], a_recv.at[i], (there, mp)
            )
        )
    own = pltpu.make_async_copy(block_for(me), kern_o.at[me, :, :, half_lanes], local)
    own.start()
    forwards = [
        remote(block_for(me), kern_o.at[me, :, :, half_lanes], f_send.at[n - 1], f_recv.at[n - 1], (me, 1 - mp))
    ]
    for t in range(depth):
        for piece in pieces:
            add_stage(t, piece)
            if t + 1 < depth:
                send_stage(t + 1, piece)
    for i in reversed(range(n - 1)):
        source = device_at(here, grid, minus((0,) * depth, far[i], grid))
        block = kern_o.at[source, :, :, half_lanes]
        exchange[i].wait_recv()
        forwards.append(remote(block, block, f_send.at[i], f_recv.at[i], (me, 1 - mp)))
    for copy in exchange:
        copy.wait_send()
    for copy in forwards:
        copy.wait()
    for copy in sends:
        copy.wait_send()
    own.wait()


def reduce(kern, attn, mlp, n, rows):
    grid = factors_of(n)
    bands, _, pixels = kern.shape
    direct = rows % 16 == 0
    if not direct:
        kern = kern.reshape(bands, n, rows, pixels).transpose(1, 0, 2, 3)
    pieces = 2 * len(orders_of(grid))
    return pl.pallas_call(
        partial(reduce_kernel, n, grid, direct),
        out_shape=[
            jax.ShapeDtypeStruct((n, bands, rows, 2 * pixels), kern.dtype),
            jax.ShapeDtypeStruct(attn.shape[1:], jnp.float32),
            jax.ShapeDtypeStruct(mlp.shape[1:], jnp.float32),
        ],
        in_specs=[ANY, VMEM, VMEM],
        out_specs=[ANY, VMEM, VMEM],
        scratch_shapes=[
            pltpu.VMEM(attn.shape, attn.dtype),
            pltpu.VMEM(mlp.shape, mlp.dtype),
            pltpu.VMEM((n - 1,) + attn.shape[1:], attn.dtype),
            pltpu.VMEM((n - 1,) + mlp.shape[1:], mlp.dtype),
            pltpu.SemaphoreType.DMA,
            pltpu.SemaphoreType.DMA((n - 1,)),
            pltpu.SemaphoreType.DMA((n - 1,)),
            pltpu.SemaphoreType.DMA((n,)),
            pltpu.SemaphoreType.DMA((n,)),
            pltpu.SemaphoreType.DMA((pieces, n - 1)),
            pltpu.SemaphoreType.DMA((pieces, n - 1)),
        ],
        compiler_params=params(2, BIG_VMEM),
        name="reduce",
    )(kern, attn, mlp)


def pair_kernel(steps, x_ref, o_ref, inbox, send, recv):
    me, mp = lax.axis_index("dp"), lax.axis_index("mp")
    there = (me, 1 - mp)
    sem = pltpu.get_barrier_semaphore()
    pl.semaphore_signal(sem, inc=1, device_id=there, device_id_type=MESH)
    pl.semaphore_wait(sem, 1)
    rows = x_ref.shape[0] // steps
    copies = []
    for i in range(steps):
        part = pl.ds(i * rows, rows)
        copies.append(remote(x_ref.at[part], inbox.at[part], send.at[i], recv.at[i], there))
    for i, copy in enumerate(copies):
        part = pl.ds(i * rows, rows)
        copy.wait_recv()
        total = x_ref[part].astype(jnp.float32) + inbox[part].astype(jnp.float32)
        o_ref[part] = total.astype(o_ref.dtype)
    for copy in copies:
        copy.wait_send()


def pair_sum(x):
    steps = 4
    return pl.pallas_call(
        partial(pair_kernel, steps),
        out_shape=jax.ShapeDtypeStruct(x.shape, x.dtype),
        in_specs=[VMEM],
        out_specs=VMEM,
        scratch_shapes=[
            pltpu.VMEM(x.shape, x.dtype),
            pltpu.SemaphoreType.DMA((steps,)),
            pltpu.SemaphoreType.DMA((steps,)),
        ],
        compiler_params=params(3 if x.dtype == jnp.float32 else 5),
        name="pair_sum",
    )(x)


def total_kernel(n, x_ref, o_ref, inbox, send, recv, back_send, back_recv):
    me, mp = lax.axis_index("dp"), lax.axis_index("mp")
    greet_all(n, me, mp, False)
    copies = []
    for k in range(1, n):
        there = lax.rem(me + k, n)
        copies.append(remote(x_ref.at[there], inbox.at[k - 1], send.at[k - 1], recv.at[k - 1], (there, mp)))
    total = x_ref[me]
    for k, copy in enumerate(copies):
        copy.wait_recv()
        total = total + inbox[k]
    o_ref[me] = total
    for k in range(1, n):
        there = lax.rem(me + k, n)
        copies.append(remote(o_ref.at[me], o_ref.at[me], back_send.at[k - 1], back_recv.at[k - 1], (there, mp)))
    for copy in copies[: n - 1]:
        copy.wait_send()
    for copy in copies[n - 1 :]:
        copy.wait()


def total_over_slots(x, n):
    return pl.pallas_call(
        partial(total_kernel, n),
        out_shape=jax.ShapeDtypeStruct(x.shape, x.dtype),
        in_specs=[VMEM],
        out_specs=VMEM,
        scratch_shapes=[pltpu.VMEM((n - 1,) + x.shape[1:], x.dtype)] + [pltpu.SemaphoreType.DMA((n - 1,))] * 4,
        compiler_params=params(4),
        name="total",
    )(x)


def exact_einsum(pattern, left_side, right_side):
    return jnp.einsum(
        pattern,
        left_side,
        right_side,
        precision=lax.Precision.HIGHEST,
        preferred_element_type=jnp.float32,
    )


def fast_einsum(pattern, left_side, right_side):
    return jnp.einsum(pattern, left_side, right_side, preferred_element_type=jnp.float32)


def norm_rows(values, gain_row, shift_row, epsilon):
    center = values - jnp.mean(values, axis=-1, keepdims=True)
    spread = jnp.mean(center * center, axis=-1, keepdims=True)
    return center * lax.rsqrt(spread + epsilon) * gain_row + shift_row


def exact_gelu(values):
    return jax.nn.gelu(values, approximate=False)


def wave_embedding(wavelengths, model_width):
    half_width = model_width // 2
    frequency = 10000.0 ** (-jnp.arange(half_width, dtype=jnp.float32) * 2.0 / model_width)
    angles = wavelengths.astype(jnp.float32)[..., None] * frequency
    return jnp.concatenate([jnp.sin(angles), jnp.cos(angles)], axis=-1)


def hyper_all(
    embedding, band_valid, hyp_attn, hyp_mlp_in, hyp_mlp_out, hyp_gain, hyp_shift, bias_token, bias_w
):
    slots, bands, width = embedding.shape
    length, head_size = bands + 1, width // HYP_HEADS
    sequence = jnp.concatenate([embedding, jnp.broadcast_to(bias_token, (slots, 1, width))], axis=1)
    keys_valid = jnp.concatenate([band_valid, jnp.ones((slots, 1), dtype=bool)], axis=1)
    heads = (slots, length, HYP_HEADS, head_size)
    query_rows = exact_einsum("ste,ef->stf", sequence, hyp_attn[0]).reshape(heads)
    key_rows = exact_einsum("ste,ef->stf", sequence, hyp_attn[1]).reshape(heads)
    value_rows = exact_einsum("ste,ef->stf", sequence, hyp_attn[2]).reshape(heads)
    scores = exact_einsum("sqhd,skhd->shqk", query_rows, key_rows) * (1.0 / math.sqrt(head_size))
    scores = jnp.where(keys_valid[:, None, None, :], scores, -1e30)
    weights = jax.nn.softmax(scores, axis=-1)
    mixed_rows = exact_einsum("shqk,skhd->sqhd", weights, value_rows).reshape(slots, length, width)
    first_rows = norm_rows(
        sequence + exact_einsum("ste,ef->stf", mixed_rows, hyp_attn[3]),
        hyp_gain[0],
        hyp_shift[0],
        hyper_epsilon,
    )
    inner_rows = exact_gelu(exact_einsum("ste,ef->stf", first_rows, hyp_mlp_in))
    second_rows = norm_rows(
        first_rows + exact_einsum("stf,fe->ste", inner_rows, hyp_mlp_out),
        hyp_gain[1],
        hyp_shift[1],
        hyper_epsilon,
    )
    return second_rows[:, :-1] + embedding, exact_einsum("se,ec->sc", second_rows[:, -1], bias_w)


def per_device(
    n,
    pixels,
    band_count,
    wavelengths,
    size_class,
    token_keep,
    hyp_attn,
    hyp_mlp_in,
    hyp_mlp_out,
    hyp_gain,
    hyp_shift,
    bias_token,
    kern_weight,
    kern_bias,
    patch_bias_weight,
    norm_gain,
    norm_shift,
    attn_in,
    attn_in_bias,
    attn_out,
    attn_out_bias,
    mlp_in,
    mlp_in_bias,
    mlp_out,
    mlp_out_bias,
    cotangent,
):
    me, mp = lax.axis_index("dp"), lax.axis_index("mp")
    slot_count, band_total, tokens, pix_size = pixels.shape
    model_width = norm_gain.shape[1]
    hyper_width, rows, _ = kern_weight.shape
    half = pix_size // 2
    low = jnp.bfloat16

    facts = jnp.concatenate([wavelengths[0], band_count])
    facts = jnp.broadcast_to(jnp.pad(facts, (0, 128 - band_total - 1)), (8, 128))
    facts = share(facts, n)[:, 0]
    embedding = wave_embedding(facts[:, :band_total], hyper_width)
    every_band = jnp.arange(band_total)[None, :] < facts[:, band_total][:, None]
    (code_vals, patch_bias), hyper_back = jax.vjp(
        partial(hyper_all, embedding, every_band),
        hyp_attn,
        hyp_mlp_in,
        hyp_mlp_out,
        hyp_gain,
        hyp_shift,
        bias_token,
        patch_bias_weight,
    )
    all_codes = code_vals.astype(low).reshape(n * band_total, hyper_width)
    patch_bias = lax.dynamic_slice_in_dim(patch_bias, me, 1, 0)

    kern_low = kern_weight.astype(low)
    half_weight = lax.dynamic_slice_in_dim(kern_low, mp * half, half, 2)
    half_bias = lax.dynamic_slice_in_dim(kern_bias, mp * half, half, 1)
    half_kernels = (fast_einsum("ne,ecp->ncp", all_codes, half_weight) + half_bias).astype(low)

    inner = attn_in.shape[2]
    units = mlp_in.shape[1]
    attn_shard = jnp.concatenate([attn_in[0], attn_in[1], attn_in[2], attn_out], axis=1).astype(low)
    mlp_shard = jnp.concatenate([mlp_in, mlp_out], axis=1).astype(low)
    kernel, attn_all, mlp_all = fetch(half_kernels, attn_shard, mlp_shard, n)
    weight_qkv, weight_out = attn_all[:, : 3 * inner], attn_all[:, 3 * inner :]
    weight_up, weight_down = mlp_all[:, :units], mlp_all[:, units:]

    band_valid = jnp.arange(band_total) < band_count[0]
    live_rows = jnp.where(
        size_class[0] == 0, tokens * 49 // 256, jnp.where(size_class[0] == 1, tokens * 196 // 256, tokens)
    )
    position = jnp.arange(tokens)
    row_valid = position < live_rows
    key_valid = row_valid & ((token_keep[0] == 1) | (position == 0))
    row_scale = row_valid.astype(jnp.float32)[:, None]
    half_pixels = lax.dynamic_slice_in_dim(pixels[0], mp * half, half, 2)
    masked_pixels = half_pixels * band_valid.astype(low)[:, None, None]

    embedded = pair_sum(fast_einsum("btp,bcp->tc", masked_pixels, kernel)) + patch_bias

    local_heads = inner // HEAD_DIM
    head_grid = (tokens, local_heads, HEAD_DIM)
    score_scale = 1.0 / math.sqrt(HEAD_DIM)
    key_open = key_valid[None, None, :]
    norm_one = partial(norm_rows, epsilon=vit_epsilon)
    normed_a, first_back = jax.vjp(norm_one, embedded, norm_gain[0], norm_shift[0])
    normed_a = normed_a.astype(low)
    input_bias = jnp.concatenate([attn_in_bias[0], jnp.zeros_like(attn_in_bias[0]), attn_in_bias[1]])
    projected = (fast_einsum("nd,de->ne", normed_a, weight_qkv) + input_bias).astype(low)
    query_rows = projected[:, :inner].reshape(head_grid)
    key_rows = projected[:, inner : 2 * inner].reshape(head_grid)
    value_rows = projected[:, 2 * inner :].reshape(head_grid)
    scores = jnp.where(key_open, fast_einsum("qhd,khd->hqk", query_rows, key_rows) * score_scale, -1e30)
    row_peak = jnp.max(scores, axis=-1, keepdims=True)
    exp_scores = jnp.exp(scores - row_peak)
    prob_full = exp_scores / jnp.sum(exp_scores, axis=-1, keepdims=True)
    prob_low = prob_full.astype(low)
    context = fast_einsum("hqk,khd->qhd", prob_low, value_rows).reshape(tokens, inner).astype(low)
    middle = embedded + pair_sum(fast_einsum("ne,de->nd", context, weight_out)) + attn_out_bias
    normed_b, second_back = jax.vjp(norm_one, middle, norm_gain[1], norm_shift[1])
    normed_b = normed_b.astype(low)
    pre_act = fast_einsum("nd,df->nf", normed_b, weight_up) + mlp_in_bias
    activation, gelu_back = jax.vjp(exact_gelu, pre_act)
    activation = activation.astype(low)
    unit_part = fast_einsum("nf,df->nd", activation, weight_down).astype(low)
    final_rows = (middle + pair_sum(unit_part).astype(jnp.float32) + mlp_out_bias) * row_scale
    layer_out = final_rows.astype(low)[None]

    out_grad = cotangent[0].astype(jnp.float32) * row_scale
    out_grad_low = out_grad.astype(low)
    grad_mlp_out_bias = jnp.sum(out_grad, axis=0)
    grad_down = fast_einsum("nd,nf->df", out_grad_low, activation)
    act_grad = fast_einsum("nd,df->nf", out_grad_low, weight_down).astype(low)
    pre_grad = gelu_back(act_grad.astype(jnp.float32))[0].astype(low)
    grad_mlp_in_bias = jnp.sum(pre_grad, axis=0, dtype=jnp.float32)
    grad_up = fast_einsum("nd,nf->df", normed_b, pre_grad)
    second_part = fast_einsum("nf,df->nd", pre_grad, weight_up)
    middle_in, gain_second, shift_second = second_back(pair_sum(second_part))
    middle_grad = out_grad + middle_in
    attended_grad = middle_grad.astype(low)
    grad_attn_out_bias = jnp.sum(attended_grad, axis=0, dtype=jnp.float32)
    grad_proj = fast_einsum("nd,ne->de", attended_grad, context)
    context_grad = fast_einsum("nd,de->ne", attended_grad, weight_out).astype(low).reshape(head_grid)
    prob_grad = fast_einsum("qhd,khd->hqk", context_grad, value_rows)
    row_inner = jnp.sum(prob_full * prob_grad, axis=-1, keepdims=True)
    score_grad = (prob_full * (prob_grad - row_inner)).astype(low)
    query_grad = fast_einsum("hqk,khd->qhd", score_grad, key_rows) * score_scale
    key_grad = fast_einsum("hqk,qhd->khd", score_grad, query_rows) * score_scale
    value_grad = fast_einsum("hqk,qhd->khd", prob_low, context_grad)
    qkv_grad = jnp.concatenate(
        [g.reshape(tokens, inner).astype(low) for g in (query_grad, key_grad, value_grad)], axis=1
    )
    bias_sums = jnp.sum(qkv_grad, axis=0, dtype=jnp.float32)
    grad_in = fast_einsum("nd,ne->de", normed_a, qkv_grad)
    first_part = fast_einsum("ne,de->nd", qkv_grad, weight_qkv)
    embed_in, gain_first, shift_first = first_back(pair_sum(first_part))
    embed_grad = (middle_grad + embed_in).astype(low)
    patch_bias_grad = jnp.sum(embed_grad, axis=0, dtype=jnp.float32)

    half_grad = fast_einsum("tc,btp->bcp", embed_grad, masked_pixels).astype(low)
    attn_grads = jnp.concatenate([grad_in.astype(low), grad_proj.astype(low)], axis=1).reshape(n, rows, -1)
    mlp_grads = jnp.concatenate([grad_up.astype(low), grad_down.astype(low)], axis=1).reshape(n, rows, -1)
    local_grad, attn_sum, mlp_sum = reduce(half_grad, attn_grads, mlp_grads, n, rows)
    local_grad = local_grad.reshape(n * band_total, rows, pix_size)
    grad_attn_in = jnp.stack([attn_sum[:, i * inner : (i + 1) * inner] for i in range(3)])
    grad_attn_out = attn_sum[:, 3 * inner :]
    grad_mlp_in, grad_mlp_out = mlp_sum[:, :units], mlp_sum[:, units:]

    code_part = fast_einsum("ncp,ecp->ne", local_grad, kern_low).reshape(n, band_total, hyper_width)

    small = (
        gain_first,
        gain_second,
        shift_first,
        shift_second,
        bias_sums[:inner],
        bias_sums[2 * inner :],
        grad_attn_out_bias,
        grad_mlp_in_bias,
        grad_mlp_out_bias,
    )
    flat = jnp.concatenate([v.reshape(-1) for v in small])
    lanes = 128
    per_slot = -(-flat.size // (n * lanes))
    flat = jnp.pad(flat, (0, n * per_slot * lanes - flat.size)).reshape(n, per_slot, lanes)
    patch_rows = patch_bias_grad.reshape(1, -1, lanes) * (jnp.arange(n) == me).astype(jnp.float32)[:, None, None]
    packed = jnp.concatenate([code_part, patch_rows, flat], axis=1)
    used = packed.shape[1]
    packed = jnp.pad(packed, ((0, 0), (0, -used % 8), (0, 0)))
    packed = total_over_slots(packed, n)
    code_grad = packed[:, :band_total]
    patch_grad = packed[:, band_total : band_total + model_width // lanes].reshape(n, model_width)
    flat = packed[:, used - per_slot : used].reshape(-1)
    split = []
    start = 0
    for v in small:
        split.append(flat[start : start + v.size])
        start += v.size
    hyper_grads = hyper_back((code_grad, patch_grad))

    pixel_half = fast_einsum("tc,bcp->btp", embed_grad, kernel) * band_valid.astype(jnp.float32)[:, None, None]
    pixel_grad = lax.all_gather(pixel_half.astype(low), "mp", axis=2, tiled=True)[None]
    grad_kern_weight = fast_einsum("ne,ncp->ecp", all_codes, local_grad)
    grad_kern_bias = jnp.sum(local_grad, axis=0, dtype=jnp.float32)
    return (
        layer_out,
        pixel_grad,
        hyper_grads[0],
        hyper_grads[1],
        hyper_grads[2],
        hyper_grads[3],
        hyper_grads[4],
        hyper_grads[5],
        grad_kern_weight,
        grad_kern_bias,
        hyper_grads[6],
        jnp.stack([split[0], split[1]]),
        jnp.stack([split[2], split[3]]),
        grad_attn_in,
        jnp.stack([split[4], split[5]]),
        grad_attn_out,
        split[6],
        grad_mlp_in,
        split[7],
        grad_mlp_out,
        split[8],
    )


def solution(mesh):
    return jax.shard_map(
        partial(per_device, mesh.shape["dp"]),
        mesh=mesh,
        in_specs=(
            P("dp", None, None, None),
            P("dp"),
            P("dp", None),
            P("dp"),
            P("dp", None),
            P(),
            P(),
            P(),
            P(),
            P(),
            P(),
            P(None, "dp", None),
            P("dp", None),
            P(),
            P(),
            P(),
            P(None, "dp", "mp"),
            P(None, "mp"),
            P("dp", "mp"),
            P(),
            P("dp", "mp"),
            P("mp"),
            P("dp", "mp"),
            P(),
            P("dp", None, None),
        ),
        out_specs=(
            P("dp", None, None),
            P("dp", None, None, None),
            P(),
            P(),
            P(),
            P(),
            P(),
            P(),
            P(None, "dp", None),
            P("dp", None),
            P(),
            P(),
            P(),
            P(None, "dp", "mp"),
            P(None, "mp"),
            P("dp", "mp"),
            P(),
            P("dp", "mp"),
            P("mp"),
            P("dp", "mp"),
            P(),
        ),
        check_vma=False,
    )
```

```python
from functools import partial
import math

import jax
import jax.numpy as jnp
from jax import lax
from jax.experimental import pallas as pl
from jax.experimental.pallas import tpu as pltpu
from jax.sharding import PartitionSpec as P

HEAD_DIM = 64
HYP_HEADS = 4
MESH = pl.DeviceIdType.MESH
ANY = pl.BlockSpec(memory_space=pl.ANY)
VMEM = pl.BlockSpec(memory_space=pltpu.VMEM)
BIG_VMEM = 56 * 1024 * 1024

vit_epsilon = 1e-06
hyper_epsilon = 1e-05


def factors_of(n):
    return {16: (4, 2, 2), 128: (4, 8, 4)}.get(n, (n,))


def coords(me, grid):
    out = []
    for size in reversed(grid):
        out.append(lax.rem(me, size))
        me = me // size
    return out[::-1]


def device_at(position, grid, offset):
    index = 0
    for place, size, step in zip(position, grid, offset):
        index = index * size + (lax.rem(place + step, size) if step else place)
    return index


def offsets_in(grid, dims):
    out = [()]
    for dim, size in enumerate(grid):
        out = [o + (i,) for o in out for i in range(size if dim in dims else 1)]
    return out


def along(grid, dim, step):
    return tuple(step if d == dim else 0 for d in range(len(grid)))


def minus(a, b, grid):
    return tuple((i - j) % size for i, j, size in zip(a, b, grid))


def orders_of(grid):
    return [(0, 1, 2), (0, 2, 1)] if len(grid) == 3 else [tuple(range(len(grid)))]


def greet_all(n, me, mp, partner):
    sem = pltpu.get_barrier_semaphore()
    for k in range(1, n):
        pl.semaphore_signal(sem, inc=1, device_id=(lax.rem(me + k, n), mp), device_id_type=MESH)
    if partner:
        pl.semaphore_signal(sem, inc=1, device_id=(me, 1 - mp), device_id_type=MESH)
    pl.semaphore_wait(sem, n if partner else n - 1)


def remote(src, dst, send, recv, device):
    copy = pltpu.make_async_remote_copy(
        src_ref=src, dst_ref=dst, send_sem=send, recv_sem=recv, device_id=device, device_id_type=MESH
    )
    copy.start()
    return copy


def params(collective, limit=None):
    return pltpu.CompilerParams(collective_id=collective, has_side_effects=True, vmem_limit_bytes=limit)


def share_kernel(n, x_ref, o_ref, local, send, recv):
    me, mp = lax.axis_index("dp"), lax.axis_index("mp")
    greet_all(n, me, mp, False)
    own = pltpu.make_async_copy(x_ref, o_ref.at[me], local)
    own.start()
    copies = []
    for k in range(1, n):
        there = (lax.rem(me + k, n), mp)
        copies.append(remote(x_ref, o_ref.at[me], send.at[k - 1], recv.at[k - 1], there))
    own.wait()
    for copy in copies:
        copy.wait()


def share(x, n):
    return pl.pallas_call(
        partial(share_kernel, n),
        out_shape=jax.ShapeDtypeStruct((n,) + x.shape, x.dtype),
        in_specs=[VMEM],
        out_specs=VMEM,
        scratch_shapes=[
            pltpu.SemaphoreType.DMA,
            pltpu.SemaphoreType.DMA((n - 1,)),
            pltpu.SemaphoreType.DMA((n - 1,)),
        ],
        compiler_params=params(0),
        name="share",
    )(x)


def fetch_kernel(n, grid, direct, kern, attn, mlp, kern_o, attn_o, mlp_o, local, a_send, a_recv, g_send, g_recv):
    me, mp = lax.axis_index("dp"), lax.axis_index("mp")
    here = coords(me, grid)
    greet_all(n, me, mp, False)
    bands, rows = kern.shape[0] // n, kern.shape[1]
    orders = orders_of(grid)
    everyone = offsets_in(grid, range(len(grid)))
    index = {o: i for i, o in enumerate(everyone)}

    def kern_slot():
        if direct:
            return kern_o.at[:, pl.ds(pl.multiple_of(rows * me, 16), rows)]
        return kern_o.at[me]

    own = [
        pltpu.make_async_copy(kern.at[pl.ds(bands * me, bands)], kern_slot(), local.at[0]),
        pltpu.make_async_copy(attn, attn_o.at[me], local.at[1]),
        pltpu.make_async_copy(mlp, mlp_o.at[me], local.at[2]),
    ]
    pieces = []
    for src, dst in ((attn, attn_o), (mlp, mlp_o)):
        width = src.shape[1] // len(orders)
        for half, order in enumerate(orders):
            pieces.append((src, dst, pl.ds(half * width, width), order, len(pieces)))
    sends, count, seen = [], [0] * len(pieces), set()

    def send(piece, shard, step):
        src, dst, lanes, _, p = piece
        owner = device_at(here, grid, shard)
        there = device_at(here, grid, step)
        held = dst.at[owner, :, lanes] if any(shard) else src.at[:, lanes]
        slot = index[minus(shard, step, grid)]
        sends.append(
            remote(held, dst.at[owner, :, lanes], g_send.at[p, count[p]], g_recv.at[p, slot], (there, mp))
        )
        count[p] += 1

    def arrive(piece, shard):
        _, dst, lanes, _, p = piece
        if any(shard) and (p, shard) not in seen:
            seen.add((p, shard))
            block = dst.at[device_at(here, grid, shard), :, lanes]
            pltpu.make_async_copy(block, block, g_recv.at[p, index[shard]]).wait()

    def stage(number, piece):
        order = piece[3]
        for shard in sorted(offsets_in(grid, order[:number]), key=sum):
            arrive(piece, shard)
            for k in range(1, grid[order[number]]):
                send(piece, shard, along(grid, order[number], k))

    for piece in pieces:
        stage(0, piece)
    exchange = []
    for i, step in enumerate(sorted(everyone[1:], key=sum, reverse=True)):
        there = device_at(here, grid, step)
        exchange.append(
            remote(kern.at[pl.ds(bands * there, bands)], kern_slot(), a_send.at[i], a_recv.at[i], (there, mp))
        )
    for copy in own:
        copy.start()
    for number in range(1, len(grid)):
        for piece in pieces:
            stage(number, piece)
    for piece in pieces:
        for shard in everyone:
            arrive(piece, shard)
    for copy in sends:
        copy.wait_send()
    for copy in exchange:
        copy.wait()
    for copy in own:
        copy.wait()


def fetch(kern, attn, mlp, n):
    grid = factors_of(n)
    bands, (_, rows, pixels) = kern.shape[0] // n, kern.shape
    direct = rows % 16 == 0
    pieces = 2 * len(orders_of(grid))
    kern_shape = (bands, rows * n, pixels) if direct else (n, bands, rows, pixels)
    kernel, attn_all, mlp_all = pl.pallas_call(
        partial(fetch_kernel, n, grid, direct),
        out_shape=[
            jax.ShapeDtypeStruct(kern_shape, kern.dtype),
            jax.ShapeDtypeStruct((n,) + attn.shape, attn.dtype),
            jax.ShapeDtypeStruct((n,) + mlp.shape, mlp.dtype),
        ],
        in_specs=[ANY] * 3,
        out_specs=[ANY] * 3,
        scratch_shapes=[
            pltpu.SemaphoreType.DMA((3,)),
            pltpu.SemaphoreType.DMA((n - 1,)),
            pltpu.SemaphoreType.DMA((n - 1,)),
            pltpu.SemaphoreType.DMA((pieces, n - 1)),
            pltpu.SemaphoreType.DMA((pieces, n)),
        ],
        compiler_params=params(1),
        name="fetch",
    )(kern, attn, mlp)
    if not direct:
        kernel = kernel.transpose(1, 0, 2, 3).reshape(bands, rows * n, pixels)
    return kernel, attn_all.reshape(n * rows, -1), mlp_all.reshape(n * rows, -1)


def reduce_kernel(
    n, grid, direct, kern, attn, mlp, kern_o, attn_o, mlp_o,
    attn_sum, mlp_sum, attn_in, mlp_in, local, a_send, a_recv, f_send, f_recv, g_send, g_recv,
):
    me, mp = lax.axis_index("dp"), lax.axis_index("mp")
    here = coords(me, grid)
    greet_all(n, me, mp, True)
    rows, pixels = kern_o.shape[2], kern.shape[-1]
    depth = len(grid)
    orders = [order[::-1] for order in orders_of(grid)]
    everyone = offsets_in(grid, range(depth))
    half_lanes = pl.ds(pl.multiple_of(mp * pixels, pixels), pixels)

    def block_for(there):
        if direct:
            return kern.at[:, pl.ds(pl.multiple_of(rows * there, 16), rows)]
        return kern.at[there]

    pieces = []
    for src, acc, inbox, out in ((attn, attn_sum, attn_in, attn_o), (mlp, mlp_sum, mlp_in, mlp_o)):
        width = src.shape[2] // len(orders)
        for half, order in enumerate(orders):
            pieces.append((src, acc, inbox, out, pl.ds(half * width, width), order, len(pieces)))
    slots = {}
    for which, order in enumerate(orders):
        number = 0
        for t in range(depth):
            rest = sorted(offsets_in(grid, order[t + 1 :]), key=sum, reverse=True)
            for shard in rest:
                for k in range(1, grid[order[t]]):
                    slots[which, t, shard, k] = number
                    number += 1
    sends = []

    def send_stage(t, piece):
        src, acc, inbox, _, lanes, order, p = piece
        held = src if t == 0 else acc
        for shard in sorted(offsets_in(grid, order[t + 1 :]), key=sum, reverse=True):
            for k in range(1, grid[order[t]]):
                step = along(grid, order[t], k)
                target = tuple(i + j for i, j in zip(shard, step))
                owner = device_at(here, grid, target)
                slot = slots[p % len(orders), t, shard, grid[order[t]] - k]
                sends.append(
                    remote(
                        held.at[owner, :, lanes], inbox.at[slot, :, lanes],
                        g_send.at[p, slot], g_recv.at[p, slot], (device_at(here, grid, step), mp),
                    )
                )

    def add_stage(t, piece):
        src, acc, inbox, out, lanes, order, p = piece
        held = src if t == 0 else acc
        for shard in sorted(offsets_in(grid, order[t + 1 :]), key=sum, reverse=True):
            owner = device_at(here, grid, shard)
            total = held[owner, :, lanes].astype(jnp.float32)
            for k in range(1, grid[order[t]]):
                slot = slots[p % len(orders), t, shard, k]
                block = inbox.at[slot, :, lanes]
                pltpu.make_async_copy(block, block, g_recv.at[p, slot]).wait()
                total = total + inbox[slot, :, lanes].astype(jnp.float32)
            if t == depth - 1:
                out[:, lanes] = total
            else:
                acc[owner, :, lanes] = total.astype(acc.dtype)

    for piece in pieces:
        send_stage(0, piece)
    exchange = []
    far = sorted(everyone[1:], key=sum, reverse=True)
    for i, step in enumerate(far):
        there = device_at(here, grid, step)
        exchange.append(
            remote(
                block_for(there), kern_o.at[me, :, :, half_lanes], a_send.at[i], a_recv.at[i], (there, mp)
            )
        )
    own = pltpu.make_async_copy(block_for(me), kern_o.at[me, :, :, half_lanes], local)
    own.start()
    forwards = [
        remote(block_for(me), kern_o.at[me, :, :, half_lanes], f_send.at[n - 1], f_recv.at[n - 1], (me, 1 - mp))
    ]
    for t in range(depth):
        for piece in pieces:
            add_stage(t, piece)
            if t + 1 < depth:
                send_stage(t + 1, piece)
    for i in reversed(range(n - 1)):
        source = device_at(here, grid, minus((0,) * depth, far[i], grid))
        block = kern_o.at[source, :, :, half_lanes]
        exchange[i].wait_recv()
        forwards.append(remote(block, block, f_send.at[i], f_recv.at[i], (me, 1 - mp)))
    for copy in exchange:
        copy.wait_send()
    for copy in forwards:
        copy.wait()
    for copy in sends:
        copy.wait_send()
    own.wait()


def reduce(kern, attn, mlp, n, rows):
    grid = factors_of(n)
    bands, _, pixels = kern.shape
    direct = rows % 16 == 0
    if not direct:
        kern = kern.reshape(bands, n, rows, pixels).transpose(1, 0, 2, 3)
    pieces = 2 * len(orders_of(grid))
    return pl.pallas_call(
        partial(reduce_kernel, n, grid, direct),
        out_shape=[
            jax.ShapeDtypeStruct((n, bands, rows, 2 * pixels), kern.dtype),
            jax.ShapeDtypeStruct(attn.shape[1:], jnp.float32),
            jax.ShapeDtypeStruct(mlp.shape[1:], jnp.float32),
        ],
        in_specs=[ANY, VMEM, VMEM],
        out_specs=[ANY, VMEM, VMEM],
        scratch_shapes=[
            pltpu.VMEM(attn.shape, attn.dtype),
            pltpu.VMEM(mlp.shape, mlp.dtype),
            pltpu.VMEM((n - 1,) + attn.shape[1:], attn.dtype),
            pltpu.VMEM((n - 1,) + mlp.shape[1:], mlp.dtype),
            pltpu.SemaphoreType.DMA,
            pltpu.SemaphoreType.DMA((n - 1,)),
            pltpu.SemaphoreType.DMA((n - 1,)),
            pltpu.SemaphoreType.DMA((n,)),
            pltpu.SemaphoreType.DMA((n,)),
            pltpu.SemaphoreType.DMA((pieces, n - 1)),
            pltpu.SemaphoreType.DMA((pieces, n - 1)),
        ],
        compiler_params=params(2, BIG_VMEM),
        name="reduce",
    )(kern, attn, mlp)


def total_kernel(n, x_ref, o_ref, inbox, send, recv, back_send, back_recv):
    me, mp = lax.axis_index("dp"), lax.axis_index("mp")
    greet_all(n, me, mp, False)
    copies = []
    for k in range(1, n):
        there = lax.rem(me + k, n)
        copies.append(remote(x_ref.at[there], inbox.at[k - 1], send.at[k - 1], recv.at[k - 1], (there, mp)))
    total = x_ref[me]
    for k, copy in enumerate(copies):
        copy.wait_recv()
        total = total + inbox[k]
    o_ref[me] = total
    for k in range(1, n):
        there = lax.rem(me + k, n)
        copies.append(remote(o_ref.at[me], o_ref.at[me], back_send.at[k - 1], back_recv.at[k - 1], (there, mp)))
    for copy in copies[: n - 1]:
        copy.wait_send()
    for copy in copies[n - 1 :]:
        copy.wait()


def total_over_slots(x, n):
    return pl.pallas_call(
        partial(total_kernel, n),
        out_shape=jax.ShapeDtypeStruct(x.shape, x.dtype),
        in_specs=[VMEM],
        out_specs=VMEM,
        scratch_shapes=[pltpu.VMEM((n - 1,) + x.shape[1:], x.dtype)] + [pltpu.SemaphoreType.DMA((n - 1,))] * 4,
        compiler_params=params(4),
        name="total",
    )(x)


def dot(a, b, contract):
    return lax.dot_general(a, b, ((contract[0], contract[1]), ((), ())), preferred_element_type=jnp.float32)


NN, NT, TN = ((1,), (0,)), ((1,), (1,)), ((0,), (0,))


def lanes_at(i, width):
    return pl.ds(pl.multiple_of(i * width, width), width)


def row_mean(x):
    return jnp.mean(x, axis=-1, keepdims=True)


def column_sums(x):
    return dot(jnp.ones((8, x.shape[0]), x.dtype), x, NN)[:1]


def middle_kernel(
    inner, pix, kern, attn, mlp, cot, band_mask, key_mask, row_scale, patch_bias, gains, shifts, in_bias, out_bias, up_bias, down_bias,
    out_o, emb_grad_o, attn_grad, mlp_grad, small_o, small_up_o, small_in_o,
    masked, emb, mid, part, inbox, norm_a, norm_b, qkv, prob, ctx, act, slope, d_out, d_pre, d_mid, d_att, d_ctx, d_qkv, turned, send, recv,
):
    me, mp = lax.axis_index("dp"), lax.axis_index("mp")
    partner = (me, 1 - mp)
    low = jnp.bfloat16
    sem = pltpu.get_barrier_semaphore()
    pl.semaphore_signal(sem, inc=1, device_id=partner, device_id_type=MESH)
    pl.semaphore_wait(sem, 1)
    bands, tokens, _ = pix.shape
    width = emb.shape[1]
    units = act.shape[1]
    halves = 2
    span = tokens // halves
    tile = 256
    copies = {}

    def swap(i, compute):
        for h in range(halves):
            r = pl.ds(h * span, span)

            @pl.loop(0, width // tile)
            def _(j):
                part[i, r, lanes_at(j, tile)] = compute(r, j)

            copies[i, h] = remote(part.at[i, r], inbox.at[i, r], send.at[i, h], recv.at[i, h], partner)

    def swapped(i, h):
        copies[i, h].wait_recv()
        r = pl.ds(h * span, span)
        return part[i, r] + inbox[i, r]

    for b in range(bands):
        masked[b] = pix[b] * band_mask[b : b + 1, :].astype(low)

    def embed_terms(r, j):
        total = jnp.zeros((span, tile), jnp.float32)
        for b in range(bands):
            total = total + dot(masked[b, r], kern[b, lanes_at(j, tile)], NT)
        return total

    swap(0, embed_terms)
    d_out[...] = (cot[...].astype(jnp.float32) * row_scale[...]).astype(low)
    turned[0] = d_out[...].T
    for h in range(halves):
        r = pl.ds(h * span, span)
        rows = swapped(0, h) + patch_bias[...]
        emb[r] = rows
        center = rows - row_mean(rows)
        hat = center * lax.rsqrt(row_mean(center * center) + vit_epsilon)
        norm_a[r] = (hat * gains[0:1] + shifts[0:1]).astype(low)

    @pl.loop(0, 3 * inner // 384)
    def _(j):
        cols = lanes_at(j, 384)
        qkv[:, cols] = (dot(norm_a[...], attn[:, cols], NN) + in_bias[:, cols]).astype(low)

    lane = lax.broadcasted_iota(jnp.int32, (1, 2 * HEAD_DIM), 1)
    in_head = [(lane < HEAD_DIM).astype(low), (lane >= HEAD_DIM).astype(low)]
    scale = 1.0 / math.sqrt(HEAD_DIM)
    pairs = inner // (2 * HEAD_DIM)
    wide = 2 * HEAD_DIM

    def head_lanes(j, which):
        return pl.ds(pl.multiple_of(which * inner + j * wide, wide), wide)

    @pl.loop(0, pairs)
    def _(j):
        q, k, v = (qkv[:, head_lanes(j, w)] for w in range(3))
        total = jnp.zeros((tokens, wide), jnp.float32)
        for h in range(2):
            scores = jnp.where(key_mask[...] > 0.0, dot(q * in_head[h], k, NT) * scale, -1e30)
            raised = jnp.exp(scores - jnp.max(scores, axis=-1, keepdims=True))
            p = raised / jnp.sum(raised, axis=-1, keepdims=True)
            prob[2 * j + h] = p
            total = total + dot(p.astype(low), v * in_head[h], NN)
        ctx[:, lanes_at(j, wide)] = total.astype(low)

    def out_terms(r, j):
        return dot(ctx[r], attn[lanes_at(j, tile), pl.ds(3 * inner, inner)], NT)

    swap(1, out_terms)
    turned[1] = norm_a[...].T
    for h in range(halves):
        r = pl.ds(h * span, span)
        rows = emb[r] + swapped(1, h) + out_bias[...]
        mid[r] = rows
        center = rows - row_mean(rows)
        hat = center * lax.rsqrt(row_mean(center * center) + vit_epsilon)
        norm_b[r] = (hat * gains[1:2] + shifts[1:2]).astype(low)

    @pl.loop(0, units // tile)
    def _(j):
        cols = lanes_at(j, tile)
        pre = dot(norm_b[...], mlp[:, cols], NN) + up_bias[:, cols]
        phi = 0.5 + 0.5 * lax.erf(pre * math.sqrt(0.5))
        act[:, cols] = (pre * phi).astype(low)
        slope[:, cols] = phi + pre * (jnp.exp(-0.5 * pre * pre) * (1.0 / math.sqrt(2.0 * math.pi)))

    def down_terms(r, j):
        return dot(act[r], mlp[lanes_at(j, tile), pl.ds(units, units)], NT)

    @pl.loop(0, units // tile)
    def _(j):
        cols = lanes_at(j, tile)
        d_act = dot(d_out[...], mlp[:, pl.ds(pl.multiple_of(units + j * tile, tile), tile)], NN).astype(low)
        d_pre[:, cols] = (d_act.astype(jnp.float32) * slope[:, cols]).astype(low)

    def up_terms(r, j):
        return dot(d_pre[r], mlp[lanes_at(j, tile), pl.ds(0, units)], NT)

    swap(2, up_terms)
    swap(3, down_terms)
    turned[2] = norm_b[...].T

    def weight_grad(turned_ref, x, out, start):
        @pl.loop(0, width // tile)
        def _(i):
            for j in range(x.shape[1] // 384):
                out[lanes_at(i, tile), pl.ds(start + j * 384, 384)] = dot(
                    turned_ref[lanes_at(i, tile)], x[:, j * 384 : (j + 1) * 384], NN
                ).astype(low)

    weight_grad(turned.at[2], d_pre, mlp_grad, 0)
    small_up_o[...] = column_sums(d_pre[...])
    small_o[5:6] = column_sums(d_out[...])

    def norm_back(x, d_y, which):
        center = x - row_mean(x)
        r = lax.rsqrt(row_mean(center * center) + vit_epsilon)
        hat = center * r
        u = d_y * gains[which : which + 1]
        d_x = r * (u - row_mean(u) - hat * row_mean(u * hat))
        return d_x, jnp.sum(d_y * hat, axis=0, keepdims=True), jnp.sum(d_y, axis=0, keepdims=True)

    sums = []
    for h in range(halves):
        r = pl.ds(h * span, span)
        d_x, gain, shift = norm_back(mid[r], swapped(2, h), 1)
        d_x = d_x + d_out[r].astype(jnp.float32)
        d_mid[r] = d_x
        d_att[r] = d_x.astype(low)
        sums.append((gain, shift))
    small_o[1:2] = sums[0][0] + sums[1][0]
    small_o[3:4] = sums[0][1] + sums[1][1]
    small_o[4:5] = column_sums(d_att[...])

    @pl.loop(0, inner // 384)
    def _(j):
        d_ctx[:, lanes_at(j, 384)] = dot(
            d_att[...], attn[:, pl.ds(pl.multiple_of(3 * inner + j * 384, 384), 384)], NN
        ).astype(low)

    @pl.loop(0, pairs)
    def _(j):
        q, k, v = (qkv[:, head_lanes(j, w)] for w in range(3))
        d_c = d_ctx[:, lanes_at(j, wide)]
        d_q = jnp.zeros((tokens, wide), jnp.float32)
        d_k, d_v = d_q, d_q
        for h in range(2):
            p = prob[2 * j + h]
            d_p = dot(d_c * in_head[h], v, NT)
            d_s = (p * (d_p - jnp.sum(p * d_p, axis=-1, keepdims=True))).astype(low)
            d_q = d_q + dot(d_s, k * in_head[h], NN)
            d_k = d_k + dot(d_s, q * in_head[h], TN)
            d_v = d_v + dot(p.astype(low), d_c * in_head[h], TN)
        d_qkv[:, head_lanes(j, 0)] = (d_q * scale).astype(low)
        d_qkv[:, head_lanes(j, 1)] = (d_k * scale).astype(low)
        d_qkv[:, head_lanes(j, 2)] = d_v.astype(low)

    def in_terms(r, j):
        return dot(d_qkv[r], attn[lanes_at(j, tile), pl.ds(0, 3 * inner)], NT)

    swap(4, in_terms)
    weight_grad(turned.at[1], d_qkv, attn_grad, 0)
    turned[2] = d_att[...].T
    weight_grad(turned.at[2], ctx, attn_grad, 3 * inner)
    weight_grad(turned.at[0], act, mlp_grad, units)
    small_in_o[...] = column_sums(d_qkv[...])
    for h in range(halves):
        r = pl.ds(h * span, span)
        rows = (mid[r] + swapped(3, h) + down_bias[...]) * row_scale[r]
        out_o[r] = rows.astype(low)
    sums = []
    for h in range(halves):
        r = pl.ds(h * span, span)
        d_x, gain, shift = norm_back(emb[r], swapped(4, h), 0)
        emb_grad_o[r] = (d_x + d_mid[r]).astype(low)
        sums.append((gain, shift))
    small_o[0:1] = sums[0][0] + sums[1][0]
    small_o[2:3] = sums[0][1] + sums[1][1]
    small_o[6:7] = column_sums(emb_grad_o[...])
    small_o[7:8] = jnp.zeros((1, width), jnp.float32)
    for copy in copies.values():
        copy.wait_send()


def middle(inner, pix, kern, attn, mlp, cot, *rest):
    bands, tokens, _ = pix.shape
    width, units = attn.shape[0], mlp.shape[1] // 2
    f32, low = jnp.float32, jnp.bfloat16
    heads = inner // HEAD_DIM

    def shape(dims, dtype):
        return jax.ShapeDtypeStruct(dims, dtype)

    flops = 2 * tokens * width * (bands * 128 + 9 * inner * 2 + 9 * units)
    return pl.pallas_call(
        partial(middle_kernel, inner),
        out_shape=[
            shape((tokens, width), low),
            shape((tokens, width), low),
            shape(attn.shape, low),
            shape(mlp.shape, low),
            shape((8, width), f32),
            shape((1, units), f32),
            shape((1, 3 * inner), f32),
        ],
        in_specs=[VMEM] * 15,
        out_specs=[VMEM] * 7,
        scratch_shapes=[
            pltpu.VMEM(pix.shape, low),
            pltpu.VMEM((tokens, width), f32),
            pltpu.VMEM((tokens, width), f32),
            pltpu.VMEM((5, tokens, width), f32),
            pltpu.VMEM((5, tokens, width), f32),
            pltpu.VMEM((tokens, width), low),
            pltpu.VMEM((tokens, width), low),
            pltpu.VMEM((tokens, 3 * inner), low),
            pltpu.VMEM((heads, tokens, tokens), f32),
            pltpu.VMEM((tokens, inner), low),
            pltpu.VMEM((tokens, units), low),
            pltpu.VMEM((tokens, units), f32),
            pltpu.VMEM((tokens, width), low),
            pltpu.VMEM((tokens, units), low),
            pltpu.VMEM((tokens, width), f32),
            pltpu.VMEM((tokens, width), low),
            pltpu.VMEM((tokens, inner), low),
            pltpu.VMEM((tokens, 3 * inner), low),
            pltpu.VMEM((3, width, tokens), low),
            pltpu.SemaphoreType.DMA((5, 2)),
            pltpu.SemaphoreType.DMA((5, 2)),
        ],
        compiler_params=params(3, BIG_VMEM),
        cost_estimate=pl.CostEstimate(flops=flops, bytes_accessed=2 * 10**7, transcendentals=10**6),
        name="middle",
    )(pix, kern, attn, mlp, cot, *rest)


def exact_einsum(pattern, left_side, right_side):
    return jnp.einsum(
        pattern,
        left_side,
        right_side,
        precision=lax.Precision.HIGHEST,
        preferred_element_type=jnp.float32,
    )


def fast_einsum(pattern, left_side, right_side):
    return jnp.einsum(pattern, left_side, right_side, preferred_element_type=jnp.float32)


def norm_rows(values, gain_row, shift_row, epsilon):
    center = values - jnp.mean(values, axis=-1, keepdims=True)
    spread = jnp.mean(center * center, axis=-1, keepdims=True)
    return center * lax.rsqrt(spread + epsilon) * gain_row + shift_row


def exact_gelu(values):
    return jax.nn.gelu(values, approximate=False)


def wave_embedding(wavelengths, model_width):
    half_width = model_width // 2
    frequency = 10000.0 ** (-jnp.arange(half_width, dtype=jnp.float32) * 2.0 / model_width)
    angles = wavelengths.astype(jnp.float32)[..., None] * frequency
    return jnp.concatenate([jnp.sin(angles), jnp.cos(angles)], axis=-1)


def hyper_all(
    embedding, band_valid, hyp_attn, hyp_mlp_in, hyp_mlp_out, hyp_gain, hyp_shift, bias_token, bias_w
):
    slots, bands, width = embedding.shape
    length, head_size = bands + 1, width // HYP_HEADS
    sequence = jnp.concatenate([embedding, jnp.broadcast_to(bias_token, (slots, 1, width))], axis=1)
    keys_valid = jnp.concatenate([band_valid, jnp.ones((slots, 1), dtype=bool)], axis=1)
    heads = (slots, length, HYP_HEADS, head_size)
    query_rows = exact_einsum("ste,ef->stf", sequence, hyp_attn[0]).reshape(heads)
    key_rows = exact_einsum("ste,ef->stf", sequence, hyp_attn[1]).reshape(heads)
    value_rows = exact_einsum("ste,ef->stf", sequence, hyp_attn[2]).reshape(heads)
    scores = exact_einsum("sqhd,skhd->shqk", query_rows, key_rows) * (1.0 / math.sqrt(head_size))
    scores = jnp.where(keys_valid[:, None, None, :], scores, -1e30)
    weights = jax.nn.softmax(scores, axis=-1)
    mixed_rows = exact_einsum("shqk,skhd->sqhd", weights, value_rows).reshape(slots, length, width)
    first_rows = norm_rows(
        sequence + exact_einsum("ste,ef->stf", mixed_rows, hyp_attn[3]),
        hyp_gain[0],
        hyp_shift[0],
        hyper_epsilon,
    )
    inner_rows = exact_gelu(exact_einsum("ste,ef->stf", first_rows, hyp_mlp_in))
    second_rows = norm_rows(
        first_rows + exact_einsum("stf,fe->ste", inner_rows, hyp_mlp_out),
        hyp_gain[1],
        hyp_shift[1],
        hyper_epsilon,
    )
    return second_rows[:, :-1] + embedding, exact_einsum("se,ec->sc", second_rows[:, -1], bias_w)


def per_device(
    n,
    pixels,
    band_count,
    wavelengths,
    size_class,
    token_keep,
    hyp_attn,
    hyp_mlp_in,
    hyp_mlp_out,
    hyp_gain,
    hyp_shift,
    bias_token,
    kern_weight,
    kern_bias,
    patch_bias_weight,
    norm_gain,
    norm_shift,
    attn_in,
    attn_in_bias,
    attn_out,
    attn_out_bias,
    mlp_in,
    mlp_in_bias,
    mlp_out,
    mlp_out_bias,
    cotangent,
):
    me, mp = lax.axis_index("dp"), lax.axis_index("mp")
    slot_count, band_total, tokens, pix_size = pixels.shape
    model_width = norm_gain.shape[1]
    hyper_width, rows, _ = kern_weight.shape
    half = pix_size // 2
    low = jnp.bfloat16

    facts = jnp.concatenate([wavelengths[0], band_count])
    facts = jnp.broadcast_to(jnp.pad(facts, (0, 128 - band_total - 1)), (8, 128))
    facts = share(facts, n)[:, 0]
    embedding = wave_embedding(facts[:, :band_total], hyper_width)
    every_band = jnp.arange(band_total)[None, :] < facts[:, band_total][:, None]
    (code_vals, patch_bias), hyper_back = jax.vjp(
        partial(hyper_all, embedding, every_band),
        hyp_attn,
        hyp_mlp_in,
        hyp_mlp_out,
        hyp_gain,
        hyp_shift,
        bias_token,
        patch_bias_weight,
    )
    all_codes = code_vals.astype(low).reshape(n * band_total, hyper_width)
    patch_bias = lax.dynamic_slice_in_dim(patch_bias, me, 1, 0)

    kern_low = kern_weight.astype(low)
    half_weight = lax.dynamic_slice_in_dim(kern_low, mp * half, half, 2)
    half_bias = lax.dynamic_slice_in_dim(kern_bias, mp * half, half, 1)
    half_kernels = (fast_einsum("ne,ecp->ncp", all_codes, half_weight) + half_bias).astype(low)

    inner = attn_in.shape[2]
    units = mlp_in.shape[1]
    attn_shard = jnp.concatenate([attn_in[0], attn_in[1], attn_in[2], attn_out], axis=1).astype(low)
    mlp_shard = jnp.concatenate([mlp_in, mlp_out], axis=1).astype(low)
    kernel, attn_all, mlp_all = fetch(half_kernels, attn_shard, mlp_shard, n)

    band_valid = jnp.arange(band_total) < band_count[0]
    live_rows = jnp.where(
        size_class[0] == 0, tokens * 49 // 256, jnp.where(size_class[0] == 1, tokens * 196 // 256, tokens)
    )
    position = jnp.arange(tokens)
    row_valid = position < live_rows
    key_valid = row_valid & ((token_keep[0] == 1) | (position == 0))
    row_scale = row_valid.astype(jnp.float32)[:, None]
    half_pixels = lax.dynamic_slice_in_dim(pixels[0], mp * half, half, 2)
    band_rows = jnp.broadcast_to(jnp.pad(band_valid.astype(jnp.float32), (0, 3))[:, None], (band_total + 3, half))
    masked_pixels = half_pixels * band_valid.astype(low)[:, None, None]
    input_bias = jnp.concatenate([attn_in_bias[0], jnp.zeros_like(attn_in_bias[0]), attn_in_bias[1]])
    layer_out, embed_grad, attn_grads, mlp_grads, small_rows, up_sums, in_sums = middle(
        inner,
        half_pixels,
        kernel,
        attn_all,
        mlp_all,
        cotangent[0],
        band_rows,
        key_valid.astype(jnp.float32)[None],
        row_scale,
        patch_bias,
        norm_gain,
        norm_shift,
        input_bias[None],
        attn_out_bias[None],
        mlp_in_bias[None],
        mlp_out_bias[None],
    )
    layer_out = layer_out[None]
    patch_bias_grad = small_rows[6]
    half_grad = fast_einsum("tc,btp->bcp", embed_grad, masked_pixels).astype(low)
    attn_grads = attn_grads.reshape(n, rows, -1)
    mlp_grads = mlp_grads.reshape(n, rows, -1)
    local_grad, attn_sum, mlp_sum = reduce(half_grad, attn_grads, mlp_grads, n, rows)
    local_grad = local_grad.reshape(n * band_total, rows, pix_size)
    grad_attn_in = jnp.stack([attn_sum[:, i * inner : (i + 1) * inner] for i in range(3)])
    grad_attn_out = attn_sum[:, 3 * inner :]
    grad_mlp_in, grad_mlp_out = mlp_sum[:, :units], mlp_sum[:, units:]

    code_part = fast_einsum("ncp,ecp->ne", local_grad, kern_low).reshape(n, band_total, hyper_width)

    small = (
        small_rows[0],
        small_rows[1],
        small_rows[2],
        small_rows[3],
        in_sums[0, :inner],
        in_sums[0, 2 * inner :],
        small_rows[4],
        up_sums[0],
        small_rows[5],
    )
    flat = jnp.concatenate([v.reshape(-1) for v in small])
    lanes = 128
    per_slot = -(-flat.size // (n * lanes))
    flat = jnp.pad(flat, (0, n * per_slot * lanes - flat.size)).reshape(n, per_slot, lanes)
    patch_rows = patch_bias_grad.reshape(1, -1, lanes) * (jnp.arange(n) == me).astype(jnp.float32)[:, None, None]
    packed = jnp.concatenate([code_part, patch_rows, flat], axis=1)
    used = packed.shape[1]
    packed = jnp.pad(packed, ((0, 0), (0, -used % 8), (0, 0)))
    packed = total_over_slots(packed, n)
    code_grad = packed[:, :band_total]
    patch_grad = packed[:, band_total : band_total + model_width // lanes].reshape(n, model_width)
    flat = packed[:, used - per_slot : used].reshape(-1)
    split = []
    start = 0
    for v in small:
        split.append(flat[start : start + v.size])
        start += v.size
    hyper_grads = hyper_back((code_grad, patch_grad))

    pixel_half = fast_einsum("tc,bcp->btp", embed_grad, kernel) * band_valid.astype(jnp.float32)[:, None, None]
    pixel_grad = lax.all_gather(pixel_half.astype(low), "mp", axis=2, tiled=True)[None]
    grad_kern_weight = fast_einsum("ne,ncp->ecp", all_codes, local_grad)
    grad_kern_bias = jnp.sum(local_grad, axis=0, dtype=jnp.float32)
    return (
        layer_out,
        pixel_grad,
        hyper_grads[0],
        hyper_grads[1],
        hyper_grads[2],
        hyper_grads[3],
        hyper_grads[4],
        hyper_grads[5],
        grad_kern_weight,
        grad_kern_bias,
        hyper_grads[6],
        jnp.stack([split[0], split[1]]),
        jnp.stack([split[2], split[3]]),
        grad_attn_in,
        jnp.stack([split[4], split[5]]),
        grad_attn_out,
        split[6],
        grad_mlp_in,
        split[7],
        grad_mlp_out,
        split[8],
    )


def solution(mesh):
    return jax.shard_map(
        partial(per_device, mesh.shape["dp"]),
        mesh=mesh,
        in_specs=(
            P("dp", None, None, None),
            P("dp"),
            P("dp", None),
            P("dp"),
            P("dp", None),
            P(),
            P(),
            P(),
            P(),
            P(),
            P(),
            P(None, "dp", None),
            P("dp", None),
            P(),
            P(),
            P(),
            P(None, "dp", "mp"),
            P(None, "mp"),
            P("dp", "mp"),
            P(),
            P("dp", "mp"),
            P("mp"),
            P("dp", "mp"),
            P(),
            P("dp", None, None),
        ),
        out_specs=(
            P("dp", None, None),
            P("dp", None, None, None),
            P(),
            P(),
            P(),
            P(),
            P(),
            P(),
            P(None, "dp", None),
            P("dp", None),
            P(),
            P(),
            P(),
            P(None, "dp", "mp"),
            P(None, "mp"),
            P("dp", "mp"),
            P(),
            P("dp", "mp"),
            P("mp"),
            P("dp", "mp"),
            P(),
        ),
        check_vma=False,
    )
```

```python
from functools import partial
import math

import jax
import jax.numpy as jnp
from jax import lax
from jax.experimental import pallas as pl
from jax.experimental.pallas import tpu as pltpu
from jax.sharding import PartitionSpec as P

HEAD_DIM = 64
HYP_HEADS = 4
MESH = pl.DeviceIdType.MESH
ANY = pl.BlockSpec(memory_space=pl.ANY)
VMEM = pl.BlockSpec(memory_space=pltpu.VMEM)
BIG_VMEM = 58 * 1024 * 1024

vit_epsilon = 1e-06
hyper_epsilon = 1e-05


def factors_of(n):
    return {16: (4, 2, 2), 128: (4, 8, 4)}.get(n, (n,))


def coords(me, grid):
    out = []
    for size in reversed(grid):
        out.append(lax.rem(me, size))
        me = me // size
    return out[::-1]


def device_at(position, grid, offset):
    index = 0
    for place, size, step in zip(position, grid, offset):
        index = index * size + (lax.rem(place + step, size) if step else place)
    return index


def offsets_in(grid, dims):
    out = [()]
    for dim, size in enumerate(grid):
        out = [o + (i,) for o in out for i in range(size if dim in dims else 1)]
    return out


def along(grid, dim, step):
    return tuple(step if d == dim else 0 for d in range(len(grid)))


def minus(a, b, grid):
    return tuple((i - j) % size for i, j, size in zip(a, b, grid))


def orders_of(grid):
    return [(0, 1, 2), (0, 2, 1)] if len(grid) == 3 else [tuple(range(len(grid)))]


def greet(n, me, mp, both):
    sem = pltpu.get_barrier_semaphore()
    for k in range(1, n):
        pl.semaphore_signal(sem, inc=1, device_id=(lax.rem(me + k, n), mp), device_id_type=MESH)
    if both:
        for k in range(n):
            pl.semaphore_signal(sem, inc=1, device_id=(lax.rem(me + k, n), 1 - mp), device_id_type=MESH)
    pl.semaphore_wait(sem, 2 * n - 1 if both else n - 1)


def remote(src, dst, send, recv, device):
    copy = pltpu.make_async_remote_copy(
        src_ref=src, dst_ref=dst, send_sem=send, recv_sem=recv, device_id=device, device_id_type=MESH
    )
    copy.start()
    return copy


def params(collective, limit=None):
    return pltpu.CompilerParams(collective_id=collective, has_side_effects=True, vmem_limit_bytes=limit)


NN, NT, TN = ((1,), (0,)), ((1,), (1,)), ((0,), (0,))
GROUP = 16
SPAN = 16


def dot(a, b, contract):
    return lax.dot_general(a, b, (contract, ((), ())), preferred_element_type=jnp.float32)


def exact(a, b, contract=NN):
    return lax.dot_general(
        a, b, (contract, ((), ())), precision=lax.Precision.HIGHEST, preferred_element_type=jnp.float32
    )


def lanes_at(i, width):
    return pl.ds(pl.multiple_of(i * width, width), width)


def row_mean(x):
    return jnp.mean(x, axis=-1, keepdims=True)


def row_sum(x):
    return jnp.sum(x, axis=-1, keepdims=True)


def all_rows(x):
    return jnp.sum(x, axis=0, keepdims=True)


def column_sums(x):
    return dot(jnp.ones((8, x.shape[0]), x.dtype), x, NN)[:1]


def normal_parts(x):
    return 0.5 + 0.5 * lax.erf(x * math.sqrt(0.5)), jnp.exp(-0.5 * x * x) * (1.0 / math.sqrt(2.0 * math.pi))


def normed(x, epsilon):
    center = x - row_mean(x)
    r = lax.rsqrt(row_mean(center * center) + epsilon)
    return center * r, r


def norm_back(hat, r, d_y, gain_row):
    u = d_y * gain_row
    return r * (u - row_mean(u) - hat * row_mean(u * hat)), all_rows(d_y * hat), all_rows(d_y)


def tiled(rows):
    return -(-rows // 8) * 8


def first_rows(ref, rows):
    return ref if ref.shape[-2] == rows else ref.at[:, pl.ds(0, rows)]


def arrived(block, sem):
    pltpu.make_async_copy(block, block, sem).wait()


SEQ, QUERY, KEY, VALUE, MIXED, HAT_A, FIRST, HAT_B, SECOND, SCALE_A, SCALE_B = range(11)


def head_masks(width):
    lane = lax.broadcasted_iota(jnp.int32, (1, width), 1)
    size = width // HYP_HEADS
    return [((lane >= h * size) & (lane < (h + 1) * size)).astype(jnp.float32) for h in range(HYP_HEADS)]


def generator_forward(facts, g, w_attn, w_in, w_out, gain, shift, rows, wide, prob):
    count, width = GROUP * SPAN, facts.shape[-1]
    block = facts[pl.ds(g * GROUP, GROUP)]
    seq = block[:, :SPAN].reshape(count, width)
    valid = block[:, SPAN:].reshape(count, width)
    columns = dot(jnp.ones((8, width), jnp.bfloat16), valid.astype(jnp.bfloat16), NT)[:1]
    slot = [lax.shift_right_logical(lax.broadcasted_iota(jnp.int32, (count, count), d), 4) for d in range(2)]
    allowed = (slot[0] == slot[1]) & (columns > 0.5)
    rows[SEQ] = seq
    for i in range(3):
        rows[QUERY + i] = exact(seq, w_attn[i])
    scale = 1.0 / math.sqrt(width // HYP_HEADS)
    mixed = jnp.zeros((count, width), jnp.float32)
    for h, mask in enumerate(head_masks(width)):
        scores = jnp.where(allowed, exact(rows[QUERY] * mask, rows[KEY], NT) * scale, -1e30)
        raised = jnp.exp(scores - jnp.max(scores, axis=-1, keepdims=True))
        weights = raised / row_sum(raised)
        prob[h] = weights
        mixed = mixed + exact(weights, rows[VALUE] * mask)
    rows[MIXED] = mixed
    hat, r = normed(seq + exact(mixed, w_attn[3]), hyper_epsilon)
    rows[HAT_A] = hat
    rows[SCALE_A] = jnp.broadcast_to(r, (count, width))
    rows[FIRST] = hat * gain[0:1] + shift[0:1]
    tile = 512

    @pl.loop(0, w_in.shape[1] // tile)
    def _(j):
        cols = lanes_at(j, tile)
        pre = exact(rows[FIRST], w_in[:, cols])
        phi, density = normal_parts(pre)
        wide[0, :, cols] = pre * phi
        wide[1, :, cols] = phi + pre * density

    rows[SECOND] = rows[FIRST]

    @pl.loop(0, w_in.shape[1] // tile)
    def _(j):
        cols = lanes_at(j, tile)
        rows[SECOND] = rows[SECOND] + exact(wide[0, :, cols], w_out[cols])

    hat, r = normed(rows[SECOND], hyper_epsilon)
    rows[HAT_B] = hat
    rows[SCALE_B] = jnp.broadcast_to(r, (count, width))
    rows[SECOND] = hat * gain[1:2] + shift[1:2]


def generator_backward(d_second, put, w_attn, w_in, w_out, gain, rows, wide, prob, d_mlp, outs):
    g_attn, g_in, g_out, g_gain, g_shift, g_token = outs
    width = d_second.shape[1]
    d_sum, gain_b, shift_b = norm_back(rows[HAT_B], rows[SCALE_B], d_second, gain[1:2])
    put(g_gain, slice(1, 2), gain_b)
    put(g_shift, slice(1, 2), shift_b)
    d_mlp[0] = d_sum
    d_mlp[1] = d_sum
    tile = 512

    @pl.loop(0, w_in.shape[1] // tile)
    def _(j):
        cols = lanes_at(j, tile)
        put(g_out, cols, exact(wide[0, :, cols], d_mlp[0], TN))
        d_pre = exact(d_mlp[0], w_out[cols], NT) * wide[1, :, cols]
        put(g_in, (slice(None), cols), exact(rows[FIRST], d_pre, TN))
        d_mlp[1] = d_mlp[1] + exact(d_pre, w_in[:, cols], NT)

    d_res, gain_a, shift_a = norm_back(rows[HAT_A], rows[SCALE_A], d_mlp[1], gain[0:1])
    put(g_gain, slice(0, 1), gain_a)
    put(g_shift, slice(0, 1), shift_a)
    put(g_attn, 3, exact(rows[MIXED], d_res, TN))
    d_mixed = exact(d_res, w_attn[3], NT)
    scale = 1.0 / math.sqrt(width // HYP_HEADS)
    d_q = jnp.zeros_like(d_res)
    d_k, d_v = d_q, d_q
    for h, mask in enumerate(head_masks(width)):
        p, d_m = prob[h], d_mixed * mask
        d_p = exact(d_m, rows[VALUE], NT)
        d_s = p * (d_p - row_sum(p * d_p)) * scale
        d_q = d_q + exact(d_s, rows[KEY] * mask)
        d_k = d_k + exact(d_s, rows[QUERY] * mask, TN)
        d_v = d_v + exact(p, d_m, TN)
    d_seq = d_res
    for i, grad in enumerate((d_q, d_k, d_v)):
        put(g_attn, i, exact(rows[SEQ], grad, TN))
        d_seq = d_seq + exact(grad, w_attn[i], NT)
    d_mlp[0] = d_seq


def generator_scratch(width, units):
    f32, count = jnp.float32, GROUP * SPAN
    return [(11, count, width), (2, count, units), (HYP_HEADS, count, count)], f32


def front_kernel(
    n, grid, direct, bands,
    facts_own, w_attn, w_in, w_out, gain, shift, patch_w, kern_w, kern_b, attn, mlp,
    kern_o, attn_o, mlp_o, facts, patch_o, codes_o, rows_o, wide_o, prob_o,
    second, w_half, b_half, k32, k16, local, f_send, f_recv, a_send, a_recv, g_send, g_recv,
):
    me, mp = lax.axis_index("dp"), lax.axis_index("mp")
    here = coords(me, grid)
    low = jnp.bfloat16
    rows, half = kern_w.shape[1], kern_w.shape[2] // 2
    lanes = lanes_at(mp, half)
    orders = orders_of(grid)
    depth = len(grid)
    everyone = offsets_in(grid, range(depth))
    index = {o: i for i, o in enumerate(everyone)}
    zero = (0,) * depth

    def kern_slot():
        if direct:
            return kern_o.at[:, pl.ds(pl.multiple_of(rows * me, 16), rows)]
        return kern_o.at[me]

    load = pltpu.make_async_copy(kern_w.at[:, :, lanes], first_rows(w_half, rows), local.at[0])
    load.start()
    own = [
        pltpu.make_async_copy(attn, attn_o.at[me], local.at[1]),
        pltpu.make_async_copy(mlp, mlp_o.at[me], local.at[2]),
    ]
    for copy in own:
        copy.start()
    greet(n, me, mp, False)
    shares = []
    for k in range(1, n):
        there = (lax.rem(me + k, n), mp)
        shares.append(remote(facts_own, facts.at[me], f_send.at[k - 1], f_recv.at[k - 1], there))
    facts[me] = facts_own[...]

    pieces = []
    for src, dst in ((attn, attn_o), (mlp, mlp_o)):
        width = src.shape[1] // len(orders)
        for part, order in enumerate(orders):
            pieces.append((src, dst, pl.ds(part * width, width), order, len(pieces)))
    sends, count, seen = [], [0] * len(pieces), set()

    def send(piece, shard, step):
        src, dst, cols, _, p = piece
        owner = device_at(here, grid, shard)
        there = device_at(here, grid, step)
        held = dst.at[owner, :, cols] if any(shard) else src.at[:, cols]
        slot = index[minus(shard, step, grid)]
        sends.append(
            remote(held, dst.at[owner, :, cols], g_send.at[p, count[p]], g_recv.at[p, slot], (there, mp))
        )
        count[p] += 1

    def arrive(piece, shard):
        _, dst, cols, _, p = piece
        if any(shard) and (p, shard) not in seen:
            seen.add((p, shard))
            arrived(dst.at[device_at(here, grid, shard), :, cols], g_recv.at[p, index[shard]])

    def stage(number, piece, own_shard):
        order = piece[3]
        for shard in sorted(offsets_in(grid, order[:number]), key=sum):
            if any(shard) != own_shard:
                arrive(piece, shard)
                for k in range(1, grid[order[number]]):
                    send(piece, shard, along(grid, order[number], k))

    for piece in pieces:
        for number in range(depth):
            stage(number, piece, True)

    for copy in shares:
        copy.wait_recv()
    position = lax.broadcasted_iota(jnp.int32, (GROUP * SPAN, facts.shape[-1]), 0)
    is_band = lax.rem(position, SPAN) < bands
    for g in range(n // GROUP):
        generator_forward(facts, g, w_attn, w_in, w_out, gain, shift, rows_o, wide_o, prob_o)
        group = pl.ds(g * GROUP * SPAN, GROUP * SPAN)
        second[group] = rows_o[SECOND]
        codes_o[group] = jnp.where(is_band, rows_o[SECOND] + rows_o[SEQ], 0.0).astype(low)
    patch_o[...] = exact(second[pl.ds(pl.multiple_of(me * SPAN, SPAN), SPAN)], patch_w[...])

    half_pieces = len(pieces) // 2
    for piece in pieces[:half_pieces]:
        stage(1, piece, False)

    load.wait()
    b_half[...] = kern_b[:, lanes]
    step = tiled(rows)
    w_rows = w_half.reshape(w_half.shape[0] * step, half)
    k_rows = k32.reshape(n * SPAN * step, half)

    @pl.loop(0, rows // 2)
    def _(j):
        both = [w_rows[pl.ds(2 * j + i, w_half.shape[0], stride=step), :].astype(low) for i in range(2)]
        made = dot(codes_o[...], jnp.concatenate(both, axis=1), NN)
        for i in range(2):
            c = 2 * j + i
            k_rows[pl.ds(c, n * SPAN, stride=step), :] = made[:, i * half : (i + 1) * half] + b_half[pl.ds(c, 1)]

    exchange = []
    for i, away in enumerate(sorted(everyone[1:], key=sum, reverse=True)):
        there = device_at(here, grid, away)
        k16[there] = k32[there, :bands, :rows].astype(low)
        exchange.append(remote(k16.at[there], kern_slot(), a_send.at[i], a_recv.at[i], (there, mp)))
    k16[me] = k32[me, :bands, :rows].astype(low)
    own.append(pltpu.make_async_copy(k16.at[me], kern_slot(), local.at[3]))
    own[-1].start()

    for piece in pieces[half_pieces:]:
        stage(1, piece, False)
    for number in range(2, depth):
        for piece in pieces:
            stage(number, piece, False)
    for piece in pieces:
        for shard in everyone:
            arrive(piece, shard)
    for copy in sends + shares:
        copy.wait_send()
    for copy in exchange:
        copy.wait()
    for copy in own:
        copy.wait()


def front(n, bands, facts_own, w_attn, w_in, w_out, gain, shift, patch_w, kern_w, kern_b, attn, mlp):
    grid = factors_of(n)
    hyper_width, rows, pixels = kern_w.shape
    half = pixels // 2
    direct = rows % 16 == 0
    pieces = 2 * len(orders_of(grid))
    f32, low = jnp.float32, jnp.bfloat16
    kept, _ = generator_scratch(hyper_width, w_in.shape[1])
    kern_shape = (bands, rows * n, half) if direct else (n, bands, rows, half)
    shapes = [
        (kern_shape, low),
        ((n,) + attn.shape, low),
        ((n,) + mlp.shape, low),
        ((n,) + facts_own.shape, f32),
        ((SPAN, patch_w.shape[1]), f32),
        ((n * SPAN, hyper_width), low),
    ] + [(k, f32) for k in kept]
    out = pl.pallas_call(
        partial(front_kernel, n, grid, direct, bands),
        out_shape=[jax.ShapeDtypeStruct(*s) for s in shapes],
        in_specs=[VMEM] * 7 + [ANY, VMEM, ANY, ANY],
        out_specs=[ANY] * 3 + [VMEM] * 6,
        scratch_shapes=[
            pltpu.VMEM((n * SPAN, hyper_width), f32),
            pltpu.VMEM((hyper_width, tiled(rows), half), f32),
            pltpu.VMEM((rows, half), f32),
            pltpu.VMEM((n, SPAN, tiled(rows), half), f32),
            pltpu.VMEM((n, bands, rows, half), low),
            pltpu.SemaphoreType.DMA((4,)),
            pltpu.SemaphoreType.DMA((n - 1,)),
            pltpu.SemaphoreType.DMA((n - 1,)),
            pltpu.SemaphoreType.DMA((n - 1,)),
            pltpu.SemaphoreType.DMA((n - 1,)),
            pltpu.SemaphoreType.DMA((pieces, n - 1)),
            pltpu.SemaphoreType.DMA((pieces, n)),
        ],
        compiler_params=params(1, BIG_VMEM),
        name="front",
    )(facts_own, w_attn, w_in, w_out, gain, shift, patch_w, kern_w, kern_b, attn, mlp)
    kernel = out[0]
    if not direct:
        kernel = kernel.transpose(1, 0, 2, 3).reshape(bands, rows * n, half)
    return [kernel, out[1].reshape(n * rows, -1), out[2].reshape(n * rows, -1)] + list(out[3:])


def layer_body(
    inner, after_mlp, after_attn,
    pix, kern, attn, mlp, cot, band_mask, key_mask, row_scale, patch_bias, gains, shifts, in_bias, out_bias, up_bias, down_bias,
    out_o, emb_grad_o, attn_grad, mlp_grad, small_o, small_up_o, small_in_o,
    emb, mid, part, inbox, norm_a, norm_b, qkv, prob, ctx, act, slope, d_out, d_pre, d_mid, d_att, d_ctx, d_qkv, turned, send, recv,
):
    me, mp = lax.axis_index("dp"), lax.axis_index("mp")
    partner = (me, 1 - mp)
    low = jnp.bfloat16
    bands, tokens, _ = pix.shape
    width = emb.shape[1]
    units = act.shape[1]
    halves = 2
    span = tokens // halves
    tile = 256
    copies = {}

    def swap(i, compute):
        for h in range(halves):
            r = pl.ds(h * span, span)
            if i >= 2:
                copies[i - 2, h].wait_send()

            @pl.loop(0, width // tile)
            def _(j):
                part[i % 2, r, lanes_at(j, tile)] = compute(r, j)

            copies[i, h] = remote(part.at[i % 2, r], inbox.at[i % 2, r], send.at[i, h], recv.at[i, h], partner)

    def swapped(i, h):
        copies[i, h].wait_recv()
        r = pl.ds(h * span, span)
        return part[i % 2, r] + inbox[i % 2, r]

    def embed_terms(r, j):
        total = jnp.zeros((span, tile), jnp.float32)
        for b in range(bands):
            total = total + dot(pix[b, r] * band_mask[b : b + 1].astype(low), kern[b, lanes_at(j, tile)], NT)
        return total

    swap(0, embed_terms)
    d_out[...] = (cot[...].astype(jnp.float32) * row_scale[...]).astype(low)
    turned[0] = d_out[...].T
    for h in range(halves):
        r = pl.ds(h * span, span)
        emb[r] = swapped(0, h) + patch_bias[...]
        hat, _ = normed(emb[r], vit_epsilon)
        norm_a[r] = (hat * gains[0:1] + shifts[0:1]).astype(low)

    @pl.loop(0, 3 * inner // 384)
    def _(j):
        cols = lanes_at(j, 384)
        qkv[:, cols] = (dot(norm_a[...], attn[:, cols], NN) + in_bias[:, cols]).astype(low)

    wide = 2 * HEAD_DIM
    lane = lax.broadcasted_iota(jnp.int32, (1, wide), 1)
    in_head = [(lane < HEAD_DIM).astype(low), (lane >= HEAD_DIM).astype(low)]
    scale = 1.0 / math.sqrt(HEAD_DIM)
    pairs = inner // wide

    def head_lanes(j, which):
        return pl.ds(pl.multiple_of(which * inner + j * wide, wide), wide)

    @pl.loop(0, pairs)
    def _(j):
        q, k, v = (qkv[:, head_lanes(j, w)] for w in range(3))
        total = jnp.zeros((tokens, wide), jnp.float32)
        for h in range(2):
            scores = jnp.where(key_mask[...] > 0.0, dot(q * in_head[h], k, NT) * scale, -1e30)
            raised = jnp.exp(scores - jnp.max(scores, axis=-1, keepdims=True))
            p = raised / row_sum(raised)
            prob[2 * j + h] = p
            total = total + dot(p.astype(low), v * in_head[h], NN)
        ctx[:, lanes_at(j, wide)] = total.astype(low)

    def out_terms(r, j):
        return dot(ctx[r], attn[lanes_at(j, tile), pl.ds(3 * inner, inner)], NT)

    swap(1, out_terms)
    turned[1] = norm_a[...].T
    for h in range(halves):
        r = pl.ds(h * span, span)
        mid[r] = emb[r] + swapped(1, h) + out_bias[...]
        hat, _ = normed(mid[r], vit_epsilon)
        norm_b[r] = (hat * gains[1:2] + shifts[1:2]).astype(low)

    @pl.loop(0, units // tile)
    def _(j):
        cols = lanes_at(j, tile)
        pre = dot(norm_b[...], mlp[:, cols], NN) + up_bias[:, cols]
        phi, density = normal_parts(pre)
        act[:, cols] = (pre * phi).astype(low)
        slope[:, cols] = phi + pre * density

    def down_terms(r, j):
        return dot(act[r], mlp[lanes_at(j, tile), pl.ds(units, units)], NT)

    @pl.loop(0, units // tile)
    def _(j):
        cols = lanes_at(j, tile)
        d_act = dot(d_out[...], mlp[:, pl.ds(pl.multiple_of(units + j * tile, tile), tile)], NN).astype(low)
        d_pre[:, cols] = (d_act.astype(jnp.float32) * slope[:, cols]).astype(low)

    def up_terms(r, j):
        return dot(d_pre[r], mlp[lanes_at(j, tile), pl.ds(0, units)], NT)

    def weight_grad(turned_ref, x, out, start):
        @pl.loop(0, width // tile)
        def _(i):
            for j in range(x.shape[1] // 384):
                out[lanes_at(i, tile), pl.ds(start + j * 384, 384)] = dot(
                    turned_ref[lanes_at(i, tile)], x[:, j * 384 : (j + 1) * 384], NN
                ).astype(low)

    swap(2, up_terms)
    turned[2] = norm_b[...].T
    weight_grad(turned.at[2], d_pre, mlp_grad, 0)
    weight_grad(turned.at[0], act, mlp_grad, units)
    after_mlp()
    small_up_o[...] = column_sums(d_pre[...])
    small_o[5:6] = column_sums(d_out[...])

    def back_through(x, i, h, which):
        hat, r = normed(x, vit_epsilon)
        return norm_back(hat, r, swapped(i, h), gains[which : which + 1])

    sums = []
    for h in range(halves):
        r = pl.ds(h * span, span)
        d_x, gain, shift = back_through(mid[r], 2, h, 1)
        d_x = d_x + d_out[r].astype(jnp.float32)
        d_mid[r] = d_x
        d_att[r] = d_x.astype(low)
        sums.append((gain, shift))
    small_o[1:2] = sums[0][0] + sums[1][0]
    small_o[3:4] = sums[0][1] + sums[1][1]
    small_o[4:5] = column_sums(d_att[...])

    @pl.loop(0, inner // 384)
    def _(j):
        d_ctx[:, lanes_at(j, 384)] = dot(
            d_att[...], attn[:, pl.ds(pl.multiple_of(3 * inner + j * 384, 384), 384)], NN
        ).astype(low)

    @pl.loop(0, pairs)
    def _(j):
        q, k, v = (qkv[:, head_lanes(j, w)] for w in range(3))
        d_c = d_ctx[:, lanes_at(j, wide)]
        d_q = jnp.zeros((tokens, wide), jnp.float32)
        d_k, d_v = d_q, d_q
        for h in range(2):
            p = prob[2 * j + h]
            d_p = dot(d_c * in_head[h], v, NT)
            d_s = (p * (d_p - row_sum(p * d_p))).astype(low)
            d_q = d_q + dot(d_s, k * in_head[h], NN)
            d_k = d_k + dot(d_s, q * in_head[h], TN)
            d_v = d_v + dot(p.astype(low), d_c * in_head[h], TN)
        d_qkv[:, head_lanes(j, 0)] = (d_q * scale).astype(low)
        d_qkv[:, head_lanes(j, 1)] = (d_k * scale).astype(low)
        d_qkv[:, head_lanes(j, 2)] = d_v.astype(low)

    def in_terms(r, j):
        return dot(d_qkv[r], attn[lanes_at(j, tile), pl.ds(0, 3 * inner)], NT)

    swap(3, in_terms)
    weight_grad(turned.at[1], d_qkv, attn_grad, 0)
    turned[2] = d_att[...].T
    weight_grad(turned.at[2], ctx, attn_grad, 3 * inner)
    after_attn()
    sums = []
    for h in range(halves):
        r = pl.ds(h * span, span)
        d_x, gain, shift = back_through(emb[r], 3, h, 0)
        emb_grad_o[r] = (d_x + d_mid[r]).astype(low)
        sums.append((gain, shift))
    small_o[0:1] = sums[0][0] + sums[1][0]
    small_o[2:3] = sums[0][1] + sums[1][1]
    small_o[6:7] = column_sums(emb_grad_o[...])
    small_o[7:8] = jnp.zeros((1, width), jnp.float32)
    small_in_o[...] = column_sums(d_qkv[...])

    def finish():
        swap(4, down_terms)
        for h in range(halves):
            r = pl.ds(h * span, span)
            out_o[r] = ((mid[r] + swapped(4, h) + down_bias[...]) * row_scale[r]).astype(low)
        for i in range(3, 5):
            for h in range(halves):
                copies[i, h].wait_send()

    return finish


def layer_buffers(inner, units, tokens, width):
    f32, low = jnp.float32, jnp.bfloat16
    return [
        pltpu.VMEM((tokens, width), f32),
        pltpu.VMEM((tokens, width), f32),
        pltpu.VMEM((2, tokens, width), f32),
        pltpu.VMEM((2, tokens, width), f32),
        pltpu.VMEM((tokens, width), low),
        pltpu.VMEM((tokens, width), low),
        pltpu.VMEM((tokens, 3 * inner), low),
        pltpu.VMEM((inner // HEAD_DIM, tokens, tokens), f32),
        pltpu.VMEM((tokens, inner), low),
        pltpu.VMEM((tokens, units), low),
        pltpu.VMEM((tokens, units), f32),
        pltpu.VMEM((tokens, width), low),
        pltpu.VMEM((tokens, units), low),
        pltpu.VMEM((tokens, width), f32),
        pltpu.VMEM((tokens, width), low),
        pltpu.VMEM((tokens, inner), low),
        pltpu.VMEM((tokens, 3 * inner), low),
        pltpu.VMEM((3, width, tokens), low),
        pltpu.SemaphoreType.DMA((5, 2)),
        pltpu.SemaphoreType.DMA((5, 2)),
    ]


LAYER_INS, LAYER_BUFFERS, TURNED = 15, 20, 17


class Scatter:
    def __init__(self, n, grid, rows, attn, mlp, attn_acc, mlp_acc, attn_box, mlp_box, outs, send, recv):
        self.me, self.mp = lax.axis_index("dp"), lax.axis_index("mp")
        self.here, self.grid, self.depth, self.rows = coords(self.me, grid), grid, len(grid), rows
        self.orders = [order[::-1] for order in orders_of(grid)]
        self.send_sem, self.recv_sem, self.sends = send, recv, []
        self.pieces = []
        for src, acc, box, out in ((attn, attn_acc, attn_box, outs[:4]), (mlp, mlp_acc, mlp_box, outs[4:])):
            width, share = src.shape[-1] // len(self.orders), len(out) // len(self.orders)
            for i, order in enumerate(self.orders):
                cols, to = pl.ds(i * width, width), out[i * share : (i + 1) * share]
                self.pieces.append((src, acc, box, to, cols, order, len(self.pieces)))
        self.slots = {}
        for which, order in enumerate(self.orders):
            number = 0
            for t in range(self.depth):
                for shard in self.rest(order, t):
                    for k in range(1, grid[order[t]]):
                        self.slots[which, t, shard, k] = number
                        number += 1

    def rest(self, order, t):
        return sorted(offsets_in(self.grid, order[t + 1 :]), key=sum, reverse=True)

    def shard(self, ref, owner, cols):
        if len(ref.shape) == 2:
            return ref.at[pl.ds(pl.multiple_of(self.rows * owner, 16), self.rows), cols]
        return ref.at[owner, :, cols]

    def start(self, t, piece):
        src, acc, box, _, cols, order, p = piece
        held = src if t == 0 else acc
        for shard in self.rest(order, t):
            for k in range(1, self.grid[order[t]]):
                step = along(self.grid, order[t], k)
                owner = device_at(self.here, self.grid, tuple(i + j for i, j in zip(shard, step)))
                slot = self.slots[p % len(self.orders), t, shard, self.grid[order[t]] - k]
                there = (device_at(self.here, self.grid, step), self.mp)
                block = self.shard(held, owner, cols)
                self.sends.append(
                    remote(block, box.at[slot, :, cols], self.send_sem.at[p, slot], self.recv_sem.at[p, slot], there)
                )

    def add(self, t, piece):
        src, acc, box, outs, cols, order, p = piece
        held = src if t == 0 else acc
        for shard in self.rest(order, t):
            owner = device_at(self.here, self.grid, shard)
            total = self.shard(held, owner, cols)[...].astype(jnp.float32)
            for k in range(1, self.grid[order[t]]):
                slot = self.slots[p % len(self.orders), t, shard, k]
                arrived(box.at[slot, :, cols], self.recv_sem.at[p, slot])
                total = total + box[slot, :, cols].astype(jnp.float32)
            if t < self.depth - 1:
                self.shard(acc, owner, cols)[...] = total.astype(acc.dtype)
            else:
                width = total.shape[1] // len(outs)
                for i, out in enumerate(outs):
                    out[...] = total[:, i * width : (i + 1) * width]


BACK_BUFFERS = 20


def back_body(
    n, grid, scatter, ordered, finish, block_for,
    pix, kern, band_mask, emb_grad, small, small_up, small_in, patch_w,
    pixel_o, local_o, blocks_o, bias_o,
    w_half, d_pix, got, got32, code, terms, term_box, bias_half, load, local, a_send, a_recv, f_send, f_recv,
    c_send, c_recv, b_send, b_recv,
):
    me, mp = lax.axis_index("dp"), lax.axis_index("mp")
    here = coords(me, grid)
    depth = len(grid)
    partner = (me, 1 - mp)
    low = jnp.bfloat16
    bands, tokens, half = pix.shape
    rows = got.shape[2]
    lanes = lanes_at(mp, half)
    far = sorted(offsets_in(grid, range(depth))[1:], key=sum, reverse=True)
    first, second = ordered
    own, to_partner = [], []

    exchange = []
    for i, step in enumerate(far):
        there = device_at(here, grid, step)
        exchange.append(remote(block_for(there), got.at[me], a_send.at[i], a_recv.at[i], (there, mp)))
    own.append(pltpu.make_async_copy(block_for(me), got.at[me], local.at[0]))
    own[-1].start()
    finish()

    @pl.loop(0, bands)
    def _(b):
        made = dot(emb_grad[...], kern[b], NN) * band_mask[pl.ds(b, 1)]
        d_pix[b] = made.astype(low)

    own.append(pltpu.make_async_copy(d_pix, pixel_o.at[:, :, lanes], local.at[1]))
    own[-1].start()
    to_partner.append(remote(d_pix, pixel_o.at[:, :, lanes], f_send.at[0], f_recv.at[0], partner))

    lane = 128
    per_slot = terms.shape[1] - SPAN
    terms[...] = jnp.zeros_like(terms)
    chunks = []
    for r in range(4):
        chunks += [small[r : r + 1, i * lane : (i + 1) * lane] for i in range(small.shape[1] // lane)]
    inner = small_in.shape[1] // 3
    for start in (0, 2 * inner):
        chunks += [small_in[:, start + i * lane : start + (i + 1) * lane] for i in range(inner // lane)]
    chunks += [small[4:5, i * lane : (i + 1) * lane] for i in range(small.shape[1] // lane)]
    chunks += [small_up[:, i * lane : (i + 1) * lane] for i in range(small_up.shape[1] // lane)]
    chunks += [small[5:6, i * lane : (i + 1) * lane] for i in range(small.shape[1] // lane)]
    each = -(-len(chunks) // n)
    for i, chunk in enumerate(chunks):
        terms[i // each, SPAN + i % each : SPAN + i % each + 1] = chunk
    patch_grad = small[6:7]
    d_tail = exact(jnp.broadcast_to(patch_grad, (8, patch_grad.shape[1])), patch_w[...], NT)[:1]

    for t in range(depth):
        for piece in first:
            scatter.add(t, piece)
            if t + 1 < depth:
                scatter.start(t + 1, piece)
        for piece in second:
            scatter.add(t, piece)
            if t + 1 < depth:
                scatter.start(t + 1, piece)

    bias_half[...] = jnp.zeros_like(bias_half)

    def take(source):
        block = got[source].astype(jnp.float32)
        got32[source, :bands, :rows] = block
        got32[source, bands:, :rows] = jnp.zeros((SPAN - bands,) + block.shape[1:], jnp.float32)
        bias_half[...] = bias_half[...] + jnp.sum(block, axis=0)

    own[0].wait()
    take(me)
    for i in reversed(range(n - 1)):
        source = device_at(here, grid, minus((0,) * depth, far[i], grid))
        exchange[i].wait_recv()
        take(source)
    to_partner.append(remote(got, local_o.at[mp], f_send.at[1], f_recv.at[1], partner))
    own.append(pltpu.make_async_copy(got, local_o.at[mp], local.at[2]))
    own[-1].start()
    bias_o[:, lanes] = bias_half[...]
    to_partner.append(remote(bias_half, bias_o.at[:, lanes], f_send.at[2], f_recv.at[2], partner))

    load.wait()
    step = tiled(rows)
    w_rows = w_half.reshape(w_half.shape[0] * step, half)
    g_rows = got32.reshape(n * SPAN * step, half)
    code[...] = jnp.zeros_like(code)

    @pl.loop(0, rows // 2)
    def _(j):
        taken = [g_rows[pl.ds(2 * j + i, n * SPAN, stride=step), :].astype(low) for i in range(2)]
        weights = [w_rows[pl.ds(2 * j + i, w_half.shape[0], stride=step), :].astype(low) for i in range(2)]
        code[...] = code[...] + dot(jnp.concatenate(taken, axis=1), jnp.concatenate(weights, axis=1), NT)

    terms[:, :SPAN] = code[...].reshape(n, SPAN, code.shape[1])
    sums = []
    for k in range(1, n):
        there = lax.rem(me + k, n)
        slot = n - k
        sums.append(remote(terms.at[there], term_box.at[mp, slot], c_send.at[k], c_recv.at[slot], (there, mp)))
    for k in range(n):
        there = lax.rem(me + k, n)
        slot = (n - k) % n
        sums.append(
            remote(terms.at[there], term_box.at[mp, slot], c_send.at[n + k], c_recv.at[n + slot], (there, 1 - mp))
        )
    term_box[mp, 0] = terms[me]
    for copy in sums:
        copy.wait_recv()
    total = term_box[0, 0, :SPAN]
    for i in range(1, 2 * n):
        total = total + term_box[i // n, i % n, :SPAN]
    vectors = term_box[mp, 0, SPAN:]
    for k in range(1, n):
        vectors = vectors + term_box[mp, k, SPAN:]
    is_tail = lax.broadcasted_iota(jnp.int32, total.shape, 0) == bands
    blocks_o[me, :SPAN] = jnp.where(is_tail, d_tail, total)
    blocks_o[me, SPAN : SPAN + per_slot] = vectors
    for i in range(patch_grad.shape[1] // lane):
        r = SPAN + per_slot + i
        blocks_o[me, r : r + 1] = patch_grad[:, i * lane : (i + 1) * lane]
    back = []
    for k in range(1, n):
        there = lax.rem(me + k, n)
        back.append(remote(blocks_o.at[me], blocks_o.at[me], b_send.at[k - 1], b_recv.at[k - 1], (there, mp)))
    for copy in back + to_partner:
        copy.wait()
    for copy in sums + exchange + scatter.sends:
        copy.wait_send()
    for copy in own[1:]:
        copy.wait()


def back_shapes(n, bands, tokens, rows, half, width, inner, units, hyper_width):
    f32, low = jnp.float32, jnp.bfloat16
    chunks = (6 * width + 2 * inner + units) // 128
    per_slot = -(-(-(-chunks // n)) // 8) * 8
    block = SPAN + per_slot + width // 128 + -(width // 128) % 8
    outs = [((rows, inner), f32)] * 4 + [((rows, units), f32)] * 2
    outs += [
        ((bands, tokens, 2 * half), low),
        ((2, n, bands, rows, half), low),
        ((n, block, 128), f32),
        ((rows, 2 * half), f32),
    ]
    specs = [VMEM] * 6 + [ANY, ANY, VMEM, VMEM]
    buffers = [
        pltpu.VMEM((hyper_width, tiled(rows), half), f32),
        pltpu.VMEM((bands, tokens, half), low),
        pltpu.VMEM((n, bands, rows, half), low),
        pltpu.VMEM((n, SPAN, tiled(rows), half), f32),
        pltpu.VMEM((n * SPAN, hyper_width), f32),
        pltpu.VMEM((n, SPAN + per_slot, 128), f32),
        pltpu.VMEM((2, n, SPAN + per_slot, 128), f32),
        pltpu.VMEM((rows, half), f32),
        pltpu.SemaphoreType.DMA,
        pltpu.SemaphoreType.DMA((3,)),
        pltpu.SemaphoreType.DMA((n - 1,)),
        pltpu.SemaphoreType.DMA((n - 1,)),
        pltpu.SemaphoreType.DMA((3,)),
        pltpu.SemaphoreType.DMA((3,)),
        pltpu.SemaphoreType.DMA((2 * n,)),
        pltpu.SemaphoreType.DMA((2 * n,)),
        pltpu.SemaphoreType.DMA((n - 1,)),
        pltpu.SemaphoreType.DMA((n - 1,)),
    ]
    return outs, specs, buffers


def scatter_buffers(n, grid, rows, attn_lanes, mlp_lanes):
    low, pieces = jnp.bfloat16, 2 * len(orders_of(grid))
    return [
        pltpu.VMEM((n - 1, rows, attn_lanes), low),
        pltpu.VMEM((n - 1, rows, mlp_lanes), low),
        pltpu.SemaphoreType.DMA((pieces, n - 1)),
        pltpu.SemaphoreType.DMA((pieces, n - 1)),
    ]


def weight_load(kern_w, w_half, sem, mp):
    half = w_half.shape[2]
    copy = pltpu.make_async_copy(kern_w.at[:, :, lanes_at(mp, half)], first_rows(w_half, kern_w.shape[1]), sem)
    copy.start()
    return copy


def whole_kernel(n, grid, inner, *refs):
    ins, refs = refs[: LAYER_INS + 2], refs[LAYER_INS + 2 :]
    outs, refs = refs[:11], refs[11:]
    layer, refs = refs[:LAYER_BUFFERS], refs[LAYER_BUFFERS:]
    (emb_grad, attn_grad, mlp_grad, small, small_up, small_in, d_kern), refs = refs[:7], refs[7:]
    turned = layer[TURNED].at[2]
    (attn_box, mlp_box, g_send, g_recv), back = refs[:4], refs[4:]
    kern_w, patch_w = ins[LAYER_INS:]
    pix, kern, band_mask = ins[0], ins[1], ins[5]
    me, mp = lax.axis_index("dp"), lax.axis_index("mp")
    rows = back[2].shape[2]
    load = weight_load(kern_w, back[0], back[8], mp)
    greet(n, me, mp, True)
    scatter = Scatter(
        n, grid, rows, attn_grad, mlp_grad, attn_grad, mlp_grad, attn_box, mlp_box, outs[1:7], g_send, g_recv
    )
    half = len(scatter.pieces) // 2
    attn_pieces, mlp_pieces = scatter.pieces[:half], scatter.pieces[half:]

    def begin(pieces):
        for piece in pieces:
            scatter.start(0, piece)

    finish = layer_body(
        inner, lambda: begin(mlp_pieces), lambda: begin(attn_pieces), *ins[:LAYER_INS],
        outs[0], emb_grad, attn_grad, mlp_grad, small, small_up, small_in, *layer,
    )
    turned[...] = emb_grad[...].T
    tile = 256

    @pl.loop(0, pix.shape[0])
    def _(b):
        masked = pix[b] * band_mask[pl.ds(b, 1)].astype(pix.dtype)
        for i in range(turned.shape[0] // tile):
            part = slice(i * tile, (i + 1) * tile)
            d_kern[b, part] = dot(turned[part], masked, NN).astype(d_kern.dtype)

    def block_for(there):
        return d_kern.at[:, pl.ds(pl.multiple_of(rows * there, 16), rows)]

    back_body(
        n, grid, scatter, (mlp_pieces, attn_pieces), finish, block_for,
        pix, kern, band_mask, emb_grad, small, small_up, small_in, patch_w, *outs[7:], *back[:8], load, *back[9:],
    )


def layer_kernel(inner, *refs):
    me, mp = lax.axis_index("dp"), lax.axis_index("mp")
    sem = pltpu.get_barrier_semaphore()
    pl.semaphore_signal(sem, inc=1, device_id=(me, 1 - mp), device_id_type=MESH)
    pl.semaphore_wait(sem, 1)
    layer_body(inner, lambda: None, lambda: None, *refs)()


def back_kernel(n, grid, *refs):
    (pix, kern, band_mask, emb_grad, small, small_up, small_in, attn, mlp, d_kern, kern_w, patch_w), refs = refs[:12], refs[12:]
    outs, refs = refs[:10], refs[10:]
    (attn_acc, mlp_acc, attn_box, mlp_box, g_send, g_recv), back = refs[:6], refs[6:]
    me, mp = lax.axis_index("dp"), lax.axis_index("mp")
    load = weight_load(kern_w, back[0], back[8], mp)
    greet(n, me, mp, True)
    scatter = Scatter(
        n, grid, attn.shape[1], attn, mlp, attn_acc, mlp_acc, attn_box, mlp_box, outs[:6], g_send, g_recv
    )
    for piece in scatter.pieces:
        scatter.start(0, piece)
    back_body(
        n, grid, scatter, (scatter.pieces, []), lambda: None, lambda there: d_kern.at[there],
        pix, kern, band_mask, emb_grad, small, small_up, small_in, patch_w, *outs[6:], *back[:8], load, *back[9:],
    )


def layer_and_back(n, inner, kern_w, patch_w, layer_ins):
    pix, kern, attn, mlp, _, band_mask = layer_ins[:6]
    grid = factors_of(n)
    bands, tokens, half = pix.shape
    width, units = attn.shape[0], mlp.shape[1] // 2
    hyper_width, rows, _ = kern_w.shape
    f32, low = jnp.float32, jnp.bfloat16
    shape = jax.ShapeDtypeStruct
    outs, specs, buffers = back_shapes(n, bands, tokens, rows, half, width, inner, units, hyper_width)
    layer = layer_buffers(inner, units, tokens, width)
    layer_outs = [
        ((tokens, width), low),
        (attn.shape, low),
        (mlp.shape, low),
        ((8, width), f32),
        ((1, units), f32),
        ((1, 3 * inner), f32),
    ]
    flops = 2 * tokens * width * (3 * bands * half + 9 * inner * 2 + 9 * units)
    cost = pl.CostEstimate(flops=flops, bytes_accessed=3 * 10**7, transcendentals=10**6)
    scattered = scatter_buffers(n, grid, rows, attn.shape[1], mlp.shape[1])
    if rows % 16 == 0:
        return pl.pallas_call(
            partial(whole_kernel, n, grid, inner),
            out_shape=[shape((tokens, width), low)] + [shape(*o) for o in outs],
            in_specs=[VMEM] * LAYER_INS + [ANY, VMEM],
            out_specs=[VMEM] + specs,
            scratch_shapes=layer
            + [pltpu.VMEM(*o) for o in layer_outs]
            + [pltpu.VMEM((bands, width, half), low)]
            + scattered
            + buffers,
            compiler_params=params(2, BIG_VMEM),
            cost_estimate=cost,
            name="layer",
        )(*layer_ins, kern_w, patch_w)
    layer_out, emb_grad, attn_grad, mlp_grad, small, small_up, small_in = pl.pallas_call(
        partial(layer_kernel, inner),
        out_shape=[shape((tokens, width), low)] + [shape(*o) for o in layer_outs],
        in_specs=[VMEM] * LAYER_INS,
        out_specs=[VMEM] * 7,
        scratch_shapes=layer,
        compiler_params=params(3, BIG_VMEM),
        cost_estimate=cost,
        name="layer",
    )(*layer_ins)
    d_kern = fast_einsum("tc,btp->bcp", emb_grad, pix * band_mask[:bands, None].astype(low)).astype(low)
    d_kern = d_kern.reshape(bands, n, rows, half).transpose(1, 0, 2, 3)
    attn_grad, mlp_grad = attn_grad.reshape(n, rows, -1), mlp_grad.reshape(n, rows, -1)
    out = pl.pallas_call(
        partial(back_kernel, n, grid),
        out_shape=[shape(*o) for o in outs],
        in_specs=[VMEM] * 9 + [ANY, ANY, VMEM],
        out_specs=specs,
        scratch_shapes=[pltpu.VMEM(attn_grad.shape, low), pltpu.VMEM(mlp_grad.shape, low)] + scattered + buffers,
        compiler_params=params(2, BIG_VMEM),
        name="back",
    )(pix, kern, band_mask, emb_grad, small, small_up, small_in, attn_grad, mlp_grad, d_kern, kern_w, patch_w)
    return [layer_out] + list(out)


def tail_kernel(
    n, bands, per_slot, recompute,
    blocks, codes, facts, rows_k, wide_k, prob_k, w_attn, w_in, w_out, gain, shift, patch_w, local_grad,
    g_attn, g_in, g_out, g_gain, g_shift, g_token, g_patch, g_kern, n_gain, n_shift, in_bias, out_bias, up_bias, down_bias,
    rows_s, wide_s, prob_s, d_mlp, tails, got, got32, made, sem, store,
):
    low = jnp.bfloat16
    rows, half = got.shape[3], got.shape[4]
    step = tiled(rows)
    loads = []
    for i in range(2):
        loads.append(pltpu.make_async_copy(local_grad.at[i], got.at[i], sem.at[i]))
        loads[-1].start()

    stores = []
    for i in range(2):
        loads[i].wait()

        @pl.loop(0, n)
        def _(s):
            block = got[i, s].astype(jnp.float32)
            got32[s, :bands, :rows] = block
            got32[s, bands:, :rows] = jnp.zeros((SPAN - bands,) + block.shape[1:], jnp.float32)

        g_rows = got32.reshape(n * SPAN * step, half)
        m_rows = made.at[i].reshape(made.shape[1] * step, half)

        @pl.loop(0, rows // 2)
        def _(j):
            taken = [g_rows[pl.ds(2 * j + c, n * SPAN, stride=step), :].astype(low) for c in range(2)]
            both = dot(codes[...], jnp.concatenate(taken, axis=1), TN)
            for c in range(2):
                m_rows[pl.ds(2 * j + c, made.shape[1], stride=step), :] = both[:, c * half : (c + 1) * half]

        stores.append(pltpu.make_async_copy(first_rows(made.at[i], rows), g_kern.at[:, :, pl.ds(i * half, half)], store.at[i]))
        stores[-1].start()

    groups = n // GROUP

    def put(ref, where, value):
        ref[where] = value if groups == 1 else ref[where] + value

    outs = (g_attn, g_in, g_out, g_gain, g_shift)
    if groups > 1:
        for ref in outs:
            ref[...] = jnp.zeros_like(ref)
    token = jnp.zeros_like(g_token)
    for g in range(groups):
        kept = (rows_k, wide_k, prob_k)
        if recompute:
            kept = (rows_s, wide_s, prob_s)
            generator_forward(facts, g, w_attn, w_in, w_out, gain, shift, *kept)
        count = GROUP * SPAN
        d_second = blocks[pl.ds(g * GROUP, GROUP), :SPAN].reshape(count, blocks.shape[2])
        generator_backward(d_second, put, w_attn, w_in, w_out, gain, *kept, d_mlp, outs + (g_token,))
        tails[pl.ds(g * GROUP, GROUP)] = kept[0].at[SECOND][pl.ds(bands, GROUP, stride=SPAN), :]
        token = token + all_rows(d_mlp.at[0][pl.ds(bands, GROUP, stride=SPAN), :])
    g_token[...] = token
    lane = 128
    for i in range(g_patch.shape[1] // lane):
        g_patch[:, i * lane : (i + 1) * lane] = exact(tails[...], blocks[:, SPAN + per_slot + i, :], TN)

    chunks = []
    for ref, r in ((n_gain, 0), (n_gain, 1), (n_shift, 0), (n_shift, 1), (in_bias, 0), (in_bias, 1)):
        chunks += [(ref, r, i) for i in range(ref.shape[1] // lane)]
    for ref in (out_bias, up_bias, down_bias):
        chunks += [(ref, 0, i) for i in range(ref.shape[1] // lane)]
    each = -(-len(chunks) // n)
    for k, (ref, r, i) in enumerate(chunks):
        row = SPAN + k % each
        ref[r : r + 1, i * lane : (i + 1) * lane] = blocks[k // each, row : row + 1]
    for copy in stores:
        copy.wait()


def tail(n, bands, inner, units, blocks, codes, facts, kept, weights, patch_w, local_grad):
    w_attn, w_in, w_out, gain, shift = weights
    width = patch_w.shape[1]
    hyper_width = w_attn.shape[1]
    rows, half = local_grad.shape[3:]
    f32 = jnp.float32
    chunks = (6 * width + 2 * inner + units) // 128
    per_slot = -(-(-(-chunks // n)) // 8) * 8
    recompute = n > GROUP
    kept_shapes, _ = generator_scratch(hyper_width, w_in.shape[1])
    shapes = [
        w_attn.shape, w_in.shape, w_out.shape, gain.shape, shift.shape, (1, hyper_width), patch_w.shape,
        (hyper_width, rows, 2 * half), (2, width), (2, width), (2, inner), (1, width), (1, units), (1, width),
    ]
    return pl.pallas_call(
        partial(tail_kernel, n, bands, per_slot, recompute),
        out_shape=[jax.ShapeDtypeStruct(s, f32) for s in shapes],
        in_specs=[VMEM] * 12 + [ANY],
        out_specs=[VMEM] * 7 + [ANY] + [VMEM] * 6,
        scratch_shapes=[pltpu.VMEM(k if recompute else (8, 128), f32) for k in kept_shapes]
        + [
            pltpu.VMEM((2, GROUP * SPAN, hyper_width), f32),
            pltpu.VMEM((n, hyper_width), f32),
            pltpu.VMEM(local_grad.shape, local_grad.dtype),
            pltpu.VMEM((n, SPAN, tiled(rows), half), f32),
            pltpu.VMEM((2, hyper_width, tiled(rows), half), f32),
            pltpu.SemaphoreType.DMA((2,)),
            pltpu.SemaphoreType.DMA((2,)),
        ],
        compiler_params=pltpu.CompilerParams(vmem_limit_bytes=BIG_VMEM),
        name="tail",
    )(blocks, codes, facts, *kept, w_attn, w_in, w_out, gain, shift, patch_w, local_grad)


def fast_einsum(pattern, left_side, right_side):
    return jnp.einsum(pattern, left_side, right_side, preferred_element_type=jnp.float32)


def wave_embedding(wavelengths, model_width):
    half_width = model_width // 2
    frequency = 10000.0 ** (-jnp.arange(half_width, dtype=jnp.float32) * 2.0 / model_width)
    angles = wavelengths.astype(jnp.float32)[..., None] * frequency
    return jnp.concatenate([jnp.sin(angles), jnp.cos(angles)], axis=-1)


def per_device(
    n,
    pixels,
    band_count,
    wavelengths,
    size_class,
    token_keep,
    hyp_attn,
    hyp_mlp_in,
    hyp_mlp_out,
    hyp_gain,
    hyp_shift,
    bias_token,
    kern_weight,
    kern_bias,
    patch_bias_weight,
    norm_gain,
    norm_shift,
    attn_in,
    attn_in_bias,
    attn_out,
    attn_out_bias,
    mlp_in,
    mlp_in_bias,
    mlp_out,
    mlp_out_bias,
    cotangent,
):
    mp = lax.axis_index("mp")
    slot_count, bands, tokens, pix_size = pixels.shape
    assert slot_count == 1 and n % GROUP == 0 and bands + 1 <= SPAN
    hyper_width = hyp_attn.shape[1]
    half = pix_size // 2
    low = jnp.bfloat16
    inner, units = attn_in.shape[2], mlp_in.shape[1]

    band_valid = jnp.arange(SPAN) < band_count[0]
    sequence = jnp.concatenate([wave_embedding(wavelengths[0], hyper_width), bias_token[None]], axis=0)
    sequence = jnp.pad(sequence, ((0, SPAN - bands - 1), (0, 0)))
    usable = (band_valid & (jnp.arange(SPAN) < bands)) | (jnp.arange(SPAN) == bands)
    usable = jnp.broadcast_to(usable.astype(jnp.float32)[:, None], (SPAN, hyper_width))
    facts_own = jnp.concatenate([sequence, usable], axis=0)

    attn_shard = jnp.concatenate([attn_in[0], attn_in[1], attn_in[2], attn_out], axis=1).astype(low)
    mlp_shard = jnp.concatenate([mlp_in, mlp_out], axis=1).astype(low)
    weights = (hyp_attn, hyp_mlp_in, hyp_mlp_out, hyp_gain, hyp_shift)
    kernel, attn_all, mlp_all, facts, patch_rows, codes, *kept = front(
        n, bands, facts_own, *weights, patch_bias_weight, kern_weight, kern_bias, attn_shard, mlp_shard
    )

    live_rows = jnp.where(
        size_class[0] == 0, tokens * 49 // 256, jnp.where(size_class[0] == 1, tokens * 196 // 256, tokens)
    )
    position = jnp.arange(tokens)
    row_valid = position < live_rows
    key_valid = row_valid & ((token_keep[0] == 1) | (position == 0))
    input_bias = jnp.concatenate([attn_in_bias[0], jnp.zeros_like(attn_in_bias[0]), attn_in_bias[1]])
    layer_ins = (
        lax.dynamic_slice_in_dim(pixels[0], mp * half, half, 2),
        kernel,
        attn_all,
        mlp_all,
        cotangent[0],
        jnp.broadcast_to(band_valid.astype(jnp.float32)[:, None], (SPAN, half)),
        key_valid.astype(jnp.float32)[None],
        row_valid.astype(jnp.float32)[:, None],
        patch_rows[bands : bands + 1],
        norm_gain,
        norm_shift,
        input_bias[None],
        attn_out_bias[None],
        mlp_in_bias[None],
        mlp_out_bias[None],
    )
    (
        layer_out,
        grad_q,
        grad_k,
        grad_v,
        grad_attn_out,
        grad_mlp_in,
        grad_mlp_out,
        pixel_grad,
        local_grad,
        blocks,
        grad_kern_bias,
    ) = layer_and_back(n, inner, kern_weight, patch_bias_weight, layer_ins)
    (
        g_attn,
        g_in,
        g_out,
        g_gain,
        g_shift,
        g_token,
        g_patch,
        grad_kern_weight,
        grad_norm_gain,
        grad_norm_shift,
        grad_in_bias,
        grad_attn_out_bias,
        grad_mlp_in_bias,
        grad_mlp_out_bias,
    ) = tail(n, bands, inner, units, blocks, codes, facts, kept, weights, patch_bias_weight, local_grad)
    return (
        layer_out[None],
        pixel_grad[None],
        g_attn,
        g_in,
        g_out,
        g_gain,
        g_shift,
        g_token[0],
        grad_kern_weight,
        grad_kern_bias,
        g_patch,
        grad_norm_gain,
        grad_norm_shift,
        jnp.stack([grad_q, grad_k, grad_v]),
        grad_in_bias,
        grad_attn_out,
        grad_attn_out_bias[0],
        grad_mlp_in,
        grad_mlp_in_bias[0],
        grad_mlp_out,
        grad_mlp_out_bias[0],
    )


def solution(mesh):
    return jax.shard_map(
        partial(per_device, mesh.shape["dp"]),
        mesh=mesh,
        in_specs=(
            P("dp", None, None, None),
            P("dp"),
            P("dp", None),
            P("dp"),
            P("dp", None),
            P(),
            P(),
            P(),
            P(),
            P(),
            P(),
            P(None, "dp", None),
            P("dp", None),
            P(),
            P(),
            P(),
            P(None, "dp", "mp"),
            P(None, "mp"),
            P("dp", "mp"),
            P(),
            P("dp", "mp"),
            P("mp"),
            P("dp", "mp"),
            P(),
            P("dp", None, None),
        ),
        out_specs=(
            P("dp", None, None),
            P("dp", None, None, None),
            P(),
            P(),
            P(),
            P(),
            P(),
            P(),
            P(None, "dp", None),
            P("dp", None),
            P(),
            P(),
            P(),
            P(None, "dp", "mp"),
            P(None, "mp"),
            P("dp", "mp"),
            P(),
            P("dp", "mp"),
            P("mp"),
            P("dp", "mp"),
            P(),
        ),
        check_vma=False,
    )
```

```python
from functools import partial
import math

import jax
import jax.numpy as jnp
from jax import lax
from jax.experimental import pallas as pl
from jax.experimental.pallas import tpu as pltpu
from jax.sharding import PartitionSpec as P

HEAD_DIM = 64
HYP_HEADS = 4
MESH = pl.DeviceIdType.MESH
ANY = pl.BlockSpec(memory_space=pl.ANY)
VMEM = pl.BlockSpec(memory_space=pltpu.VMEM)
BIG_VMEM = 58 * 1024 * 1024

vit_epsilon = 1e-06
hyper_epsilon = 1e-05


def factors_of(n):
    return {16: (4, 2, 2), 128: (4, 8, 4)}.get(n, (n,))


def coords(me, grid):
    out = []
    for size in reversed(grid):
        out.append(lax.rem(me, size))
        me = me // size
    return out[::-1]


def device_at(position, grid, offset):
    index = 0
    for place, size, step in zip(position, grid, offset):
        index = index * size + (lax.rem(place + step, size) if step else place)
    return index


def offsets_in(grid, dims):
    out = [()]
    for dim, size in enumerate(grid):
        out = [o + (i,) for o in out for i in range(size if dim in dims else 1)]
    return out


def along(grid, dim, step):
    return tuple(step if d == dim else 0 for d in range(len(grid)))


def minus(a, b, grid):
    return tuple((i - j) % size for i, j, size in zip(a, b, grid))


def orders_of(grid):
    return [(0, 1, 2), (0, 2, 1)] if len(grid) == 3 else [tuple(range(len(grid)))]


def greet(n, me, mp, both):
    sem = pltpu.get_barrier_semaphore()
    for k in range(1, n):
        pl.semaphore_signal(sem, inc=1, device_id=(lax.rem(me + k, n), mp), device_id_type=MESH)
    if both:
        for k in range(n):
            pl.semaphore_signal(sem, inc=1, device_id=(lax.rem(me + k, n), 1 - mp), device_id_type=MESH)
    pl.semaphore_wait(sem, 2 * n - 1 if both else n - 1)


def remote(src, dst, send, recv, device):
    copy = pltpu.make_async_remote_copy(
        src_ref=src, dst_ref=dst, send_sem=send, recv_sem=recv, device_id=device, device_id_type=MESH
    )
    copy.start()
    return copy


def params(collective, limit=None):
    return pltpu.CompilerParams(collective_id=collective, has_side_effects=True, vmem_limit_bytes=limit)


NN, NT, TN = ((1,), (0,)), ((1,), (1,)), ((0,), (0,))
GROUP = 16
SPAN = 16


def dot(a, b, contract):
    return lax.dot_general(a, b, (contract, ((), ())), preferred_element_type=jnp.float32)


def exact(a, b, contract=NN):
    return lax.dot_general(
        a, b, (contract, ((), ())), precision=lax.Precision.HIGH, preferred_element_type=jnp.float32
    )


def lanes_at(i, width):
    return pl.ds(pl.multiple_of(i * width, width), width)


def row_mean(x):
    return jnp.mean(x, axis=-1, keepdims=True)


def row_sum(x):
    return jnp.sum(x, axis=-1, keepdims=True)


def all_rows(x):
    return jnp.sum(x, axis=0, keepdims=True)


def column_sums(x):
    return dot(jnp.ones((8, x.shape[0]), x.dtype), x, NN)[:1]


def normal_parts(x):
    return 0.5 + 0.5 * lax.erf(x * math.sqrt(0.5)), jnp.exp(-0.5 * x * x) * (1.0 / math.sqrt(2.0 * math.pi))


def normed(x, epsilon):
    center = x - row_mean(x)
    r = lax.rsqrt(row_mean(center * center) + epsilon)
    return center * r, r


def norm_back(hat, r, d_y, gain_row):
    u = d_y * gain_row
    return r * (u - row_mean(u) - hat * row_mean(u * hat)), all_rows(d_y * hat), all_rows(d_y)


def tiled(rows):
    return -(-rows // 8) * 8


def first_rows(ref, rows):
    return ref if ref.shape[-2] == rows else ref.at[:, pl.ds(0, rows)]


def under(conditions, step):
    if conditions:
        pl.when(conditions[0])(lambda: under(conditions[1:], step))
    else:
        step()


def arrived(block, sem):
    pltpu.make_async_copy(block, block, sem).wait()


SEQ, QUERY, KEY, VALUE, MIXED, HAT_A, FIRST, HAT_B, SECOND, SCALE_A, SCALE_B = range(11)


def head_masks(width):
    lane = lax.broadcasted_iota(jnp.int32, (1, width), 1)
    size = width // HYP_HEADS
    return [((lane >= h * size) & (lane < (h + 1) * size)).astype(jnp.float32) for h in range(HYP_HEADS)]


def generator_forward(facts, g, w_attn, w_in, w_out, gain, shift, rows, wide, prob):
    count, width = GROUP * SPAN, facts.shape[-1]
    block = facts[pl.ds(g * GROUP, GROUP)]
    seq = block[:, :SPAN].reshape(count, width)
    valid = block[:, SPAN:].reshape(count, width)
    columns = dot(jnp.ones((8, width), jnp.bfloat16), valid.astype(jnp.bfloat16), NT)[:1]
    slot = [lax.shift_right_logical(lax.broadcasted_iota(jnp.int32, (count, count), d), 4) for d in range(2)]
    allowed = (slot[0] == slot[1]) & (columns > 0.5)
    rows[SEQ] = seq
    for i in range(3):
        rows[QUERY + i] = exact(seq, w_attn[i])
    scale = 1.0 / math.sqrt(width // HYP_HEADS)
    mixed = jnp.zeros((count, width), jnp.float32)
    for h, mask in enumerate(head_masks(width)):
        scores = jnp.where(allowed, exact(rows[QUERY] * mask, rows[KEY], NT) * scale, -1e30)
        raised = jnp.exp(scores - jnp.max(scores, axis=-1, keepdims=True))
        weights = raised / row_sum(raised)
        prob[h] = weights
        mixed = mixed + exact(weights, rows[VALUE] * mask)
    rows[MIXED] = mixed
    hat, r = normed(seq + exact(mixed, w_attn[3]), hyper_epsilon)
    rows[HAT_A] = hat
    rows[SCALE_A] = jnp.broadcast_to(r, (count, width))
    rows[FIRST] = hat * gain[0:1] + shift[0:1]
    tile = 512

    @pl.loop(0, w_in.shape[1] // tile)
    def _(j):
        cols = lanes_at(j, tile)
        pre = exact(rows[FIRST], w_in[:, cols])
        phi, density = normal_parts(pre)
        wide[0, :, cols] = pre * phi
        wide[1, :, cols] = phi + pre * density

    rows[SECOND] = rows[FIRST]

    @pl.loop(0, w_in.shape[1] // tile)
    def _(j):
        cols = lanes_at(j, tile)
        rows[SECOND] = rows[SECOND] + exact(wide[0, :, cols], w_out[cols])

    hat, r = normed(rows[SECOND], hyper_epsilon)
    rows[HAT_B] = hat
    rows[SCALE_B] = jnp.broadcast_to(r, (count, width))
    rows[SECOND] = hat * gain[1:2] + shift[1:2]


def generator_backward(d_second, put, w_attn, w_in, w_out, gain, rows, wide, prob, d_mlp, outs):
    g_attn, g_in, g_out, g_gain, g_shift, g_token = outs
    width = d_second.shape[1]
    d_sum, gain_b, shift_b = norm_back(rows[HAT_B], rows[SCALE_B], d_second, gain[1:2])
    put(g_gain, slice(1, 2), gain_b)
    put(g_shift, slice(1, 2), shift_b)
    d_mlp[0] = d_sum
    d_mlp[1] = d_sum
    tile = 512

    @pl.loop(0, w_in.shape[1] // tile)
    def _(j):
        cols = lanes_at(j, tile)
        put(g_out, cols, exact(wide[0, :, cols], d_mlp[0], TN))
        d_pre = exact(d_mlp[0], w_out[cols], NT) * wide[1, :, cols]
        put(g_in, (slice(None), cols), exact(rows[FIRST], d_pre, TN))
        d_mlp[1] = d_mlp[1] + exact(d_pre, w_in[:, cols], NT)

    d_res, gain_a, shift_a = norm_back(rows[HAT_A], rows[SCALE_A], d_mlp[1], gain[0:1])
    put(g_gain, slice(0, 1), gain_a)
    put(g_shift, slice(0, 1), shift_a)
    put(g_attn, 3, exact(rows[MIXED], d_res, TN))
    d_mixed = exact(d_res, w_attn[3], NT)
    scale = 1.0 / math.sqrt(width // HYP_HEADS)
    d_q = jnp.zeros_like(d_res)
    d_k, d_v = d_q, d_q
    for h, mask in enumerate(head_masks(width)):
        p, d_m = prob[h], d_mixed * mask
        d_p = exact(d_m, rows[VALUE], NT)
        d_s = p * (d_p - row_sum(p * d_p)) * scale
        d_q = d_q + exact(d_s, rows[KEY] * mask)
        d_k = d_k + exact(d_s, rows[QUERY] * mask, TN)
        d_v = d_v + exact(p, d_m, TN)
    d_seq = d_res
    for i, grad in enumerate((d_q, d_k, d_v)):
        put(g_attn, i, exact(rows[SEQ], grad, TN))
        d_seq = d_seq + exact(grad, w_attn[i], NT)
    d_mlp[0] = d_seq


def generator_scratch(width, units):
    f32, count = jnp.float32, GROUP * SPAN
    return [(11, count, width), (2, count, units), (HYP_HEADS, count, count)], f32


def front_kernel(
    n, grid, direct, bands,
    facts_own, w_attn, w_in, w_out, gain, shift, patch_w, kern_w, kern_b, attn, mlp,
    kern_o, attn_o, mlp_o, facts, patch_o, codes_o, rows_o, wide_o, prob_o,
    second, w_half, b_half, k32, k16, local, f_send, f_recv, a_send, a_recv, g_send, g_recv,
):
    me, mp = lax.axis_index("dp"), lax.axis_index("mp")
    here = coords(me, grid)
    low = jnp.bfloat16
    rows, half = kern_w.shape[1], kern_w.shape[2] // 2
    lanes = lanes_at(mp, half)
    orders = orders_of(grid)
    depth = len(grid)
    everyone = offsets_in(grid, range(depth))
    zero = (0,) * depth

    def kern_slot():
        if direct:
            return kern_o.at[:, pl.ds(pl.multiple_of(rows * me, 16), rows)]
        return kern_o.at[me]

    load = pltpu.make_async_copy(kern_w.at[:, :, lanes], first_rows(w_half, rows), local.at[0])
    load.start()
    own = [
        pltpu.make_async_copy(attn, attn_o.at[me], local.at[1]),
        pltpu.make_async_copy(mlp, mlp_o.at[me], local.at[2]),
    ]
    for copy in own:
        copy.start()
    greet(n, me, mp, False)
    shares = []
    for k in range(1, n):
        there = (lax.rem(me + k, n), mp)
        shares.append(remote(facts_own, facts.at[me], f_send.at[k - 1], f_recv.at[k - 1], there))
    facts[me] = facts_own[...]

    pieces = []
    for src, dst in ((attn, attn_o), (mlp, mlp_o)):
        width = src.shape[1] // len(orders)
        for part, order in enumerate(orders):
            pieces.append((src, dst, pl.ds(part * width, width), order, len(pieces)))
    sends, count = [], [0] * len(pieces)
    size = grid[0]
    place = here[0]

    def send(piece, owner, there, conditions):
        src, dst, cols, _, p = piece
        held = src.at[:, cols] if owner is None else dst.at[owner, :, cols]
        owner = me if owner is None else owner
        remote(held, dst.at[owner, :, cols], g_send.at[p, count[p]], g_recv.at[p, owner], (there, mp))
        sends.append((conditions, src, cols, p, count[p]))
        count[p] += 1

    def spread(piece, owner, number, conditions):
        for dim in piece[3][number:]:
            for k in range(1, grid[dim]):
                send(piece, owner, device_at(here, grid, along(grid, dim, k)), conditions)

    def beside(piece, step, k):
        offset = along(grid, piece[3][1], k) if k else zero
        position = [place + step] + here[1:]
        return device_at(position, grid, offset)

    def arrive(piece, owner):
        _, dst, cols, _, p = piece
        arrived(dst.at[owner, :, cols], g_recv.at[p, owner])

    def neighbour(step):
        return device_at([place + step] + here[1:], grid, zero)

    def line(piece, d):
        for side in (-1, 1):
            inside = (place >= d) if side < 0 else (place + d < size)
            onward = (place + 1 < size) if side < 0 else (place > 0)

            @pl.when(inside)
            def _():
                owner = beside(piece, side * d, 0)
                arrive(piece, owner)

                @pl.when(onward)
                def _():
                    send(piece, owner, neighbour(-side), (inside, onward))

                spread(piece, owner, 1, (inside,))

    def other_lines(piece, d):
        if depth == 1:
            return
        for k in range(1, grid[piece[3][1]]):
            for side in (-1, 1) if d else (1,):
                inside = (place >= d) if side < 0 else (place + d < size)

                @pl.when(inside)
                def _():
                    owner = beside(piece, side * d, k)
                    arrive(piece, owner)
                    spread(piece, owner, 2, (inside,))

    for piece in pieces:
        for side in (-1, 1):
            onward = (place + 1 < size) if side < 0 else (place > 0)

            @pl.when(onward)
            def _():
                send(piece, None, neighbour(-side), (onward,))

        spread(piece, None, 1, ())

    for copy in shares:
        copy.wait_recv()
    position = lax.broadcasted_iota(jnp.int32, (GROUP * SPAN, facts.shape[-1]), 0)
    is_band = lax.rem(position, SPAN) < bands
    for g in range(n // GROUP):
        generator_forward(facts, g, w_attn, w_in, w_out, gain, shift, rows_o, wide_o, prob_o)
        group = pl.ds(g * GROUP * SPAN, GROUP * SPAN)
        second[group] = rows_o[SECOND]
        codes_o[group] = jnp.where(is_band, rows_o[SECOND] + rows_o[SEQ], 0.0).astype(low)
    patch_o[...] = exact(second[pl.ds(pl.multiple_of(me * SPAN, SPAN), SPAN)], patch_w[...])

    for piece in pieces:
        line(piece, 1)

    load.wait()
    b_half[...] = kern_b[:, lanes]
    step = tiled(rows)
    w_rows = w_half.reshape(w_half.shape[0] * step, half)
    k_rows = k32.reshape(n * SPAN * step, half)

    @pl.loop(0, rows // 2)
    def _(j):
        both = [w_rows[pl.ds(2 * j + i, w_half.shape[0], stride=step), :].astype(low) for i in range(2)]
        made = dot(codes_o[...], jnp.concatenate(both, axis=1), NN)
        for i in range(2):
            c = 2 * j + i
            k_rows[pl.ds(c, n * SPAN, stride=step), :] = made[:, i * half : (i + 1) * half] + b_half[pl.ds(c, 1)]

    exchange = []
    for i, away in enumerate(sorted(everyone[1:], key=sum, reverse=True)):
        there = device_at(here, grid, away)
        k16[there] = k32[there, :bands, :rows].astype(low)
        exchange.append(remote(k16.at[there], kern_slot(), a_send.at[i], a_recv.at[i], (there, mp)))
    k16[me] = k32[me, :bands, :rows].astype(low)
    own.append(pltpu.make_async_copy(k16.at[me], kern_slot(), local.at[3]))
    own[-1].start()

    for d in range(2, size):
        for piece in pieces:
            line(piece, d)
            other_lines(piece, d - 2)
    for d in range(max(size - 2, 0), size):
        for piece in pieces:
            other_lines(piece, d)
    for piece in pieces:
        order = piece[3]
        for shard in offsets_in(grid, order[2:]) if depth > 2 else []:
            if any(shard):
                for rest in offsets_in(grid, order[:2]):
                    arrive(piece, device_at(here, grid, tuple(i + j for i, j in zip(shard, rest))))
    for conditions, src, cols, p, i in sends:
        under(conditions, lambda: arrived(src.at[:, cols], g_send.at[p, i]))
    for copy in shares:
        copy.wait_send()
    for copy in exchange:
        copy.wait()
    for copy in own:
        copy.wait()


def front(n, bands, facts_own, w_attn, w_in, w_out, gain, shift, patch_w, kern_w, kern_b, attn, mlp):
    grid = factors_of(n)
    hyper_width, rows, pixels = kern_w.shape
    half = pixels // 2
    direct = rows % 16 == 0
    pieces = 2 * len(orders_of(grid))
    f32, low = jnp.float32, jnp.bfloat16
    kept, _ = generator_scratch(hyper_width, w_in.shape[1])
    kern_shape = (bands, rows * n, half) if direct else (n, bands, rows, half)
    shapes = [
        (kern_shape, low),
        ((n,) + attn.shape, low),
        ((n,) + mlp.shape, low),
        ((n,) + facts_own.shape, f32),
        ((SPAN, patch_w.shape[1]), f32),
        ((n * SPAN, hyper_width), low),
    ] + [(k, f32) for k in kept]
    out = pl.pallas_call(
        partial(front_kernel, n, grid, direct, bands),
        out_shape=[jax.ShapeDtypeStruct(*s) for s in shapes],
        in_specs=[VMEM] * 7 + [ANY, VMEM, ANY, ANY],
        out_specs=[ANY] * 3 + [VMEM] * 6,
        scratch_shapes=[
            pltpu.VMEM((n * SPAN, hyper_width), f32),
            pltpu.VMEM((hyper_width, tiled(rows), half), f32),
            pltpu.VMEM((rows, half), f32),
            pltpu.VMEM((n, SPAN, tiled(rows), half), f32),
            pltpu.VMEM((n, bands, rows, half), low),
            pltpu.SemaphoreType.DMA((4,)),
            pltpu.SemaphoreType.DMA((n - 1,)),
            pltpu.SemaphoreType.DMA((n - 1,)),
            pltpu.SemaphoreType.DMA((n - 1,)),
            pltpu.SemaphoreType.DMA((n - 1,)),
            pltpu.SemaphoreType.DMA((pieces, n + 2 * sum(grid) * grid[-1])),
            pltpu.SemaphoreType.DMA((pieces, n)),
        ],
        compiler_params=params(1, BIG_VMEM),
        name="front",
    )(facts_own, w_attn, w_in, w_out, gain, shift, patch_w, kern_w, kern_b, attn, mlp)
    kernel = out[0]
    if not direct:
        kernel = kernel.transpose(1, 0, 2, 3).reshape(bands, rows * n, half)
    return [kernel, out[1].reshape(n * rows, -1), out[2].reshape(n * rows, -1)] + list(out[3:])


def layer_body(
    inner, after_mlp, after_attn,
    pix, kern, attn, mlp, cot, band_mask, key_mask, row_scale, patch_bias, gains, shifts, in_bias, out_bias, up_bias, down_bias,
    out_o, emb_grad_o, attn_grad, mlp_grad, small_o, small_up_o, small_in_o,
    emb, mid, part, inbox, norm_a, norm_b, qkv, prob, ctx, act, slope, d_out, d_pre, d_mid, d_att, d_ctx, d_qkv, turned, send, recv,
):
    me, mp = lax.axis_index("dp"), lax.axis_index("mp")
    partner = (me, 1 - mp)
    low = jnp.bfloat16
    bands, tokens, _ = pix.shape
    width = emb.shape[1]
    units = act.shape[1]
    halves = 2
    span = tokens // halves
    tile = 256
    copies = {}

    def swap(i, compute):
        for h in range(halves):
            r = pl.ds(h * span, span)
            if i >= 2:
                copies[i - 2, h].wait_send()

            @pl.loop(0, width // tile)
            def _(j):
                part[i % 2, r, lanes_at(j, tile)] = compute(r, j)

            copies[i, h] = remote(part.at[i % 2, r], inbox.at[i % 2, r], send.at[i, h], recv.at[i, h], partner)

    def swapped(i, h):
        copies[i, h].wait_recv()
        r = pl.ds(h * span, span)
        return part[i % 2, r] + inbox[i % 2, r]

    def embed_terms(r, j):
        total = jnp.zeros((span, tile), jnp.float32)
        for b in range(bands):
            total = total + dot(pix[b, r] * band_mask[b : b + 1].astype(low), kern[b, lanes_at(j, tile)], NT)
        return total

    swap(0, embed_terms)
    d_out[...] = (cot[...].astype(jnp.float32) * row_scale[...]).astype(low)
    turned[0] = d_out[...].T
    for h in range(halves):
        r = pl.ds(h * span, span)
        emb[r] = swapped(0, h) + patch_bias[...]
        hat, _ = normed(emb[r], vit_epsilon)
        norm_a[r] = (hat * gains[0:1] + shifts[0:1]).astype(low)

    @pl.loop(0, 3 * inner // 384)
    def _(j):
        cols = lanes_at(j, 384)
        qkv[:, cols] = (dot(norm_a[...], attn[:, cols], NN) + in_bias[:, cols]).astype(low)

    wide = 2 * HEAD_DIM
    lane = lax.broadcasted_iota(jnp.int32, (1, wide), 1)
    in_head = [(lane < HEAD_DIM).astype(low), (lane >= HEAD_DIM).astype(low)]
    scale = 1.0 / math.sqrt(HEAD_DIM)
    pairs = inner // wide

    def head_lanes(j, which):
        return pl.ds(pl.multiple_of(which * inner + j * wide, wide), wide)

    @pl.loop(0, pairs)
    def _(j):
        q, k, v = (qkv[:, head_lanes(j, w)] for w in range(3))
        total = jnp.zeros((tokens, wide), jnp.float32)
        for h in range(2):
            scores = jnp.where(key_mask[...] > 0.0, dot(q * in_head[h], k, NT) * scale, -1e30)
            raised = jnp.exp(scores - jnp.max(scores, axis=-1, keepdims=True))
            p = raised / row_sum(raised)
            prob[2 * j + h] = p
            total = total + dot(p.astype(low), v * in_head[h], NN)
        ctx[:, lanes_at(j, wide)] = total.astype(low)

    def out_terms(r, j):
        return dot(ctx[r], attn[lanes_at(j, tile), pl.ds(3 * inner, inner)], NT)

    swap(1, out_terms)
    turned[1] = norm_a[...].T
    for h in range(halves):
        r = pl.ds(h * span, span)
        mid[r] = emb[r] + swapped(1, h) + out_bias[...]
        hat, _ = normed(mid[r], vit_epsilon)
        norm_b[r] = (hat * gains[1:2] + shifts[1:2]).astype(low)

    @pl.loop(0, units // tile)
    def _(j):
        cols = lanes_at(j, tile)
        pre = dot(norm_b[...], mlp[:, cols], NN) + up_bias[:, cols]
        phi, density = normal_parts(pre)
        act[:, cols] = (pre * phi).astype(low)
        slope[:, cols] = phi + pre * density

    def down_terms(r, j):
        return dot(act[r], mlp[lanes_at(j, tile), pl.ds(units, units)], NT)

    @pl.loop(0, units // tile)
    def _(j):
        cols = lanes_at(j, tile)
        d_act = dot(d_out[...], mlp[:, pl.ds(pl.multiple_of(units + j * tile, tile), tile)], NN).astype(low)
        d_pre[:, cols] = (d_act.astype(jnp.float32) * slope[:, cols]).astype(low)

    def up_terms(r, j):
        return dot(d_pre[r], mlp[lanes_at(j, tile), pl.ds(0, units)], NT)

    def weight_grad(turned_ref, x, out, start):
        @pl.loop(0, width // tile)
        def _(i):
            for j in range(x.shape[1] // 384):
                out[lanes_at(i, tile), pl.ds(start + j * 384, 384)] = dot(
                    turned_ref[lanes_at(i, tile)], x[:, j * 384 : (j + 1) * 384], NN
                ).astype(low)

    swap(2, up_terms)
    turned[2] = norm_b[...].T
    weight_grad(turned.at[2], d_pre, mlp_grad, 0)
    weight_grad(turned.at[0], act, mlp_grad, units)
    after_mlp()
    small_up_o[...] = column_sums(d_pre[...])
    small_o[5:6] = column_sums(d_out[...])

    def back_through(x, i, h, which):
        hat, r = normed(x, vit_epsilon)
        return norm_back(hat, r, swapped(i, h), gains[which : which + 1])

    sums = []
    for h in range(halves):
        r = pl.ds(h * span, span)
        d_x, gain, shift = back_through(mid[r], 2, h, 1)
        d_x = d_x + d_out[r].astype(jnp.float32)
        d_mid[r] = d_x
        d_att[r] = d_x.astype(low)
        sums.append((gain, shift))
    small_o[1:2] = sums[0][0] + sums[1][0]
    small_o[3:4] = sums[0][1] + sums[1][1]
    small_o[4:5] = column_sums(d_att[...])

    @pl.loop(0, inner // 384)
    def _(j):
        d_ctx[:, lanes_at(j, 384)] = dot(
            d_att[...], attn[:, pl.ds(pl.multiple_of(3 * inner + j * 384, 384), 384)], NN
        ).astype(low)

    @pl.loop(0, pairs)
    def _(j):
        q, k, v = (qkv[:, head_lanes(j, w)] for w in range(3))
        d_c = d_ctx[:, lanes_at(j, wide)]
        d_q = jnp.zeros((tokens, wide), jnp.float32)
        d_k, d_v = d_q, d_q
        for h in range(2):
            p = prob[2 * j + h]
            d_p = dot(d_c * in_head[h], v, NT)
            d_s = (p * (d_p - row_sum(p * d_p))).astype(low)
            d_q = d_q + dot(d_s, k * in_head[h], NN)
            d_k = d_k + dot(d_s, q * in_head[h], TN)
            d_v = d_v + dot(p.astype(low), d_c * in_head[h], TN)
        d_qkv[:, head_lanes(j, 0)] = (d_q * scale).astype(low)
        d_qkv[:, head_lanes(j, 1)] = (d_k * scale).astype(low)
        d_qkv[:, head_lanes(j, 2)] = d_v.astype(low)

    def in_terms(r, j):
        return dot(d_qkv[r], attn[lanes_at(j, tile), pl.ds(0, 3 * inner)], NT)

    swap(3, in_terms)
    weight_grad(turned.at[1], d_qkv, attn_grad, 0)
    turned[2] = d_att[...].T
    weight_grad(turned.at[2], ctx, attn_grad, 3 * inner)
    after_attn()
    sums = []
    for h in range(halves):
        r = pl.ds(h * span, span)
        d_x, gain, shift = back_through(emb[r], 3, h, 0)
        emb_grad_o[r] = (d_x + d_mid[r]).astype(low)
        sums.append((gain, shift))
    small_o[0:1] = sums[0][0] + sums[1][0]
    small_o[2:3] = sums[0][1] + sums[1][1]
    small_o[6:7] = column_sums(emb_grad_o[...])
    small_o[7:8] = jnp.zeros((1, width), jnp.float32)
    small_in_o[...] = column_sums(d_qkv[...])

    def finish():
        swap(4, down_terms)
        for h in range(halves):
            r = pl.ds(h * span, span)
            out_o[r] = ((mid[r] + swapped(4, h) + down_bias[...]) * row_scale[r]).astype(low)
        for i in range(3, 5):
            for h in range(halves):
                copies[i, h].wait_send()

    return finish


def layer_buffers(inner, units, tokens, width):
    f32, low = jnp.float32, jnp.bfloat16
    return [
        pltpu.VMEM((tokens, width), f32),
        pltpu.VMEM((tokens, width), f32),
        pltpu.VMEM((2, tokens, width), f32),
        pltpu.VMEM((2, tokens, width), f32),
        pltpu.VMEM((tokens, width), low),
        pltpu.VMEM((tokens, width), low),
        pltpu.VMEM((tokens, 3 * inner), low),
        pltpu.VMEM((inner // HEAD_DIM, tokens, tokens), f32),
        pltpu.VMEM((tokens, inner), low),
        pltpu.VMEM((tokens, units), low),
        pltpu.VMEM((tokens, units), f32),
        pltpu.VMEM((tokens, width), low),
        pltpu.VMEM((tokens, units), low),
        pltpu.VMEM((tokens, width), f32),
        pltpu.VMEM((tokens, width), low),
        pltpu.VMEM((tokens, inner), low),
        pltpu.VMEM((tokens, 3 * inner), low),
        pltpu.VMEM((3, width, tokens), low),
        pltpu.SemaphoreType.DMA((5, 2)),
        pltpu.SemaphoreType.DMA((5, 2)),
    ]


LAYER_INS, LAYER_BUFFERS, TURNED = 15, 20, 17


class Scatter:
    def __init__(self, n, grid, rows, attn, mlp, attn_acc, mlp_acc, attn_box, mlp_box, outs, send, recv):
        self.me, self.mp = lax.axis_index("dp"), lax.axis_index("mp")
        self.here, self.grid, self.rows = coords(self.me, grid), grid, rows
        self.size, self.place = grid[0], self.here[0]
        self.orders = [order[:0:-1] for order in orders_of(grid)]
        self.stages = len(grid) - 1
        self.send_sem, self.recv_sem, self.sends = send, recv, []
        self.pieces = []
        for src, acc, box, out in ((attn, attn_acc, attn_box, outs[:4]), (mlp, mlp_acc, mlp_box, outs[4:])):
            width, share = src.shape[-1] // len(self.orders), len(out) // len(self.orders)
            for i, order in enumerate(self.orders):
                cols, to = pl.ds(i * width, width), out[i * share : (i + 1) * share]
                self.pieces.append((src, acc, box, to, cols, order, len(self.pieces)))
        self.slots = {}
        for which, order in enumerate(self.orders):
            number = 0
            for t in range(self.stages):
                for shard in self.rest(order, t):
                    for k in range(1, grid[order[t]]):
                        self.slots[which, t, shard, k] = number
                        number += 1
        self.line_slots = number if self.stages else 0

    def rest(self, order, t):
        return sorted(offsets_in(self.grid, (0,) + order[t + 1 :]), key=sum, reverse=True)

    def shard(self, ref, owner, cols):
        if len(ref.shape) == 2:
            return ref.at[pl.ds(pl.multiple_of(self.rows * owner, 16), self.rows), cols]
        return ref.at[owner, :, cols]

    def send(self, block, piece, index, slot, there, conditions=()):
        _, _, box, _, cols, _, p = piece
        remote(block, box.at[slot, :, cols], self.send_sem.at[p, index], self.recv_sem.at[p, slot], (there, self.mp))
        self.sends.append((conditions, box, cols, p, index))

    def receive(self, piece, slot):
        _, _, box, _, cols, _, p = piece
        arrived(box.at[slot, :, cols], self.recv_sem.at[p, slot])
        return box[slot, :, cols].astype(jnp.float32)

    def start(self, t, piece):
        src, acc, _, _, cols, order, p = piece
        held = src if t == 0 else acc
        for shard in self.rest(order, t):
            for k in range(1, self.grid[order[t]]):
                step = along(self.grid, order[t], k)
                owner = device_at(self.here, self.grid, tuple(i + j for i, j in zip(shard, step)))
                slot = self.slots[p % len(self.orders), t, shard, self.grid[order[t]] - k]
                self.send(self.shard(held, owner, cols), piece, slot, slot, device_at(self.here, self.grid, step))

    def add(self, t, piece):
        src, acc, _, _, cols, order, p = piece
        held = src if t == 0 else acc
        for shard in self.rest(order, t):
            owner = device_at(self.here, self.grid, shard)
            total = self.shard(held, owner, cols)[...].astype(jnp.float32)
            for k in range(1, self.grid[order[t]]):
                total = total + self.receive(piece, self.slots[p % len(self.orders), t, shard, k])
            self.shard(acc, owner, cols)[...] = total.astype(acc.dtype)

    def on_line(self, step):
        return device_at([self.place + step] + self.here[1:], self.grid, (0,) * len(self.grid))

    def pass_on(self, piece, j):
        src, acc, _, _, cols, _, p = piece
        held = acc if self.stages else src
        for side in (1, -1):
            inside = (self.place + j < self.size) if side > 0 else (self.place >= j)
            behind = (self.place > 0) if side > 0 else (self.place + 1 < self.size)

            @pl.when(inside)
            def _():
                mine = self.shard(held, self.on_line(side * j), cols)
                target = self.shard(acc, self.on_line(side * j), cols)
                slot = self.line_slots + self.place + side * j

                @pl.when(behind)
                def _():
                    target[...] = (mine[...].astype(jnp.float32) + self.receive(piece, slot)).astype(acc.dtype)

                if not self.stages:

                    @pl.when(jnp.logical_not(behind))
                    def _():
                        target[...] = mine[...]

                to = self.line_slots + self.size if side < 0 and j == 1 else slot
                index = self.line_slots + 2 * j + (side > 0) - 2
                self.send(target, piece, index, to, self.on_line(side), (inside,))

    def end(self, piece):
        src, acc, box, outs, cols, _, _ = piece
        held = acc if self.stages else src
        total = self.shard(held, self.me, cols)[...].astype(jnp.float32)
        width = total.shape[1] // len(outs)
        for i, out in enumerate(outs):
            out[...] = total[:, i * width : (i + 1) * width]
        for condition, slot in (
            (self.place > 0, self.line_slots + self.place),
            (self.place + 1 < self.size, self.line_slots + self.size),
        ):

            @pl.when(condition)
            def _():
                more = self.receive(piece, slot)
                for i, out in enumerate(outs):
                    out[...] = out[...] + more[:, i * width : (i + 1) * width]


BACK_BUFFERS = 20


def back_body(
    n, grid, scatter, ordered, finish, block_for,
    pix, kern, band_mask, emb_grad, small, small_up, small_in, patch_w,
    pixel_o, local_o, blocks_o, bias_o,
    w_half, d_pix, got, got32, code, terms, term_box, bias_half, load, local, a_send, a_recv, f_send, f_recv,
    c_send, c_recv, b_send, b_recv,
):
    me, mp = lax.axis_index("dp"), lax.axis_index("mp")
    here = coords(me, grid)
    depth = len(grid)
    partner = (me, 1 - mp)
    low = jnp.bfloat16
    bands, tokens, half = pix.shape
    rows = got.shape[2]
    lanes = lanes_at(mp, half)
    far = sorted(offsets_in(grid, range(depth))[1:], key=sum, reverse=True)
    own, to_partner = [], []

    exchange = []
    for i, step in enumerate(far):
        there = device_at(here, grid, step)
        exchange.append(remote(block_for(there), got.at[me], a_send.at[i], a_recv.at[i], (there, mp)))
    own.append(pltpu.make_async_copy(block_for(me), got.at[me], local.at[0]))
    own[-1].start()
    finish()

    @pl.loop(0, bands)
    def _(b):
        made = dot(emb_grad[...], kern[b], NN) * band_mask[pl.ds(b, 1)]
        d_pix[b] = made.astype(low)

    own.append(pltpu.make_async_copy(d_pix, pixel_o.at[:, :, lanes], local.at[1]))
    own[-1].start()
    to_partner.append(remote(d_pix, pixel_o.at[:, :, lanes], f_send.at[0], f_recv.at[0], partner))

    lane = 128
    per_slot = terms.shape[1] - SPAN
    terms[...] = jnp.zeros_like(terms)
    chunks = []
    for r in range(4):
        chunks += [small[r : r + 1, i * lane : (i + 1) * lane] for i in range(small.shape[1] // lane)]
    inner = small_in.shape[1] // 3
    for start in (0, 2 * inner):
        chunks += [small_in[:, start + i * lane : start + (i + 1) * lane] for i in range(inner // lane)]
    chunks += [small[4:5, i * lane : (i + 1) * lane] for i in range(small.shape[1] // lane)]
    chunks += [small_up[:, i * lane : (i + 1) * lane] for i in range(small_up.shape[1] // lane)]
    chunks += [small[5:6, i * lane : (i + 1) * lane] for i in range(small.shape[1] // lane)]
    each = -(-len(chunks) // n)
    for i, chunk in enumerate(chunks):
        terms[i // each, SPAN + i % each : SPAN + i % each + 1] = chunk
    patch_grad = small[6:7]
    d_tail = exact(jnp.broadcast_to(patch_grad, (8, patch_grad.shape[1])), patch_w[...], NT)[:1]

    for t in range(scatter.stages):
        for piece in ordered:
            scatter.add(t, piece)
            if t + 1 < scatter.stages:
                scatter.start(t + 1, piece)
    for piece in ordered:
        scatter.pass_on(piece, scatter.size - 1)

    bias_half[...] = jnp.zeros_like(bias_half)

    def take(source):
        block = got[source].astype(jnp.float32)
        got32[source, :bands, :rows] = block
        got32[source, bands:, :rows] = jnp.zeros((SPAN - bands,) + block.shape[1:], jnp.float32)
        bias_half[...] = bias_half[...] + jnp.sum(block, axis=0)

    own[0].wait()
    take(me)
    for i in reversed(range(n - 1)):
        source = device_at(here, grid, minus((0,) * depth, far[i], grid))
        exchange[i].wait_recv()
        take(source)
    to_partner.append(remote(got, local_o.at[mp], f_send.at[1], f_recv.at[1], partner))
    own.append(pltpu.make_async_copy(got, local_o.at[mp], local.at[2]))
    own[-1].start()
    bias_o[:, lanes] = bias_half[...]
    to_partner.append(remote(bias_half, bias_o.at[:, lanes], f_send.at[2], f_recv.at[2], partner))

    load.wait()
    step = tiled(rows)
    w_rows = w_half.reshape(w_half.shape[0] * step, half)
    g_rows = got32.reshape(n * SPAN * step, half)
    code[...] = jnp.zeros_like(code)

    @pl.loop(0, rows // 2)
    def _(j):
        taken = [g_rows[pl.ds(2 * j + i, n * SPAN, stride=step), :].astype(low) for i in range(2)]
        weights = [w_rows[pl.ds(2 * j + i, w_half.shape[0], stride=step), :].astype(low) for i in range(2)]
        code[...] = code[...] + dot(jnp.concatenate(taken, axis=1), jnp.concatenate(weights, axis=1), NT)

    terms[:, :SPAN] = code[...].reshape(n, SPAN, code.shape[1])
    sums = []
    for k in range(1, n):
        there = lax.rem(me + k, n)
        slot = n - k
        sums.append(remote(terms.at[there], term_box.at[mp, slot], c_send.at[k], c_recv.at[slot], (there, mp)))
    for k in range(n):
        there = lax.rem(me + k, n)
        slot = (n - k) % n
        sums.append(
            remote(terms.at[there], term_box.at[mp, slot], c_send.at[n + k], c_recv.at[n + slot], (there, 1 - mp))
        )
    term_box[mp, 0] = terms[me]
    for copy in sums:
        copy.wait_recv()
    total = term_box[0, 0, :SPAN]
    for i in range(1, 2 * n):
        total = total + term_box[i // n, i % n, :SPAN]
    vectors = term_box[mp, 0, SPAN:]
    for k in range(1, n):
        vectors = vectors + term_box[mp, k, SPAN:]
    is_tail = lax.broadcasted_iota(jnp.int32, total.shape, 0) == bands
    blocks_o[me, :SPAN] = jnp.where(is_tail, d_tail, total)
    blocks_o[me, SPAN : SPAN + per_slot] = vectors
    for i in range(patch_grad.shape[1] // lane):
        r = SPAN + per_slot + i
        blocks_o[me, r : r + 1] = patch_grad[:, i * lane : (i + 1) * lane]
    back = []
    for k in range(1, n):
        there = lax.rem(me + k, n)
        back.append(remote(blocks_o.at[me], blocks_o.at[me], b_send.at[k - 1], b_recv.at[k - 1], (there, mp)))
    for j in reversed(range(1, scatter.size - 1)):
        for piece in ordered:
            scatter.pass_on(piece, j)
    for piece in ordered:
        scatter.end(piece)
    for copy in back + to_partner:
        copy.wait()
    for copy in sums + exchange:
        copy.wait_send()
    for conditions, box, cols, p, i in scatter.sends:
        under(conditions, lambda: arrived(box.at[0, :, cols], scatter.send_sem.at[p, i]))
    for copy in own[1:]:
        copy.wait()


def back_shapes(n, bands, tokens, rows, half, width, inner, units, hyper_width):
    f32, low = jnp.float32, jnp.bfloat16
    chunks = (6 * width + 2 * inner + units) // 128
    per_slot = -(-(-(-chunks // n)) // 8) * 8
    block = SPAN + per_slot + width // 128 + -(width // 128) % 8
    outs = [((rows, inner), f32)] * 4 + [((rows, units), f32)] * 2
    outs += [
        ((bands, tokens, 2 * half), low),
        ((2, n, bands, rows, half), low),
        ((n, block, 128), f32),
        ((rows, 2 * half), f32),
    ]
    specs = [VMEM] * 6 + [ANY, ANY, VMEM, VMEM]
    buffers = [
        pltpu.VMEM((hyper_width, tiled(rows), half), f32),
        pltpu.VMEM((bands, tokens, half), low),
        pltpu.VMEM((n, bands, rows, half), low),
        pltpu.VMEM((n, SPAN, tiled(rows), half), f32),
        pltpu.VMEM((n * SPAN, hyper_width), f32),
        pltpu.VMEM((n, SPAN + per_slot, 128), f32),
        pltpu.VMEM((2, n, SPAN + per_slot, 128), f32),
        pltpu.VMEM((rows, half), f32),
        pltpu.SemaphoreType.DMA,
        pltpu.SemaphoreType.DMA((3,)),
        pltpu.SemaphoreType.DMA((n - 1,)),
        pltpu.SemaphoreType.DMA((n - 1,)),
        pltpu.SemaphoreType.DMA((3,)),
        pltpu.SemaphoreType.DMA((3,)),
        pltpu.SemaphoreType.DMA((2 * n,)),
        pltpu.SemaphoreType.DMA((2 * n,)),
        pltpu.SemaphoreType.DMA((n - 1,)),
        pltpu.SemaphoreType.DMA((n - 1,)),
    ]
    return outs, specs, buffers


def scatter_buffers(n, grid, rows, attn_lanes, mlp_lanes):
    low, pieces = jnp.bfloat16, 2 * len(orders_of(grid))
    slots = n - grid[0] + grid[0] + 1
    return [
        pltpu.VMEM((slots, rows, attn_lanes), low),
        pltpu.VMEM((slots, rows, mlp_lanes), low),
        pltpu.SemaphoreType.DMA((pieces, slots + grid[0])),
        pltpu.SemaphoreType.DMA((pieces, slots)),
    ]


def weight_load(kern_w, w_half, sem, mp):
    half = w_half.shape[2]
    copy = pltpu.make_async_copy(kern_w.at[:, :, lanes_at(mp, half)], first_rows(w_half, kern_w.shape[1]), sem)
    copy.start()
    return copy


def whole_kernel(n, grid, inner, *refs):
    ins, refs = refs[: LAYER_INS + 2], refs[LAYER_INS + 2 :]
    outs, refs = refs[:11], refs[11:]
    layer, refs = refs[:LAYER_BUFFERS], refs[LAYER_BUFFERS:]
    (emb_grad, attn_grad, mlp_grad, small, small_up, small_in, d_kern), refs = refs[:7], refs[7:]
    turned = layer[TURNED].at[2]
    (attn_box, mlp_box, g_send, g_recv), back = refs[:4], refs[4:]
    kern_w, patch_w = ins[LAYER_INS:]
    pix, kern, band_mask = ins[0], ins[1], ins[5]
    me, mp = lax.axis_index("dp"), lax.axis_index("mp")
    rows = back[2].shape[2]
    load = weight_load(kern_w, back[0], back[8], mp)
    greet(n, me, mp, True)
    scatter = Scatter(
        n, grid, rows, attn_grad, mlp_grad, attn_grad, mlp_grad, attn_box, mlp_box, outs[1:7], g_send, g_recv
    )
    half = len(scatter.pieces) // 2
    attn_pieces, mlp_pieces = scatter.pieces[:half], scatter.pieces[half:]

    def begin(pieces):
        for piece in pieces:
            if scatter.stages:
                scatter.start(0, piece)

    finish = layer_body(
        inner, lambda: begin(mlp_pieces), lambda: begin(attn_pieces), *ins[:LAYER_INS],
        outs[0], emb_grad, attn_grad, mlp_grad, small, small_up, small_in, *layer,
    )
    turned[...] = emb_grad[...].T
    tile = 256

    @pl.loop(0, pix.shape[0])
    def _(b):
        masked = pix[b] * band_mask[pl.ds(b, 1)].astype(pix.dtype)
        for i in range(turned.shape[0] // tile):
            part = slice(i * tile, (i + 1) * tile)
            d_kern[b, part] = dot(turned[part], masked, NN).astype(d_kern.dtype)

    def block_for(there):
        return d_kern.at[:, pl.ds(pl.multiple_of(rows * there, 16), rows)]

    back_body(
        n, grid, scatter, mlp_pieces + attn_pieces, finish, block_for,
        pix, kern, band_mask, emb_grad, small, small_up, small_in, patch_w, *outs[7:], *back[:8], load, *back[9:],
    )


def layer_kernel(inner, *refs):
    me, mp = lax.axis_index("dp"), lax.axis_index("mp")
    sem = pltpu.get_barrier_semaphore()
    pl.semaphore_signal(sem, inc=1, device_id=(me, 1 - mp), device_id_type=MESH)
    pl.semaphore_wait(sem, 1)
    layer_body(inner, lambda: None, lambda: None, *refs)()


def back_kernel(n, grid, *refs):
    (pix, kern, band_mask, emb_grad, small, small_up, small_in, attn, mlp, d_kern, kern_w, patch_w), refs = refs[:12], refs[12:]
    outs, refs = refs[:10], refs[10:]
    (attn_acc, mlp_acc, attn_box, mlp_box, g_send, g_recv), back = refs[:6], refs[6:]
    me, mp = lax.axis_index("dp"), lax.axis_index("mp")
    load = weight_load(kern_w, back[0], back[8], mp)
    greet(n, me, mp, True)
    scatter = Scatter(
        n, grid, attn.shape[1], attn, mlp, attn_acc, mlp_acc, attn_box, mlp_box, outs[:6], g_send, g_recv
    )
    for piece in scatter.pieces:
        if scatter.stages:
            scatter.start(0, piece)
    back_body(
        n, grid, scatter, scatter.pieces, lambda: None, lambda there: d_kern.at[there],
        pix, kern, band_mask, emb_grad, small, small_up, small_in, patch_w, *outs[6:], *back[:8], load, *back[9:],
    )


def layer_and_back(n, inner, kern_w, patch_w, layer_ins):
    pix, kern, attn, mlp, _, band_mask = layer_ins[:6]
    grid = factors_of(n)
    bands, tokens, half = pix.shape
    width, units = attn.shape[0], mlp.shape[1] // 2
    hyper_width, rows, _ = kern_w.shape
    f32, low = jnp.float32, jnp.bfloat16
    shape = jax.ShapeDtypeStruct
    outs, specs, buffers = back_shapes(n, bands, tokens, rows, half, width, inner, units, hyper_width)
    layer = layer_buffers(inner, units, tokens, width)
    layer_outs = [
        ((tokens, width), low),
        (attn.shape, low),
        (mlp.shape, low),
        ((8, width), f32),
        ((1, units), f32),
        ((1, 3 * inner), f32),
    ]
    flops = 2 * tokens * width * (3 * bands * half + 9 * inner * 2 + 9 * units)
    cost = pl.CostEstimate(flops=flops, bytes_accessed=3 * 10**7, transcendentals=10**6)
    scattered = scatter_buffers(n, grid, rows, attn.shape[1], mlp.shape[1])
    if rows % 16 == 0:
        return pl.pallas_call(
            partial(whole_kernel, n, grid, inner),
            out_shape=[shape((tokens, width), low)] + [shape(*o) for o in outs],
            in_specs=[VMEM] * LAYER_INS + [ANY, VMEM],
            out_specs=[VMEM] + specs,
            scratch_shapes=layer
            + [pltpu.VMEM(*o) for o in layer_outs]
            + [pltpu.VMEM((bands, width, half), low)]
            + scattered
            + buffers,
            compiler_params=params(2, BIG_VMEM),
            cost_estimate=cost,
            name="layer",
        )(*layer_ins, kern_w, patch_w)
    layer_out, emb_grad, attn_grad, mlp_grad, small, small_up, small_in = pl.pallas_call(
        partial(layer_kernel, inner),
        out_shape=[shape((tokens, width), low)] + [shape(*o) for o in layer_outs],
        in_specs=[VMEM] * LAYER_INS,
        out_specs=[VMEM] * 7,
        scratch_shapes=layer,
        compiler_params=params(3, BIG_VMEM),
        cost_estimate=cost,
        name="layer",
    )(*layer_ins)
    d_kern = fast_einsum("tc,btp->bcp", emb_grad, pix * band_mask[:bands, None].astype(low)).astype(low)
    d_kern = d_kern.reshape(bands, n, rows, half).transpose(1, 0, 2, 3)
    attn_grad, mlp_grad = attn_grad.reshape(n, rows, -1), mlp_grad.reshape(n, rows, -1)
    out = pl.pallas_call(
        partial(back_kernel, n, grid),
        out_shape=[shape(*o) for o in outs],
        in_specs=[VMEM] * 9 + [ANY, ANY, VMEM],
        out_specs=specs,
        scratch_shapes=[pltpu.VMEM(attn_grad.shape, low), pltpu.VMEM(mlp_grad.shape, low)] + scattered + buffers,
        compiler_params=params(2, BIG_VMEM),
        name="back",
    )(pix, kern, band_mask, emb_grad, small, small_up, small_in, attn_grad, mlp_grad, d_kern, kern_w, patch_w)
    return [layer_out] + list(out)


def tail_kernel(
    n, bands, per_slot, recompute,
    blocks, codes, facts, rows_k, wide_k, prob_k, w_attn, w_in, w_out, gain, shift, patch_w, local_grad,
    g_attn, g_in, g_out, g_gain, g_shift, g_token, g_patch, g_kern, n_gain, n_shift, in_bias, out_bias, up_bias, down_bias,
    rows_s, wide_s, prob_s, d_mlp, tails, turned, got, got32, made, sem, store,
):
    low = jnp.bfloat16
    rows, half = got.shape[3], got.shape[4]
    step = tiled(rows)
    loads = []
    for i in range(2):
        loads.append(pltpu.make_async_copy(local_grad.at[i], got.at[i], sem.at[i]))
        loads[-1].start()

    turned[...] = codes[...].T

    stores = []
    for i in range(2):
        loads[i].wait()

        @pl.loop(0, n)
        def _(s):
            block = got[i, s].astype(jnp.float32)
            got32[s, :bands, :rows] = block
            got32[s, bands:, :rows] = jnp.zeros((SPAN - bands,) + block.shape[1:], jnp.float32)

        g_rows = got32.reshape(n * SPAN * step, half)
        m_rows = made.at[i].reshape(made.shape[1] * step, half)

        @pl.loop(0, rows // 2, unroll=3)
        def _(j):
            taken = [g_rows[pl.ds(2 * j + c, n * SPAN, stride=step), :].astype(low) for c in range(2)]
            both = dot(turned[...], jnp.concatenate(taken, axis=1), NN)
            for c in range(2):
                m_rows[pl.ds(2 * j + c, made.shape[1], stride=step), :] = both[:, c * half : (c + 1) * half]

        stores.append(pltpu.make_async_copy(first_rows(made.at[i], rows), g_kern.at[:, :, pl.ds(i * half, half)], store.at[i]))
        stores[-1].start()

    groups = n // GROUP

    def put(ref, where, value):
        ref[where] = value if groups == 1 else ref[where] + value

    outs = (g_attn, g_in, g_out, g_gain, g_shift)
    if groups > 1:
        for ref in outs:
            ref[...] = jnp.zeros_like(ref)
    token = jnp.zeros_like(g_token)
    for g in range(groups):
        kept = (rows_k, wide_k, prob_k)
        if recompute:
            kept = (rows_s, wide_s, prob_s)
            generator_forward(facts, g, w_attn, w_in, w_out, gain, shift, *kept)
        count = GROUP * SPAN
        d_second = blocks[pl.ds(g * GROUP, GROUP), :SPAN].reshape(count, blocks.shape[2])
        generator_backward(d_second, put, w_attn, w_in, w_out, gain, *kept, d_mlp, outs + (g_token,))
        tails[pl.ds(g * GROUP, GROUP)] = kept[0].at[SECOND][pl.ds(bands, GROUP, stride=SPAN), :]
        token = token + all_rows(d_mlp.at[0][pl.ds(bands, GROUP, stride=SPAN), :])
    g_token[...] = token
    lane = 128
    for i in range(g_patch.shape[1] // lane):
        g_patch[:, i * lane : (i + 1) * lane] = exact(tails[...], blocks[:, SPAN + per_slot + i, :], TN)

    chunks = []
    for ref, r in ((n_gain, 0), (n_gain, 1), (n_shift, 0), (n_shift, 1), (in_bias, 0), (in_bias, 1)):
        chunks += [(ref, r, i) for i in range(ref.shape[1] // lane)]
    for ref in (out_bias, up_bias, down_bias):
        chunks += [(ref, 0, i) for i in range(ref.shape[1] // lane)]
    each = -(-len(chunks) // n)
    for k, (ref, r, i) in enumerate(chunks):
        row = SPAN + k % each
        ref[r : r + 1, i * lane : (i + 1) * lane] = blocks[k // each, row : row + 1]
    for copy in stores:
        copy.wait()


def tail(n, bands, inner, units, blocks, codes, facts, kept, weights, patch_w, local_grad):
    w_attn, w_in, w_out, gain, shift = weights
    width = patch_w.shape[1]
    hyper_width = w_attn.shape[1]
    rows, half = local_grad.shape[3:]
    f32 = jnp.float32
    chunks = (6 * width + 2 * inner + units) // 128
    per_slot = -(-(-(-chunks // n)) // 8) * 8
    recompute = n > GROUP
    kept_shapes, _ = generator_scratch(hyper_width, w_in.shape[1])
    shapes = [
        w_attn.shape, w_in.shape, w_out.shape, gain.shape, shift.shape, (1, hyper_width), patch_w.shape,
        (hyper_width, rows, 2 * half), (2, width), (2, width), (2, inner), (1, width), (1, units), (1, width),
    ]
    return pl.pallas_call(
        partial(tail_kernel, n, bands, per_slot, recompute),
        out_shape=[jax.ShapeDtypeStruct(s, f32) for s in shapes],
        in_specs=[VMEM] * 12 + [ANY],
        out_specs=[VMEM] * 7 + [ANY] + [VMEM] * 6,
        scratch_shapes=[pltpu.VMEM(k if recompute else (8, 128), f32) for k in kept_shapes]
        + [
            pltpu.VMEM((2, GROUP * SPAN, hyper_width), f32),
            pltpu.VMEM((n, hyper_width), f32),
            pltpu.VMEM((hyper_width, n * SPAN), jnp.bfloat16),
            pltpu.VMEM(local_grad.shape, local_grad.dtype),
            pltpu.VMEM((n, SPAN, tiled(rows), half), f32),
            pltpu.VMEM((2, hyper_width, tiled(rows), half), f32),
            pltpu.SemaphoreType.DMA((2,)),
            pltpu.SemaphoreType.DMA((2,)),
        ],
        compiler_params=pltpu.CompilerParams(vmem_limit_bytes=BIG_VMEM),
        name="tail",
    )(blocks, codes, facts, *kept, w_attn, w_in, w_out, gain, shift, patch_w, local_grad)


def fast_einsum(pattern, left_side, right_side):
    return jnp.einsum(pattern, left_side, right_side, preferred_element_type=jnp.float32)


def wave_embedding(wavelengths, model_width):
    half_width = model_width // 2
    frequency = 10000.0 ** (-jnp.arange(half_width, dtype=jnp.float32) * 2.0 / model_width)
    angles = wavelengths.astype(jnp.float32)[..., None] * frequency
    return jnp.concatenate([jnp.sin(angles), jnp.cos(angles)], axis=-1)


def per_device(
    n,
    pixels,
    band_count,
    wavelengths,
    size_class,
    token_keep,
    hyp_attn,
    hyp_mlp_in,
    hyp_mlp_out,
    hyp_gain,
    hyp_shift,
    bias_token,
    kern_weight,
    kern_bias,
    patch_bias_weight,
    norm_gain,
    norm_shift,
    attn_in,
    attn_in_bias,
    attn_out,
    attn_out_bias,
    mlp_in,
    mlp_in_bias,
    mlp_out,
    mlp_out_bias,
    cotangent,
):
    mp = lax.axis_index("mp")
    slot_count, bands, tokens, pix_size = pixels.shape
    assert slot_count == 1 and n % GROUP == 0 and bands + 1 <= SPAN
    hyper_width = hyp_attn.shape[1]
    half = pix_size // 2
    low = jnp.bfloat16
    inner, units = attn_in.shape[2], mlp_in.shape[1]

    band_valid = jnp.arange(SPAN) < band_count[0]
    sequence = jnp.concatenate([wave_embedding(wavelengths[0], hyper_width), bias_token[None]], axis=0)
    sequence = jnp.pad(sequence, ((0, SPAN - bands - 1), (0, 0)))
    usable = (band_valid & (jnp.arange(SPAN) < bands)) | (jnp.arange(SPAN) == bands)
    usable = jnp.broadcast_to(usable.astype(jnp.float32)[:, None], (SPAN, hyper_width))
    facts_own = jnp.concatenate([sequence, usable], axis=0)

    attn_shard = jnp.concatenate([attn_in[0], attn_in[1], attn_in[2], attn_out], axis=1).astype(low)
    mlp_shard = jnp.concatenate([mlp_in, mlp_out], axis=1).astype(low)
    weights = (hyp_attn, hyp_mlp_in, hyp_mlp_out, hyp_gain, hyp_shift)
    kernel, attn_all, mlp_all, facts, patch_rows, codes, *kept = front(
        n, bands, facts_own, *weights, patch_bias_weight, kern_weight, kern_bias, attn_shard, mlp_shard
    )

    live_rows = jnp.where(
        size_class[0] == 0, tokens * 49 // 256, jnp.where(size_class[0] == 1, tokens * 196 // 256, tokens)
    )
    position = jnp.arange(tokens)
    row_valid = position < live_rows
    key_valid = row_valid & ((token_keep[0] == 1) | (position == 0))
    input_bias = jnp.concatenate([attn_in_bias[0], jnp.zeros_like(attn_in_bias[0]), attn_in_bias[1]])
    layer_ins = (
        lax.dynamic_slice_in_dim(pixels[0], mp * half, half, 2),
        kernel,
        attn_all,
        mlp_all,
        cotangent[0],
        jnp.broadcast_to(band_valid.astype(jnp.float32)[:, None], (SPAN, half)),
        key_valid.astype(jnp.float32)[None],
        row_valid.astype(jnp.float32)[:, None],
        patch_rows[bands : bands + 1],
        norm_gain,
        norm_shift,
        input_bias[None],
        attn_out_bias[None],
        mlp_in_bias[None],
        mlp_out_bias[None],
    )
    (
        layer_out,
        grad_q,
        grad_k,
        grad_v,
        grad_attn_out,
        grad_mlp_in,
        grad_mlp_out,
        pixel_grad,
        local_grad,
        blocks,
        grad_kern_bias,
    ) = layer_and_back(n, inner, kern_weight, patch_bias_weight, layer_ins)
    (
        g_attn,
        g_in,
        g_out,
        g_gain,
        g_shift,
        g_token,
        g_patch,
        grad_kern_weight,
        grad_norm_gain,
        grad_norm_shift,
        grad_in_bias,
        grad_attn_out_bias,
        grad_mlp_in_bias,
        grad_mlp_out_bias,
    ) = tail(n, bands, inner, units, blocks, codes, facts, kept, weights, patch_bias_weight, local_grad)
    return (
        layer_out[None],
        pixel_grad[None],
        g_attn,
        g_in,
        g_out,
        g_gain,
        g_shift,
        g_token[0],
        grad_kern_weight,
        grad_kern_bias,
        g_patch,
        grad_norm_gain,
        grad_norm_shift,
        jnp.stack([grad_q, grad_k, grad_v]),
        grad_in_bias,
        grad_attn_out,
        grad_attn_out_bias[0],
        grad_mlp_in,
        grad_mlp_in_bias[0],
        grad_mlp_out,
        grad_mlp_out_bias[0],
    )


def solution(mesh):
    return jax.shard_map(
        partial(per_device, mesh.shape["dp"]),
        mesh=mesh,
        in_specs=(
            P("dp", None, None, None),
            P("dp"),
            P("dp", None),
            P("dp"),
            P("dp", None),
            P(),
            P(),
            P(),
            P(),
            P(),
            P(),
            P(None, "dp", None),
            P("dp", None),
            P(),
            P(),
            P(),
            P(None, "dp", "mp"),
            P(None, "mp"),
            P("dp", "mp"),
            P(),
            P("dp", "mp"),
            P("mp"),
            P("dp", "mp"),
            P(),
            P("dp", None, None),
        ),
        out_specs=(
            P("dp", None, None),
            P("dp", None, None, None),
            P(),
            P(),
            P(),
            P(),
            P(),
            P(),
            P(None, "dp", None),
            P("dp", None),
            P(),
            P(),
            P(),
            P(None, "dp", "mp"),
            P(None, "mp"),
            P("dp", "mp"),
            P(),
            P("dp", "mp"),
            P("mp"),
            P("dp", "mp"),
            P(),
        ),
        check_vma=False,
    )
```

```python
from functools import partial
import math

import jax
import jax.numpy as jnp
import numpy as np
from jax import lax
from jax.experimental import pallas as pl
from jax.experimental.pallas import tpu as pltpu
from jax.sharding import PartitionSpec as P

HEAD_DIM = 64
HYP_HEADS = 4
MESH = pl.DeviceIdType.MESH
ANY = pl.BlockSpec(memory_space=pl.ANY)
VMEM = pl.BlockSpec(memory_space=pltpu.VMEM)
BIG_VMEM = 61 * 1024 * 1024

vit_epsilon = 1e-06
hyper_epsilon = 1e-05


def factors_of(n):
    return {16: (2, 2, 2, 2), 128: (2, 2, 8, 4)}.get(n, (n,))


def coords(me, grid):
    out = []
    for size in reversed(grid):
        out.append(lax.rem(me, size))
        me = me // size
    return out[::-1]


def device_at(position, grid, offset):
    index = 0
    for place, size, step in zip(position, grid, offset):
        index = index * size + (lax.rem(place + step, size) if step else place)
    return index


def offsets_in(grid, dims):
    out = [()]
    for dim, size in enumerate(grid):
        out = [o + (i,) for o in out for i in range(size if dim in dims else 1)]
    return out


def along(grid, dim, step):
    return tuple(step if d == dim else 0 for d in range(len(grid)))


def minus(a, b, grid):
    return tuple((i - j) % size for i, j, size in zip(a, b, grid))


def orders_of(grid):
    dims = tuple(range(len(grid)))
    return [dims, dims[:-2] + (dims[-1], dims[-2])] if len(grid) > 2 else [dims]


def greet(n, me, mp, both):
    sem = pltpu.get_barrier_semaphore()
    for k in range(1, n):
        pl.semaphore_signal(sem, inc=1, device_id=(lax.rem(me + k, n), mp), device_id_type=MESH)
    if both:
        for k in range(n):
            pl.semaphore_signal(sem, inc=1, device_id=(lax.rem(me + k, n), 1 - mp), device_id_type=MESH)
    pl.semaphore_wait(sem, 2 * n - 1 if both else n - 1)


def remote(src, dst, send, recv, device):
    copy = pltpu.make_async_remote_copy(
        src_ref=src, dst_ref=dst, send_sem=send, recv_sem=recv, device_id=device, device_id_type=MESH
    )
    copy.start()
    return copy


def params(collective, limit=None):
    return pltpu.CompilerParams(collective_id=collective, has_side_effects=True, vmem_limit_bytes=limit)


NN, NT, TN = ((1,), (0,)), ((1,), (1,)), ((0,), (0,))
GROUP = 16
SPAN = 16


def dot(a, b, contract):
    return lax.dot_general(a, b, (contract, ((), ())), preferred_element_type=jnp.float32)


def exact(a, b, contract=NN):
    return lax.dot_general(
        a, b, (contract, ((), ())), precision=lax.Precision.HIGH, preferred_element_type=jnp.float32
    )


def lanes_at(i, width):
    return pl.ds(pl.multiple_of(i * width, width), width)


def row_mean(x):
    return jnp.mean(x, axis=-1, keepdims=True)


def row_sum(x):
    return jnp.sum(x, axis=-1, keepdims=True)


def all_rows(x):
    return jnp.sum(x, axis=0, keepdims=True)


def column_sums(x):
    return dot(jnp.ones((8, x.shape[0]), x.dtype), x, NN)[:1]


def normal_parts(x):
    return 0.5 + 0.5 * lax.erf(x * math.sqrt(0.5)), jnp.exp(-0.5 * x * x) * (1.0 / math.sqrt(2.0 * math.pi))


def normed(x, epsilon):
    center = x - row_mean(x)
    r = lax.rsqrt(row_mean(center * center) + epsilon)
    return center * r, r


def norm_back(hat, r, d_y, gain_row):
    u = d_y * gain_row
    return r * (u - row_mean(u) - hat * row_mean(u * hat)), all_rows(d_y * hat), all_rows(d_y)


def tiled(rows):
    return -(-rows // 8) * 8


def first_rows(ref, rows):
    return ref if ref.shape[-2] == rows else ref.at[:, pl.ds(0, rows)]


def arrived(block, sem):
    pltpu.make_async_copy(block, block, sem).wait()


class Refs:
    def __init__(self, names, refs):
        for name, ref in zip(names, refs, strict=True):
            setattr(self, name, ref)


SEQ, QUERY, KEY, VALUE, MIXED, HAT_A, FIRST, HAT_B, SECOND, SCALE_A, SCALE_B = range(11)


def head_masks(width):
    lane = lax.broadcasted_iota(jnp.int32, (1, width), 1)
    size = width // HYP_HEADS
    return [((lane >= h * size) & (lane < (h + 1) * size)).astype(jnp.float32) for h in range(HYP_HEADS)]


def wave_rows(waves, count):
    bands = len(waves)
    row = lax.broadcasted_iota(jnp.int32, (SPAN, 128), 0)
    values = jnp.zeros((SPAN, 128), jnp.float32)
    for b, wave in enumerate(waves):
        values = jnp.where(row == b, wave.astype(jnp.float32), values)
    return jnp.where(row < jnp.minimum(count, bands), values, -values).astype(jnp.bfloat16)


def generator_forward(bands, facts, frequency, token, g, w_attn, w_in, w_out, gain, shift, rows, wide, prob):
    count, width = GROUP * SPAN, facts.shape[-1]
    waves = facts[pl.ds(g * GROUP, GROUP)].astype(jnp.float32).reshape(count, width)
    angles = jnp.abs(waves) * frequency[...]
    lane = lax.broadcasted_iota(jnp.int32, (count, width), 1)
    row = lax.rem(lax.broadcasted_iota(jnp.int32, (count, width), 0), SPAN)
    embedding = jnp.where(lane < width // 2, jnp.sin(angles), jnp.cos(angles))
    last = jnp.where(row == bands, token[...].reshape(1, width), 0.0)
    seq = jnp.where(row < bands, embedding, last)
    valid = ((waves > 0.0) | (row == bands)).astype(jnp.float32)
    columns = dot(jnp.ones((8, width), jnp.bfloat16), valid.astype(jnp.bfloat16), NT)[:1]
    slot = [lax.shift_right_logical(lax.broadcasted_iota(jnp.int32, (count, count), d), 4) for d in range(2)]
    allowed = (slot[0] == slot[1]) & (columns > 0.5)
    rows[SEQ] = seq
    for i in range(3):
        rows[QUERY + i] = exact(seq, w_attn[i])
    scale = 1.0 / math.sqrt(width // HYP_HEADS)
    mixed = jnp.zeros((count, width), jnp.float32)
    for h, mask in enumerate(head_masks(width)):
        scores = jnp.where(allowed, exact(rows[QUERY] * mask, rows[KEY], NT) * scale, -1e30)
        raised = jnp.exp(scores - jnp.max(scores, axis=-1, keepdims=True))
        weights = raised / row_sum(raised)
        prob[h] = weights
        mixed = mixed + exact(weights, rows[VALUE] * mask)
    rows[MIXED] = mixed
    hat, r = normed(seq + exact(mixed, w_attn[3]), hyper_epsilon)
    rows[HAT_A] = hat
    rows[SCALE_A] = jnp.broadcast_to(r, (count, width))
    rows[FIRST] = hat * gain[0:1] + shift[0:1]
    tile = 512

    @pl.loop(0, w_in.shape[1] // tile)
    def _(j):
        cols = lanes_at(j, tile)
        pre = exact(rows[FIRST], w_in[:, cols])
        phi, density = normal_parts(pre)
        wide[0, :, cols] = pre * phi
        wide[1, :, cols] = phi + pre * density

    rows[SECOND] = rows[FIRST]

    @pl.loop(0, w_in.shape[1] // tile)
    def _(j):
        cols = lanes_at(j, tile)
        rows[SECOND] = rows[SECOND] + exact(wide[0, :, cols], w_out[cols])

    hat, r = normed(rows[SECOND], hyper_epsilon)
    rows[HAT_B] = hat
    rows[SCALE_B] = jnp.broadcast_to(r, (count, width))
    rows[SECOND] = hat * gain[1:2] + shift[1:2]


def generator_backward(d_second, put, w_attn, w_in, w_out, gain, rows, wide, prob, d_mlp, outs):
    g_attn, g_in, g_out, g_gain, g_shift = outs
    width = d_second.shape[1]
    d_sum, gain_b, shift_b = norm_back(rows[HAT_B], rows[SCALE_B], d_second, gain[1:2])
    put(g_gain, slice(1, 2), gain_b)
    put(g_shift, slice(1, 2), shift_b)
    d_mlp[0] = d_sum
    d_mlp[1] = d_sum
    tile = 512

    @pl.loop(0, w_in.shape[1] // tile)
    def _(j):
        cols = lanes_at(j, tile)
        put(g_out, cols, exact(wide[0, :, cols], d_mlp[0], TN))
        d_pre = exact(d_mlp[0], w_out[cols], NT) * wide[1, :, cols]
        put(g_in, (slice(None), cols), exact(rows[FIRST], d_pre, TN))
        d_mlp[1] = d_mlp[1] + exact(d_pre, w_in[:, cols], NT)

    d_res, gain_a, shift_a = norm_back(rows[HAT_A], rows[SCALE_A], d_mlp[1], gain[0:1])
    put(g_gain, slice(0, 1), gain_a)
    put(g_shift, slice(0, 1), shift_a)
    put(g_attn, 3, exact(rows[MIXED], d_res, TN))
    d_mixed = exact(d_res, w_attn[3], NT)
    scale = 1.0 / math.sqrt(width // HYP_HEADS)
    d_q = jnp.zeros_like(d_res)
    d_k, d_v = d_q, d_q
    for h, mask in enumerate(head_masks(width)):
        p, d_m = prob[h], d_mixed * mask
        d_p = exact(d_m, rows[VALUE], NT)
        d_s = p * (d_p - row_sum(p * d_p)) * scale
        d_q = d_q + exact(d_s, rows[KEY] * mask)
        d_k = d_k + exact(d_s, rows[QUERY] * mask, TN)
        d_v = d_v + exact(p, d_m, TN)
    d_seq = d_res
    for i, grad in enumerate((d_q, d_k, d_v)):
        put(g_attn, i, exact(rows[SEQ], grad, TN))
        d_seq = d_seq + exact(grad, w_attn[i], NT)
    d_mlp[0] = d_seq


def generator_scratch(width, units):
    f32, count = jnp.float32, GROUP * SPAN
    return [(11, count, width), (2, count, units), (HYP_HEADS, count, count)], f32


def shard_of(ref, owner, rows, cols):
    if len(ref.shape) == 2:
        return ref.at[pl.ds(pl.multiple_of(rows * owner, 16), rows), cols]
    return ref.at[owner, :, cols]


class Gather:
    def __init__(self, grid, rows, arrays, send, recv):
        self.me, self.mp = lax.axis_index("dp"), lax.axis_index("mp")
        self.grid, self.rows, self.here = grid, rows, coords(self.me, grid)
        self.send_sem, self.recv_sem, self.sends = send, recv, {}
        self.pieces = []
        orders = orders_of(grid)
        for array in arrays:
            width = array.shape[-1] // len(orders)
            for i, order in enumerate(orders):
                self.sends[len(self.pieces)] = []
                self.pieces.append((array, pl.ds(i * width, width), order, len(self.pieces)))

    def pass_on(self, piece, owner, number):
        array, cols, order, p = piece
        block = shard_of(array, owner, self.rows, cols)
        for dim in order[number:]:
            for k in range(1, self.grid[dim]):
                there = device_at(self.here, self.grid, along(self.grid, dim, k))
                sem = self.send_sem.at[p, len(self.sends[p])]
                self.sends[p].append(remote(block, block, sem, self.recv_sem.at[p, owner], (there, self.mp)))

    def begin(self, piece):
        self.pass_on(piece, self.me, 0)

    def step(self, piece, number):
        array, cols, order, p = piece
        for offset in offsets_in(self.grid, order[:number]):
            if offset[order[number - 1]]:
                owner = device_at(self.here, self.grid, offset)
                arrived(shard_of(array, owner, self.rows, cols), self.recv_sem.at[p, owner])
                self.pass_on(piece, owner, number)

    def sent(self, pieces):
        for piece in pieces:
            for copy in self.sends[piece[3]]:
                copy.wait_send()


class Exchange:
    def __init__(self, n, grid, blocks, slot, send, recv, own_sem):
        self.me, self.mp = lax.axis_index("dp"), lax.axis_index("mp")
        self.blocks, self.slot, self.sends = blocks, slot, []
        self.send_sem, self.recv_sem, self.own_sem = send, recv, own_sem
        self.grid, self.here = grid, coords(self.me, grid)
        self.near_first = sorted(offsets_in(grid, range(len(grid)))[1:], key=sum)

    def start(self):
        for i, away in enumerate(reversed(self.near_first)):
            there = device_at(self.here, self.grid, away)
            block = self.blocks.at[there]
            self.sends.append(
                remote(block, self.slot(self.me), self.send_sem.at[i], self.recv_sem.at[self.me], (there, self.mp))
            )
        self.own = pltpu.make_async_copy(self.blocks.at[self.me], self.slot(self.me), self.own_sem)
        self.own.start()

    def sources(self):
        for away in self.near_first:
            yield device_at(self.here, self.grid, away)

    def arrive(self, source):
        arrived(self.slot(source), self.recv_sem.at[source])

    def sent(self):
        for copy in self.sends:
            copy.wait_send()


def exchange_sems(n):
    dma = pltpu.SemaphoreType.DMA
    return [dma((n - 1,)), dma((n,)), dma]


class Front:
    def __init__(self, n, grid, bands, facts, frequency, token, w_half, b_half, k32, k16):
        self.n, self.grid, self.bands, self.facts = n, grid, bands, facts
        self.frequency, self.token = frequency, token
        self.w_half, self.b_half, self.k32, self.k16 = w_half, b_half, k32, k16
        self.me, self.mp = lax.axis_index("dp"), lax.axis_index("mp")
        self.shares = []

    def share(self, facts_own, send, recv):
        for k in range(1, self.n):
            there = (lax.rem(self.me + k, self.n), self.mp)
            self.shares.append(remote(facts_own, self.facts.at[self.me], send.at[k - 1], recv.at[k - 1], there))
        self.facts[self.me] = facts_own[...]

    def generate(self, weights, patch_w, second, codes, patch, kept):
        for copy in self.shares:
            copy.wait_recv()
        count = GROUP * SPAN
        position = lax.broadcasted_iota(jnp.int32, (count, self.facts.shape[-1]), 0)
        is_band = lax.rem(position, SPAN) < self.bands
        for g in range(self.n // GROUP):
            generator_forward(self.bands, self.facts, self.frequency, self.token, g, *weights, *kept)
            group = pl.ds(g * count, count)
            second[group] = kept[0][SECOND]
            codes[group] = jnp.where(is_band, kept[0][SECOND] + kept[0][SEQ], 0.0).astype(codes.dtype)
        own = second[pl.ds(pl.multiple_of(self.me * SPAN, SPAN), SPAN)]
        patch[...] = exact(own, patch_w[...])[self.bands : self.bands + 1]

    def make(self, codes, rows):
        n, half, low = self.n, self.w_half.shape[2], jnp.bfloat16
        step = tiled(rows)
        w_rows = self.w_half.reshape(self.w_half.shape[0] * step, half)
        k_rows = self.k32.reshape(n * SPAN * step, half)

        @pl.loop(0, rows // 2)
        def _(j):
            both = [w_rows[pl.ds(2 * j + i, self.w_half.shape[0], stride=step), :].astype(low) for i in range(2)]
            made = dot(codes[...], jnp.concatenate(both, axis=1), NN)
            for i in range(2):
                c = 2 * j + i
                bias = self.b_half[pl.ds(c, 1)]
                k_rows[pl.ds(c, n * SPAN, stride=step), :] = made[:, i * half : (i + 1) * half] + bias

    def ready(self, rows):
        @pl.loop(0, self.n)
        def _(t):
            self.k16[t] = self.k32[t, : self.bands, :rows].astype(self.k16.dtype)

    def sent(self):
        for copy in self.shares:
            copy.wait_send()


def front_kernel(
    n, grid, bands,
    facts_own, frequency, token, w_attn, w_in, w_out, gain, shift, patch_w, kern_w, kern_b, attn, mlp,
    kern_o, attn_o, mlp_o, facts, patch_o, codes_o, rows_o, wide_o, prob_o,
    second, w_half, b_half, k32, k16, local, f_send, f_recv, g_send, g_recv, *a_sems,
):
    me, mp = lax.axis_index("dp"), lax.axis_index("mp")
    rows, half = kern_w.shape[1], kern_w.shape[2] // 2
    load = weight_load(kern_w, w_half, local.at[0], mp)
    own = [
        pltpu.make_async_copy(attn, attn_o.at[me], local.at[1]),
        pltpu.make_async_copy(mlp, mlp_o.at[me], local.at[2]),
    ]
    for copy in own:
        copy.start()
    greet(n, me, mp, False)
    for copy in own:
        copy.wait()
    work = Front(n, grid, bands, facts, frequency, token, w_half, b_half, k32, k16)
    work.share(facts_own, f_send, f_recv)
    gather = Gather(grid, rows, (attn_o, mlp_o), g_send, g_recv)
    for piece in gather.pieces:
        gather.begin(piece)
    work.generate((w_attn, w_in, w_out, gain, shift), patch_w, second, codes_o, patch_o, (rows_o, wide_o, prob_o))
    load.wait()
    b_half[...] = kern_b[:, lanes_at(mp, half)]
    work.make(codes_o, rows)
    work.ready(rows)
    exchange = Exchange(n, grid, k16, lambda source: kern_o.at[source], *a_sems)
    exchange.start()
    for number in range(1, len(grid) + 1):
        for piece in gather.pieces:
            gather.step(piece, number)
    gather.sent(gather.pieces)
    for source in exchange.sources():
        exchange.arrive(source)
    exchange.own.wait()
    exchange.sent()
    work.sent()


def front(n, bands, facts_own, frequency, token, w_attn, w_in, w_out, gain, shift, patch_w, kern_w, kern_b, attn, mlp):
    grid = factors_of(n)
    hyper_width, rows, pixels = kern_w.shape
    half = pixels // 2
    pieces = 2 * len(orders_of(grid))
    f32, low = jnp.float32, jnp.bfloat16
    kept, _ = generator_scratch(hyper_width, w_in.shape[1])
    shapes = [
        ((n, bands, rows, half), low),
        ((n,) + attn.shape, low),
        ((n,) + mlp.shape, low),
        ((n,) + facts_own.shape, low),
        ((1, patch_w.shape[1]), f32),
        ((n * SPAN, hyper_width), low),
    ] + [(k, f32) for k in kept]
    out = pl.pallas_call(
        partial(front_kernel, n, grid, bands),
        out_shape=[jax.ShapeDtypeStruct(*s) for s in shapes],
        in_specs=[VMEM] * 9 + [ANY, VMEM, ANY, ANY],
        out_specs=[ANY] * 3 + [VMEM] * 6,
        scratch_shapes=[
            pltpu.VMEM((n * SPAN, hyper_width), f32),
            pltpu.VMEM((hyper_width, tiled(rows), half), f32),
            pltpu.VMEM((rows, half), f32),
            pltpu.VMEM((n, SPAN, tiled(rows), half), f32),
            pltpu.VMEM((n, bands, rows, half), low),
            pltpu.SemaphoreType.DMA((3,)),
            pltpu.SemaphoreType.DMA((n - 1,)),
            pltpu.SemaphoreType.DMA((n - 1,)),
            pltpu.SemaphoreType.DMA((pieces, n - 1)),
            pltpu.SemaphoreType.DMA((pieces, n)),
        ]
        + exchange_sems(n),
        compiler_params=params(1, BIG_VMEM),
        name="front",
    )(facts_own, frequency, token, w_attn, w_in, w_out, gain, shift, patch_w, kern_w, kern_b, attn, mlp)
    kernel = out[0].transpose(1, 0, 2, 3).reshape(bands, rows * n, half)
    return [kernel, out[1].reshape(n * rows, -1), out[2].reshape(n * rows, -1)] + list(out[3:])


def layer_body(
    inner, hook,
    pix, kern, attn, mlp, cot, band_mask, key_mask, row_scale, patch_bias, gains, shifts, in_bias, out_bias, up_bias, down_bias,
    out_o, emb_grad_o, attn_grad, mlp_grad, small_o, small_up_o, small_in_o,
    emb, mid, part, inbox, norm_a, norm_b, qkv, prob, ctx, act, slope, d_out, d_pre, d_mid, d_att, d_ctx, d_qkv, turned, send, recv,
):
    me, mp = lax.axis_index("dp"), lax.axis_index("mp")
    partner = (me, 1 - mp)
    low = jnp.bfloat16
    bands, tokens, _ = pix.shape
    width = emb.shape[1]
    units = act.shape[1]
    halves = 2
    span = tokens // halves
    tile = 256
    copies = {}

    def swap(i, compute):
        for h in range(halves):
            r = pl.ds(h * span, span)
            if i >= 3:
                copies[i - 3, h].wait_send()

            @pl.loop(0, width // tile)
            def _(j):
                part[i % 3, r, lanes_at(j, tile)] = compute(r, j)

            copies[i, h] = remote(part.at[i % 3, r], inbox.at[i % 3, r], send.at[i, h], recv.at[i, h], partner)

    def swapped(i, h):
        copies[i, h].wait_recv()
        r = pl.ds(h * span, span)
        return part[i % 3, r] + inbox[i % 3, r]

    def embed_terms(r, j):
        total = jnp.zeros((span, tile), jnp.float32)
        for b in range(0, bands, 2):
            both = range(b, min(b + 2, bands))
            left = jnp.concatenate([pix[i, r] * band_mask[i : i + 1].astype(low) for i in both], axis=1)
            right = jnp.concatenate([kern[i, lanes_at(j, tile)] for i in both], axis=1)
            total = total + dot(left, right, NT)
        return total

    hook("start")
    swap(0, embed_terms)
    hook("embedded")
    d_out[...] = (cot[...].astype(jnp.float32) * row_scale[...]).astype(low)
    turned[0] = d_out[...].T
    for h in range(halves):
        r = pl.ds(h * span, span)
        emb[r] = swapped(0, h) + patch_bias[...]
        hat, _ = normed(emb[r], vit_epsilon)
        norm_a[r] = (hat * gains[0:1] + shifts[0:1]).astype(low)

    @pl.loop(0, 3 * inner // 384)
    def _(j):
        cols = lanes_at(j, 384)
        qkv[:, cols] = (dot(norm_a[...], attn[:, cols], NN) + in_bias[:, cols]).astype(low)

    hook("projected")
    wide = 2 * HEAD_DIM
    lane = lax.broadcasted_iota(jnp.int32, (1, wide), 1)
    in_head = [(lane < HEAD_DIM).astype(low), (lane >= HEAD_DIM).astype(low)]
    scale = 1.0 / math.sqrt(HEAD_DIM)
    pairs = inner // wide

    def head_lanes(j, which):
        return pl.ds(pl.multiple_of(which * inner + j * wide, wide), wide)

    @pl.loop(0, pairs)
    def _(j):
        q, k, v = (qkv[:, head_lanes(j, w)] for w in range(3))
        total = jnp.zeros((tokens, wide), jnp.float32)
        for h in range(2):
            scores = jnp.where(key_mask[...] > 0.0, dot(q * in_head[h], k, NT) * scale, -1e30)
            raised = jnp.exp(scores - jnp.max(scores, axis=-1, keepdims=True))
            p = raised / row_sum(raised)
            prob[2 * j + h] = p
            total = total + dot(p.astype(low), v * in_head[h], NN)
        ctx[:, lanes_at(j, wide)] = total.astype(low)

    def out_terms(r, j):
        return dot(ctx[r], attn[lanes_at(j, tile), pl.ds(3 * inner, inner)], NT)

    swap(1, out_terms)
    hook("attended")
    turned[1] = norm_a[...].T
    for h in range(halves):
        r = pl.ds(h * span, span)
        mid[r] = emb[r] + swapped(1, h) + out_bias[...]
        hat, _ = normed(mid[r], vit_epsilon)
        norm_b[r] = (hat * gains[1:2] + shifts[1:2]).astype(low)

    @pl.loop(0, units // tile)
    def _(j):
        cols = lanes_at(j, tile)
        pre = dot(norm_b[...], mlp[:, cols], NN) + up_bias[:, cols]
        phi, density = normal_parts(pre)
        act[:, cols] = (pre * phi).astype(low)
        slope[:, cols] = phi + pre * density

    def down_terms(r, j):
        return dot(act[r], mlp[lanes_at(j, tile), pl.ds(units, units)], NT)

    @pl.loop(0, units // tile)
    def _(j):
        cols = lanes_at(j, tile)
        d_act = dot(d_out[...], mlp[:, pl.ds(pl.multiple_of(units + j * tile, tile), tile)], NN).astype(low)
        d_pre[:, cols] = (d_act.astype(jnp.float32) * slope[:, cols]).astype(low)

    def up_terms(r, j):
        return dot(d_pre[r], mlp[lanes_at(j, tile), pl.ds(0, units)], NT)

    def weight_grad(turned_ref, x, out, start):
        @pl.loop(0, width // tile)
        def _(i):
            for j in range(x.shape[1] // 384):
                out[lanes_at(i, tile), pl.ds(start + j * 384, 384)] = dot(
                    turned_ref[lanes_at(i, tile)], x[:, j * 384 : (j + 1) * 384], NN
                ).astype(low)

    swap(2, up_terms)
    swap(3, down_terms)
    turned[2] = norm_b[...].T
    hook("before feed")
    weight_grad(turned.at[2], d_pre, mlp_grad, 0)
    weight_grad(turned.at[0], act, mlp_grad, units)
    hook("fed")
    small_up_o[...] = column_sums(d_pre[...])
    small_o[5:6] = column_sums(d_out[...])

    def back_through(x, i, h, which):
        hat, r = normed(x, vit_epsilon)
        return norm_back(hat, r, swapped(i, h), gains[which : which + 1])

    sums = []
    for h in range(halves):
        r = pl.ds(h * span, span)
        d_x, gain, shift = back_through(mid[r], 2, h, 1)
        d_x = d_x + d_out[r].astype(jnp.float32)
        d_mid[r] = d_x
        d_att[r] = d_x.astype(low)
        sums.append((gain, shift))
    small_o[1:2] = sums[0][0] + sums[1][0]
    small_o[3:4] = sums[0][1] + sums[1][1]
    small_o[4:5] = column_sums(d_att[...])

    @pl.loop(0, inner // 384)
    def _(j):
        d_ctx[:, lanes_at(j, 384)] = dot(
            d_att[...], attn[:, pl.ds(pl.multiple_of(3 * inner + j * 384, 384), 384)], NN
        ).astype(low)

    @pl.loop(0, pairs)
    def _(j):
        q, k, v = (qkv[:, head_lanes(j, w)] for w in range(3))
        d_c = d_ctx[:, lanes_at(j, wide)]
        d_q = jnp.zeros((tokens, wide), jnp.float32)
        d_k, d_v = d_q, d_q
        for h in range(2):
            p = prob[2 * j + h]
            d_p = dot(d_c * in_head[h], v, NT)
            d_s = (p * (d_p - row_sum(p * d_p))).astype(low)
            d_q = d_q + dot(d_s, k * in_head[h], NN)
            d_k = d_k + dot(d_s, q * in_head[h], TN)
            d_v = d_v + dot(p.astype(low), d_c * in_head[h], TN)
        d_qkv[:, head_lanes(j, 0)] = (d_q * scale).astype(low)
        d_qkv[:, head_lanes(j, 1)] = (d_k * scale).astype(low)
        d_qkv[:, head_lanes(j, 2)] = d_v.astype(low)

    def in_terms(r, j):
        return dot(d_qkv[r], attn[lanes_at(j, tile), pl.ds(0, 3 * inner)], NT)

    swap(4, in_terms)
    hook("before attention")
    weight_grad(turned.at[1], d_qkv, attn_grad, 0)
    turned[2] = d_att[...].T
    weight_grad(turned.at[2], ctx, attn_grad, 3 * inner)
    hook("attention")
    sums = []
    for h in range(halves):
        r = pl.ds(h * span, span)
        d_x, gain, shift = back_through(emb[r], 4, h, 0)
        emb_grad_o[r] = (d_x + d_mid[r]).astype(low)
        sums.append((gain, shift))
    small_o[0:1] = sums[0][0] + sums[1][0]
    small_o[2:3] = sums[0][1] + sums[1][1]
    small_o[6:7] = column_sums(emb_grad_o[...])
    small_o[7:8] = jnp.zeros((1, width), jnp.float32)
    small_in_o[...] = column_sums(d_qkv[...])

    def finish():
        for h in range(halves):
            r = pl.ds(h * span, span)
            out_o[r] = ((mid[r] + swapped(3, h) + down_bias[...]) * row_scale[r]).astype(low)
        for i in range(2, 5):
            for h in range(halves):
                copies[i, h].wait_send()

    return finish


def layer_buffers(inner, units, tokens, width):
    f32, low = jnp.float32, jnp.bfloat16
    return [
        pltpu.VMEM((tokens, width), f32),
        pltpu.VMEM((tokens, width), f32),
        pltpu.VMEM((3, tokens, width), f32),
        pltpu.VMEM((3, tokens, width), f32),
        pltpu.VMEM((tokens, width), low),
        pltpu.VMEM((tokens, width), low),
        pltpu.VMEM((tokens, 3 * inner), low),
        pltpu.VMEM((inner // HEAD_DIM, tokens, tokens), f32),
        pltpu.VMEM((tokens, inner), low),
        pltpu.VMEM((tokens, units), low),
        pltpu.VMEM((tokens, units), f32),
        pltpu.VMEM((tokens, width), low),
        pltpu.VMEM((tokens, units), low),
        pltpu.VMEM((tokens, width), f32),
        pltpu.VMEM((tokens, width), low),
        pltpu.VMEM((tokens, inner), low),
        pltpu.VMEM((tokens, 3 * inner), low),
        pltpu.VMEM((3, width, tokens), low),
        pltpu.SemaphoreType.DMA((5, 2)),
        pltpu.SemaphoreType.DMA((5, 2)),
    ]


LAYER_INS, LAYER_BUFFERS, TURNED = 15, 20, 17


class Scatter:
    def __init__(self, n, grid, rows, attn, mlp, attn_box, mlp_box, outs, send, recv):
        self.me, self.mp = lax.axis_index("dp"), lax.axis_index("mp")
        self.here, self.grid, self.rows = coords(self.me, grid), grid, rows
        self.orders = [order[::-1] for order in orders_of(grid)]
        self.stages = len(grid)
        self.send_sem, self.recv_sem, self.sends = send, recv, []
        self.pieces = []
        for terms, box, out in ((attn, attn_box, outs[:4]), (mlp, mlp_box, outs[4:])):
            width, share = terms.shape[-1] // len(self.orders), len(out) // len(self.orders)
            for i, order in enumerate(self.orders):
                cols, to = pl.ds(i * width, width), out[i * share : (i + 1) * share]
                self.pieces.append((terms, box, to, cols, order, len(self.pieces)))
        self.slots = {}
        for which, order in enumerate(self.orders):
            number = 0
            for t in range(self.stages):
                for shard in self.rest(order, t):
                    for k in range(1, grid[order[t]]):
                        self.slots[which, t, shard, k] = number
                        number += 1

    def rest(self, order, t):
        return sorted(offsets_in(self.grid, order[t + 1 :]), key=sum, reverse=True)

    def start(self, t, pieces):
        for terms, box, _, cols, order, p in pieces:
            for shard in self.rest(order, t):
                for k in range(1, self.grid[order[t]]):
                    step = along(self.grid, order[t], k)
                    owner = device_at(self.here, self.grid, tuple(i + j for i, j in zip(shard, step)))
                    slot = self.slots[p % len(self.orders), t, shard, self.grid[order[t]] - k]
                    there = (device_at(self.here, self.grid, step), self.mp)
                    block = shard_of(terms, owner, self.rows, cols)
                    self.sends.append(
                        remote(block, box.at[slot, :, cols], self.send_sem.at[p, slot], self.recv_sem.at[p, slot], there)
                    )

    def add(self, t, pieces):
        for terms, box, outs, cols, order, p in pieces:
            for shard in self.rest(order, t):
                block = shard_of(terms, device_at(self.here, self.grid, shard), self.rows, cols)
                total = block[...].astype(jnp.float32)
                for k in range(1, self.grid[order[t]]):
                    slot = self.slots[p % len(self.orders), t, shard, k]
                    arrived(box.at[slot, :, cols], self.recv_sem.at[p, slot])
                    total = total + box[slot, :, cols].astype(jnp.float32)
                if t < self.stages - 1:
                    block[...] = total.astype(terms.dtype)
                else:
                    width = total.shape[1] // len(outs)
                    for i, out in enumerate(outs):
                        out[...] = total[:, i * width : (i + 1) * width]

    def go_on(self, t, pieces):
        if t < self.stages:
            self.add(t, pieces)
            if t + 1 < self.stages:
                self.start(t + 1, pieces)


def generator_gradients(n, bands, recompute, blocks, patch_at, w_attn, w_in, w_out, gain, shift, kept, d_mlp, tails, outs):
    g_attn, g_in, g_out, g_gain, g_shift, g_token, g_patch = outs
    groups = n // GROUP

    def put(ref, where, value):
        ref[where] = value if groups == 1 else ref[where] + value

    if groups > 1:
        for ref in (g_attn, g_in, g_out, g_gain, g_shift):
            ref[...] = jnp.zeros_like(ref)
    width = blocks.shape[2]
    token = jnp.zeros((1, width), jnp.float32)
    for g in range(groups):
        recompute(g)
        d_second = blocks[pl.ds(g * GROUP, GROUP), :SPAN].reshape(GROUP * SPAN, width)
        generator_backward(
            d_second, put, w_attn, w_in, w_out, gain, *kept, d_mlp, (g_attn, g_in, g_out, g_gain, g_shift)
        )
        tails[pl.ds(g * GROUP, GROUP)] = kept[0].at[SECOND][pl.ds(bands, GROUP, stride=SPAN), :]
        token = token + all_rows(d_mlp.at[0][pl.ds(bands, GROUP, stride=SPAN), :])
    g_token[...] = token
    lane = 128
    for i in range(g_patch.shape[1] // lane):
        g_patch[:, i * lane : (i + 1) * lane] = exact(tails[...], blocks[:, patch_at + i, :], TN)


def back_body(
    n, grid, scatter, ordered, finish, gradients, exchange,
    pix, kern, band_mask, emb_grad, small, small_up, small_in, patch_w, codes,
    pixel_o, map_o, blocks_o, bias_o,
    w_half, d_pix, got, got32, code, codes_turned, terms, term_box, vectors, vector_box, bias_half, load, local, f_send, f_recv,
    c_send, c_recv, b_send, b_recv, v_send, v_recv, u_send, u_recv,
):
    me, mp = lax.axis_index("dp"), lax.axis_index("mp")
    partner = (me, 1 - mp)
    low = jnp.bfloat16
    bands, tokens, half = pix.shape
    rows = got.shape[2]
    lanes = lanes_at(mp, half)
    own, to_partner = [], []
    mine, rest = ordered

    exchange.start()
    scatter.start(0, rest)
    scatter.go_on(0, mine)
    finish()

    def pixel_gradients(b, count):
        made = dot(emb_grad[...], jnp.concatenate([kern[b + i] for i in range(count)], axis=1), NN)
        for i in range(count):
            d_pix[b + i] = (made[:, i * half : (i + 1) * half] * band_mask[pl.ds(b + i, 1)]).astype(low)

    pl.loop(0, bands // 2)(lambda j: pixel_gradients(2 * j, 2))
    if bands % 2:
        pixel_gradients(bands - 1, 1)

    own.append(pltpu.make_async_copy(d_pix, pixel_o.at[:, :, lanes], local.at[0]))
    own[-1].start()
    to_partner.append(remote(d_pix, pixel_o.at[:, :, lanes], f_send.at[0], f_recv.at[0], partner))

    lane = 128
    per_slot = vectors.shape[1]
    vectors[...] = jnp.zeros_like(vectors)
    chunks = []
    for r in range(4):
        chunks += [small[r : r + 1, i * lane : (i + 1) * lane] for i in range(small.shape[1] // lane)]
    inner = small_in.shape[1] // 3
    for start in (0, 2 * inner):
        chunks += [small_in[:, start + i * lane : start + (i + 1) * lane] for i in range(inner // lane)]
    chunks += [small[4:5, i * lane : (i + 1) * lane] for i in range(small.shape[1] // lane)]
    chunks += [small_up[:, i * lane : (i + 1) * lane] for i in range(small_up.shape[1] // lane)]
    chunks += [small[5:6, i * lane : (i + 1) * lane] for i in range(small.shape[1] // lane)]
    each = -(-len(chunks) // n)
    for i, chunk in enumerate(chunks):
        vectors[i // each, i % each : i % each + 1] = chunk
    patch_grad = small[6:7]
    d_tail = exact(jnp.broadcast_to(patch_grad, (8, patch_grad.shape[1])), patch_w[...], NT)[:1]
    adding = []
    for k in range(1, n):
        there = lax.rem(me + k, n)
        adding.append(remote(vectors.at[there], vector_box.at[n - k], v_send.at[k], v_recv.at[n - k], (there, mp)))
    codes_turned[...] = codes[...].T

    scatter.go_on(0, rest)
    scatter.go_on(1, mine)
    scatter.go_on(1, rest)

    for copy in adding:
        copy.wait_recv()
    total = vectors[me]
    for k in range(1, n):
        total = total + vector_box[k]
    blocks_o[me, SPAN : SPAN + per_slot] = total
    for i in range(patch_grad.shape[1] // lane):
        r = SPAN + per_slot + i
        blocks_o[me, r : r + 1] = patch_grad[:, i * lane : (i + 1) * lane]
    back = []
    beyond = pl.ds(SPAN, blocks_o.shape[1] - SPAN)
    for k in range(1, n):
        there = lax.rem(me + k, n)
        block = blocks_o.at[me, beyond]
        back.append(remote(block, block, u_send.at[k - 1], u_recv.at[k - 1], (there, mp)))

    bias_half[...] = jnp.zeros_like(bias_half)

    def take(source):
        block = got[source].astype(jnp.float32)
        got32[source, :bands, :rows] = block
        got32[source, bands:, :rows] = jnp.zeros((SPAN - bands,) + block.shape[1:], jnp.float32)
        bias_half[...] = bias_half[...] + jnp.sum(block, axis=0)

    exchange.own.wait()
    take(me)
    for source in exchange.sources():
        exchange.arrive(source)
        take(source)

    if load is not None:
        load.wait()
    step = tiled(rows)
    w_rows = w_half.reshape(w_half.shape[0] * step, half)
    g_rows = got32.reshape(n * SPAN * step, half)
    code[...] = jnp.zeros_like(code)

    @pl.loop(0, rows // 2)
    def _(j):
        taken = [g_rows[pl.ds(2 * j + i, n * SPAN, stride=step), :].astype(low) for i in range(2)]
        weights = [w_rows[pl.ds(2 * j + i, w_half.shape[0], stride=step), :].astype(low) for i in range(2)]
        code[...] = code[...] + dot(jnp.concatenate(taken, axis=1), jnp.concatenate(weights, axis=1), NT)

    terms[...] = code[...].reshape(n, SPAN, code.shape[1]).astype(low)
    sums = []
    for k in range(1, n):
        there = lax.rem(me + k, n)
        slot = n - k
        sums.append(remote(terms.at[there], term_box.at[mp, slot], c_send.at[k], c_recv.at[slot], (there, mp)))
    for k in range(n):
        there = lax.rem(me + k, n)
        slot = (n - k) % n
        sums.append(
            remote(terms.at[there], term_box.at[mp, slot], c_send.at[n + k], c_recv.at[n + slot], (there, 1 - mp))
        )
    term_box[mp, 0] = terms[me]
    bias_o[:, lanes] = bias_half[...]
    to_partner.append(remote(bias_half, bias_o.at[:, lanes], f_send.at[2], f_recv.at[2], partner))

    scatter.go_on(2, mine)
    scatter.go_on(2, rest)
    @pl.loop(0, rows // 2)
    def _(j):
        taken = [g_rows[pl.ds(2 * j + c, n * SPAN, stride=step), :].astype(low) for c in range(2)]
        both = dot(codes_turned[...], jnp.concatenate(taken, axis=1), NN)
        for c in range(2):
            w_rows[pl.ds(2 * j + c, w_half.shape[0], stride=step), :] = both[:, c * half : (c + 1) * half]

    filled = first_rows(w_half, rows)
    to_partner.append(remote(filled, map_o.at[mp], f_send.at[1], f_recv.at[1], partner))
    own.append(pltpu.make_async_copy(filled, map_o.at[mp], local.at[1]))
    own[-1].start()

    for copy in sums:
        copy.wait_recv()
    total = term_box[0, 0].astype(jnp.float32)
    for i in range(1, 2 * n):
        total = total + term_box[i // n, i % n].astype(jnp.float32)
    is_tail = lax.broadcasted_iota(jnp.int32, total.shape, 0) == bands
    blocks_o[me, :SPAN] = jnp.where(is_tail, d_tail, total)
    for k in range(1, n):
        there = lax.rem(me + k, n)
        block = blocks_o.at[me, pl.ds(0, SPAN)]
        back.append(remote(block, block, b_send.at[k - 1], b_recv.at[k - 1], (there, mp)))
    for copy in back:
        copy.wait_recv()
    gradients(blocks_o, SPAN + per_slot)
    for t in range(3, scatter.stages):
        scatter.go_on(t, mine + rest)
    for copy in to_partner:
        copy.wait()
    for copy in sums + adding + back + scatter.sends:
        copy.wait_send()
    exchange.sent()
    for copy in own:
        copy.wait()


GENERATOR_OUTS = tuple(dict(
    g_attn=0, g_in=0, g_out=0, g_gain=0, g_shift=0, g_token=0, g_patch=0,
))


def rows_per_slot(n, width, inner, units):
    chunks = (6 * width + 2 * inner + units) // 128
    return -(-(-(-chunks // n)) // 8) * 8


def back_shapes(n, bands, tokens, rows, half, width, inner, units, hyper_width, hyper_units):
    f32, low = jnp.float32, jnp.bfloat16
    per_slot = rows_per_slot(n, width, inner, units)
    block = SPAN + per_slot + width // 128 + -(width // 128) % 8
    part, whole_row = ((rows, inner), f32), ((rows, units), f32)
    outs = dict(
        g_q=part, g_k=part, g_v=part, g_proj=part, g_up=whole_row, g_down=whole_row, pixel_o=((bands, tokens, 2 * half), low),
        map_o=((2, hyper_width, rows, half), f32), blocks_o=((n, block, 128), f32), bias_o=((rows, 2 * half), f32),
    )
    square = (2, hyper_width)
    shapes = [(4, hyper_width, hyper_width), (hyper_width, hyper_units), (hyper_units, hyper_width), square, square]
    shapes += [(1, hyper_width), (hyper_width, width)]
    outs.update({k: (v, f32) for k, v in zip(GENERATOR_OUTS, shapes)})
    specs = [ANY if k in dict(pixel_o=0, map_o=0) else VMEM for k in outs]
    buffers = dict(
        w_half=pltpu.VMEM((hyper_width, tiled(rows), half), f32),
        d_pix=pltpu.VMEM((bands, tokens, half), low),
        got=pltpu.VMEM((n, bands, rows, half), low),
        got32=pltpu.VMEM((n, SPAN, tiled(rows), half), f32),
        code=pltpu.VMEM((n * SPAN, hyper_width), f32),
        codes_turned=pltpu.VMEM((hyper_width, n * SPAN), low),
        terms=pltpu.VMEM((n, SPAN, hyper_width), low),
        term_box=pltpu.VMEM((2, n, SPAN, hyper_width), low),
        vectors=pltpu.VMEM((n, per_slot, 128), f32),
        vector_box=pltpu.VMEM((n, per_slot, 128), f32),
        bias_half=pltpu.VMEM((rows, half), f32),
    )
    sems = dict(
        blocal=(2,), p_send=(3,), p_recv=(3,), c_send=(2 * n,), c_recv=(2 * n,), b_send=(n - 1,),
        b_recv=(n - 1,), v_send=(n,), v_recv=(n,), u_send=(n - 1,), u_recv=(n - 1,),
    )
    buffers.update({k: pltpu.SemaphoreType.DMA(v) for k, v in sems.items()})
    return outs, specs, buffers


BACK = tuple(dict(
    w_half=0, d_pix=0, got=0, got32=0, code=0, codes_turned=0, terms=0, term_box=0, vectors=0, vector_box=0,
    bias_half=0,
))
BACK_SEMS = tuple(dict(
    blocal=0, p_send=0, p_recv=0, c_send=0, c_recv=0, b_send=0, b_recv=0, v_send=0, v_recv=0, u_send=0, u_recv=0,
))


def scatter_buffers(n, grid, rows, attn_lanes, mlp_lanes):
    low, pieces = jnp.bfloat16, 2 * len(orders_of(grid))
    slots = n - 1
    return [
        pltpu.VMEM((slots, rows, attn_lanes), low),
        pltpu.VMEM((slots, rows, mlp_lanes), low),
        pltpu.SemaphoreType.DMA((pieces, slots)),
        pltpu.SemaphoreType.DMA((pieces, slots)),
    ]


def weight_load(kern_w, w_half, sem, mp):
    half = w_half.shape[2]
    copy = pltpu.make_async_copy(kern_w.at[:, :, lanes_at(mp, half)], first_rows(w_half, kern_w.shape[1]), sem)
    copy.start()
    return copy


def whole_kernel(n, grid, names, *refs):
    r = Refs(names, refs)
    me, mp = lax.axis_index("dp"), lax.axis_index("mp")
    low, f32 = jnp.bfloat16, jnp.float32
    bands, tokens, half = r.pix.shape
    rows, inner = r.attn_out.shape
    units = r.mlp_in.shape[1]
    load = weight_load(r.kern_weight, r.w_half, r.local.at[0], mp)
    lanes = lanes_at(mp, half)
    pix_load = pltpu.make_async_copy(r.pixels.at[0, :, :, lanes], r.pix, r.local.at[1])
    pix_load.start()

    mine = pl.ds(pl.multiple_of(me * rows, 16), rows)
    for i in range(3):
        r.attn[mine, i * inner : (i + 1) * inner] = r.attn_in[i].astype(low)
    r.attn[mine, 3 * inner :] = r.attn_out[...].astype(low)
    r.mlp[mine, :units] = r.mlp_in[...].astype(low)
    r.mlp[mine, units:] = r.mlp_out[...].astype(low)
    count = r.band_count[0]
    r.facts_own[...] = wave_rows([r.wavelengths[0, b] for b in range(bands)], count)

    greet(n, me, mp, True)
    work = Front(n, grid, bands, r.facts, r.frequency, r.bias_token, r.w_half, r.b_half, r.k32, r.k16)
    work.share(r.facts_own, r.f_send, r.f_recv)
    gather = Gather(grid, rows, (r.attn, r.mlp), r.w_send, r.w_recv)
    split = len(gather.pieces) // 2
    attn_pieces, mlp_pieces = gather.pieces[:split], gather.pieces[split:]
    for piece in gather.pieces:
        gather.begin(piece)

    r.in_bias[...] = jnp.zeros_like(r.in_bias)
    r.in_bias[:, :inner] = r.attn_in_bias[0:1]
    r.in_bias[:, 2 * inner :] = r.attn_in_bias[1:2]
    r.out_bias[...] = r.attn_out_bias[...].reshape(r.out_bias.shape)
    r.up_bias[...] = r.mlp_in_bias[...].reshape(r.up_bias.shape)
    r.down_bias[...] = r.mlp_out_bias[...].reshape(r.down_bias.shape)
    r.b_half[...] = r.kern_bias[:, lanes]
    size = r.size_class[0]
    live = jnp.where(size == 0, tokens * 49 // 256, jnp.where(size == 1, tokens * 196 // 256, tokens))
    column = lax.broadcasted_iota(jnp.int32, (1, tokens), 1)
    r.key_mask[...] = ((column < live) & ((r.token_keep[...] == 1) | (column == 0))).astype(f32)
    r.row_scale[...] = (lax.broadcasted_iota(jnp.int32, (tokens, 1), 0) < live).astype(f32)
    r.band_mask[...] = (lax.broadcasted_iota(jnp.int32, r.band_mask.shape, 0) < count).astype(f32)

    kept = (r.rows, r.wide, r.prob.at[pl.ds(0, HYP_HEADS)])
    weights = (r.hyp_attn, r.hyp_mlp_in, r.hyp_mlp_out, r.hyp_gain, r.hyp_shift)
    work.generate(weights, r.patch_w, r.second, r.codes, r.patch_bias, kept)
    saves = []
    for i, (src, dst) in enumerate(zip(kept[1:], (r.wide_o, r.prob_o))):
        saves.append(pltpu.make_async_copy(src, dst, r.local.at[2 + i]))
        saves[-1].start()
    for piece in attn_pieces:
        gather.step(piece, 1)
    for piece in mlp_pieces:
        gather.step(piece, 1)
    load.wait()
    work.make(r.codes, rows)
    work.ready(rows)

    def kern_of(source):
        return r.kern.at[:, pl.ds(pl.multiple_of(rows * source, 16), rows)]

    fetch = Exchange(n, grid, r.k16, kern_of, r.k_send, r.k_recv, r.k_own)
    fetch.start()
    for number in range(2, len(grid) + 1):
        for piece in attn_pieces:
            gather.step(piece, number)
    pix_load.wait()
    for copy in saves:
        copy.wait()
    fetch.own.wait()
    for source in fetch.sources():
        fetch.arrive(source)

    scatter = Scatter(
        n, grid, rows, r.attn, r.mlp, r.attn_box, r.mlp_box,
        (r.g_q, r.g_k, r.g_v, r.g_proj, r.g_up, r.g_down), r.g_send, r.g_recv,
    )
    scatter_attn, scatter_mlp = scatter.pieces[:split], scatter.pieces[split:]

    def hook(at):
        if at in ("start", "embedded", "attended"):
            number = ("start", "embedded", "attended").index(at) + 2
            for number in range(number, number + 1 if at != "attended" else len(grid) + 1):
                for piece in mlp_pieces:
                    gather.step(piece, number)
        if at == "before feed":
            gather.sent(mlp_pieces)
        if at == "fed":
            scatter.start(0, scatter_mlp)
        if at == "before attention":
            gather.sent(attn_pieces)

    model = r.emb.shape[1]
    slope, mid, d_mid = r.wide.at[0, :, pl.ds(0, units)], r.wide.at[1, :, pl.ds(0, model)], r.wide.at[1, :, pl.ds(model, model)]
    finish = layer_body(
        inner, hook,
        r.pix, r.kern, r.attn, r.mlp, r.cotangent.at[0], r.band_mask, r.key_mask, r.row_scale, r.patch_bias, r.norm_gain,
        r.norm_shift, r.in_bias, r.out_bias, r.up_bias, r.down_bias,
        r.out_o, r.emb_grad, r.attn, r.mlp, r.small, r.small_up, r.small_in,
        r.emb, mid, r.part, r.inbox, r.norm_a, r.norm_b, r.qkv, r.prob, r.ctx, r.act, slope, r.d_out, r.d_pre, d_mid, r.d_att,
        r.d_ctx, r.d_qkv, r.turned, r.s_send, r.s_recv,
    )
    work.sent()
    fetch.sent()
    r.turned[2] = r.emb_grad[...].T
    tile = 2 * rows * (256 // (2 * rows)) if model % (2 * rows * (256 // (2 * rows))) == 0 else rows

    def kernel_gradients(b, bands_here):
        masked = [r.pix[b + i] * r.band_mask[pl.ds(b + i, 1)].astype(low) for i in range(bands_here)]
        masked = jnp.concatenate(masked, axis=1)
        for i in range(model // tile):
            made = dot(r.turned[2, i * tile : (i + 1) * tile], masked, NN).astype(low)
            for t in range(tile // rows):
                for c in range(bands_here):
                    part = made[t * rows : (t + 1) * rows, c * half : (c + 1) * half]
                    r.k16[i * (tile // rows) + t, b + c] = part

    pl.loop(0, bands // 2)(lambda j: kernel_gradients(2 * j, 2))
    if bands % 2:
        kernel_gradients(bands - 1, 1)

    exchange = Exchange(n, grid, r.k16, lambda source: r.got.at[source], r.a_send, r.a_recv, r.a_own)
    loads = []

    def finish_layer():
        finish()
        for i, (src, dst) in enumerate(zip((r.wide_o, r.prob_o), kept[1:])):
            loads.append(pltpu.make_async_copy(src, dst, r.local.at[2 + i]))
            loads[-1].start()

    def gradients(blocks, patch_at):
        for copy in loads:
            copy.wait()
        outs = [getattr(r, k) for k in GENERATOR_OUTS]
        generator_gradients(n, bands, recompute, blocks, patch_at, *weights, kept, r.d_mlp, r.tails, outs)

    def recompute(g):
        if n > GROUP:
            generator_forward(bands, r.facts, r.frequency, r.bias_token, g, *weights, *kept)

    back_body(
        n, grid, scatter, (scatter_mlp, scatter_attn), finish_layer, gradients, exchange,
        r.pix, r.kern, r.band_mask, r.emb_grad, r.small, r.small_up, r.small_in, r.patch_w, r.codes,
        r.pixel_o, r.map_o, r.blocks_o, r.bias_o,
        r.w_half, r.pix, r.got, r.k32, *[getattr(r, k) for k in BACK[4:]], None, *[getattr(r, k) for k in BACK_SEMS],
    )


def whole(n, **arguments):
    a = Refs(arguments, arguments.values())
    f32, low, dma = jnp.float32, jnp.bfloat16, pltpu.SemaphoreType.DMA
    grid = factors_of(n)
    _, bands, tokens, pixels = a.pixels.shape
    half = pixels // 2
    rows, inner = a.attn_out.shape
    units = a.mlp_in.shape[1]
    width = a.norm_gain.shape[1]
    hyper_width, hyper_units = a.hyp_mlp_in.shape
    outs, specs, buffers = back_shapes(n, bands, tokens, rows, half, width, inner, units, hyper_width, hyper_units)
    kept, _ = generator_scratch(hyper_width, hyper_units)
    outs = dict(out_o=((tokens, width), low)) | outs | dict(wide_o=(kept[1], f32), prob_o=(kept[2], f32))
    specs = [VMEM] + specs + [ANY, ANY]
    pieces = 2 * len(orders_of(grid))
    slots = n - 1
    scratch = dict(
        pix=((bands, tokens, half), low),
        attn=((width, 4 * inner), low),
        mlp=((width, 2 * units), low),
        kern=((bands, width, half), low),
        facts_own=((SPAN, hyper_width), low),
        facts=((n, SPAN, hyper_width), low),
        b_half=((rows, half), f32),
        k32=((n, SPAN, rows, half), f32),
        k16=((n, bands, rows, half), low),
        rows=(kept[0], f32),
        wide=(kept[1], f32),
        prob=((max(HYP_HEADS, inner // HEAD_DIM), tokens, tokens), f32),
        second=((n * SPAN, hyper_width), f32),
        codes=((n * SPAN, hyper_width), low),
        d_mlp=((2, GROUP * SPAN, hyper_width), f32),
        tails=((n, hyper_width), f32),
        patch_bias=((1, width), f32),
        in_bias=((1, 3 * inner), f32),
        out_bias=((1, width), f32),
        up_bias=((1, units), f32),
        down_bias=((1, width), f32),
        key_mask=((1, tokens), f32),
        row_scale=((tokens, 1), f32),
        band_mask=((SPAN, half), f32),
        emb=((tokens, width), f32),
        part=((3, tokens, width), f32),
        inbox=((3, tokens, width), f32),
        norm_a=((tokens, width), low),
        norm_b=((tokens, width), low),
        qkv=((tokens, 3 * inner), low),
        ctx=((tokens, inner), low),
        act=((tokens, units), low),
        d_out=((tokens, width), low),
        d_pre=((tokens, units), low),
        d_att=((tokens, width), low),
        d_ctx=((tokens, inner), low),
        d_qkv=((tokens, 3 * inner), low),
        turned=((3, width, tokens), low),
        emb_grad=((tokens, width), low),
        small=((8, width), f32),
        small_up=((1, units), f32),
        small_in=((1, 3 * inner), f32),
        attn_box=((slots, rows, 4 * inner), low),
        mlp_box=((slots, rows, 2 * units), low),
    )
    scratch = {k: pltpu.VMEM(*v) for k, v in scratch.items()}
    shared = dict(d_pix=0, got32=0)
    scratch.update({k: v for k, v in buffers.items() if k not in shared})
    scratch.update(zip(dict(k_send=0, k_recv=0, k_own=0), exchange_sems(n)))
    scratch.update(zip(dict(a_send=0, a_recv=0, a_own=0), exchange_sems(n)))
    sems = dict(
        local=(4,), f_send=(n - 1,), f_recv=(n - 1,), w_send=(pieces, n - 1), w_recv=(pieces, n),
        s_send=(5, 2), s_recv=(5, 2), g_send=(pieces, slots), g_recv=(pieces, slots),
    )
    names = [*arguments, *outs, *scratch, *sems]
    smem = pl.BlockSpec(memory_space=pltpu.SMEM)
    places = dict(pixels=ANY, kern_weight=ANY, band_count=smem, wavelengths=smem, size_class=smem)
    flops = 2 * tokens * width * (3 * bands * half + 9 * inner * 2 + 9 * units)
    out = pl.pallas_call(
        partial(whole_kernel, n, grid, names),
        out_shape=[jax.ShapeDtypeStruct(*o) for o in outs.values()],
        in_specs=[places.get(k, VMEM) for k in arguments],
        out_specs=specs,
        scratch_shapes=list(scratch.values()) + [dma(v) for v in sems.values()],
        compiler_params=params(6, BIG_VMEM),
        cost_estimate=pl.CostEstimate(flops=flops, bytes_accessed=3 * 10**7, transcendentals=10**6),
        name="whole",
    )(*arguments.values())
    return dict(zip(outs, out))


def layer_kernel(inner, *refs):
    me, mp = lax.axis_index("dp"), lax.axis_index("mp")
    sem = pltpu.get_barrier_semaphore()
    pl.semaphore_signal(sem, inc=1, device_id=(me, 1 - mp), device_id_type=MESH)
    pl.semaphore_wait(sem, 1)
    layer_body(inner, lambda at: None, *refs)()


BACK_INS = tuple(dict(
    pix=0, kern=0, band_mask=0, emb_grad=0, small=0, small_up=0, small_in=0, patch_w=0, codes=0, facts=0,
    frequency=0, token=0, w_attn=0, w_in=0, w_out=0, gain=0, shift=0, attn=0, mlp=0, d_kern=0, kern_w=0,
))


def back_kernel(n, grid, names, *refs):
    r = Refs(names, refs)
    me, mp = lax.axis_index("dp"), lax.axis_index("mp")
    load = weight_load(r.kern_w, r.w_half, r.load_sem.at[0], mp)
    terms = []
    for i, (src, dst) in enumerate(((r.attn, r.attn_acc), (r.mlp, r.mlp_acc))):
        terms.append(pltpu.make_async_copy(src, dst, r.load_sem.at[1 + i]))
        terms[-1].start()
    greet(n, me, mp, True)
    outs = (r.g_q, r.g_k, r.g_v, r.g_proj, r.g_up, r.g_down)
    for copy in terms:
        copy.wait()
    scatter = Scatter(
        n, grid, r.attn.shape[1], r.attn_acc, r.mlp_acc, r.attn_box, r.mlp_box, outs, r.g_send, r.g_recv
    )
    scatter.start(0, scatter.pieces)
    exchange = Exchange(n, grid, r.d_kern, lambda source: r.got.at[source], r.a_send, r.a_recv, r.a_own)
    weights = (r.w_attn, r.w_in, r.w_out, r.gain, r.shift)
    kept = (r.rows, r.wide, r.prob)
    bands = r.pix.shape[0]

    def recompute(g):
        generator_forward(bands, r.facts, r.frequency, r.token, g, *weights, *kept)

    def gradients(blocks, patch_at):
        outs = [getattr(r, k) for k in GENERATOR_OUTS]
        generator_gradients(n, bands, recompute, blocks, patch_at, *weights, kept, r.d_mlp, r.tails, outs)

    back_body(
        n, grid, scatter, (scatter.pieces, []), lambda: None, gradients, exchange,
        r.pix, r.kern, r.band_mask, r.emb_grad, r.small, r.small_up, r.small_in, r.patch_w, r.codes,
        r.pixel_o, r.map_o, r.blocks_o, r.bias_o, *[getattr(r, k) for k in BACK], load, *[getattr(r, k) for k in BACK_SEMS],
    )


def layer_and_back(n, inner, kern_w, patch_w, layer_ins, generator):
    pix, kern, attn, mlp, _, band_mask = layer_ins[:6]
    grid = factors_of(n)
    bands, tokens, half = pix.shape
    width, units = attn.shape[0], mlp.shape[1] // 2
    hyper_width, rows, _ = kern_w.shape
    hyper_units = generator["w_in"].shape[1]
    f32, low = jnp.float32, jnp.bfloat16
    shape, dma = jax.ShapeDtypeStruct, pltpu.SemaphoreType.DMA
    outs, specs, buffers = back_shapes(n, bands, tokens, rows, half, width, inner, units, hyper_width, hyper_units)
    layer_outs = [
        ((tokens, width), low),
        (attn.shape, low),
        (mlp.shape, low),
        ((8, width), f32),
        ((1, units), f32),
        ((1, 3 * inner), f32),
    ]
    layer_out, emb_grad, attn_grad, mlp_grad, small, small_up, small_in = pl.pallas_call(
        partial(layer_kernel, inner),
        out_shape=[shape((tokens, width), low)] + [shape(*o) for o in layer_outs],
        in_specs=[VMEM] * LAYER_INS,
        out_specs=[VMEM] * 7,
        scratch_shapes=layer_buffers(inner, units, tokens, width),
        compiler_params=params(3, BIG_VMEM),
        name="layer",
    )(*layer_ins)
    d_kern = fast_einsum("tc,btp->bcp", emb_grad, pix * band_mask[:bands, None].astype(low)).astype(low)
    d_kern = d_kern.reshape(bands, n, rows, half).transpose(1, 0, 2, 3)
    attn_grad, mlp_grad = attn_grad.reshape(n, rows, -1), mlp_grad.reshape(n, rows, -1)
    ins = dict(
        pix=pix, kern=kern, band_mask=band_mask, emb_grad=emb_grad, small=small, small_up=small_up, small_in=small_in,
        attn=attn_grad, mlp=mlp_grad, patch_w=patch_w, d_kern=d_kern, kern_w=kern_w, **generator,
    )
    kept, _ = generator_scratch(hyper_width, hyper_units)
    scratch = dict(attn_acc=pltpu.VMEM(attn_grad.shape, low), mlp_acc=pltpu.VMEM(mlp_grad.shape, low))
    scratch.update(
        zip(dict(attn_box=0, mlp_box=0, g_send=0, g_recv=0), scatter_buffers(n, grid, rows, attn.shape[1], mlp.shape[1]))
    )
    scratch.update(zip(dict(a_send=0, a_recv=0, a_own=0), exchange_sems(n)))
    scratch.update({k: pltpu.VMEM(v, f32) for k, v in zip(dict(rows=0, wide=0, prob=0), kept)})
    scratch.update(
        d_mlp=pltpu.VMEM((2, GROUP * SPAN, hyper_width), f32), tails=pltpu.VMEM((n, hyper_width), f32), load_sem=dma((3,))
    )
    scratch.update(buffers)
    out = pl.pallas_call(
        partial(back_kernel, n, grid, [*BACK_INS, *outs, *scratch]),
        out_shape=[shape(*o) for o in outs.values()],
        in_specs=[VMEM] * (len(BACK_INS) - 4) + [ANY] * 4,
        out_specs=specs,
        scratch_shapes=list(scratch.values()),
        compiler_params=params(2, BIG_VMEM),
        name="back",
    )(*[ins[k] for k in BACK_INS])
    return dict(out_o=layer_out) | dict(zip(outs, out))


PASSED = tuple(dict(
    out_o=0, pixel_o=0, g_q=0, g_k=0, g_v=0, g_proj=0, g_up=0, g_down=0, bias_o=0, g_in=0, g_out=0, g_attn=0,
    g_patch=0,
))
SMALL = tuple(dict(
    blocks_o=0, g_gain=0, g_shift=0, g_token=0,
))


def tail_kernel(per_slot, names, *refs):
    r = Refs(names, refs)
    loads, stores = [], []
    for i in range(2):
        loads.append(pltpu.make_async_copy(r.map_o.at[i], r.via_map.at[i], r.load.at[i]))
    for i, name in enumerate(PASSED):
        loads.append(pltpu.make_async_copy(getattr(r, name), getattr(r, "via_" + name), r.load.at[2 + i]))
    for copy in loads:
        copy.start()
    r.gain_p[...] = r.g_gain[...]
    r.shift_p[...] = r.g_shift[...]
    r.token_p[...] = r.g_token[...].reshape(r.token_p.shape)
    lane = 128
    chunks = []
    for ref, which in ((r.n_gain, 0), (r.n_gain, 1), (r.n_shift, 0), (r.n_shift, 1), (r.in_bias, 0), (r.in_bias, 1)):
        chunks += [(ref, which, i) for i in range(ref.shape[1] // lane)]
    for ref in (r.out_bias, r.up_bias, r.down_bias):
        chunks += [(ref, None, i) for i in range(ref.shape[0] // lane)]
    each = -(-len(chunks) // r.blocks_o.shape[0])
    for k, (ref, which, i) in enumerate(chunks):
        at = SPAN + k % each
        if which is None:
            ref[pl.ds(i * lane, lane)] = r.blocks_o[k // each, at]
        else:
            ref[which : which + 1, i * lane : (i + 1) * lane] = r.blocks_o[k // each, at : at + 1]
    half = r.map_p.shape[2] // 2
    sources = [r.via_map.at[0], r.via_map.at[1]] + [getattr(r, "via_" + k) for k in PASSED]
    targets = [r.map_p.at[:, :, pl.ds(i * half, half)] for i in range(2)]
    targets += [r.out_p, r.pixel_p, r.in_p.at[0], r.in_p.at[1], r.in_p.at[2], r.proj_p, r.up_p, r.down_p, r.bias_p]
    targets += [r.w_in_p, r.w_out_p, r.w_attn_p, r.patch_p]
    for i, (load, src, dst) in enumerate(zip(loads, sources, targets, strict=True)):
        load.wait()
        stores.append(pltpu.make_async_copy(src, dst, r.store.at[i]))
        stores[-1].start()
    for copy in stores:
        copy.wait()


def tail(made):
    m = Refs(made, made.values())
    f32, low = jnp.float32, jnp.bfloat16
    n = m.blocks_o.shape[0]
    (rows, inner), units = m.g_proj.shape, m.g_up.shape[1]
    hyper_width, width = m.g_patch.shape
    half = m.map_o.shape[3]
    outs = dict(
        gain_p=m.g_gain.shape, shift_p=m.g_shift.shape, token_p=(hyper_width,), n_gain=(2, width),
        n_shift=(2, width), in_bias=(2, inner), out_bias=(width,), up_bias=(units,), down_bias=(width,),
    )
    outs = {k: (v, f32) for k, v in outs.items()}
    direct = dict(
        map_p=((hyper_width, rows, 2 * half), f32), out_p=(m.out_o.shape, low),
        pixel_p=(m.pixel_o.shape, low), in_p=((3, rows, inner), f32), proj_p=((rows, inner), f32),
        up_p=((rows, units), f32), down_p=((rows, units), f32), bias_p=((rows, 2 * half), f32),
        w_in_p=(m.g_in.shape, f32), w_out_p=(m.g_out.shape, f32), w_attn_p=(m.g_attn.shape, f32),
        patch_p=(m.g_patch.shape, f32),
    )
    scratch = {"via_" + k: (made[k].shape, made[k].dtype) for k in PASSED}
    scratch.update(via_map=(m.map_o.shape, f32))
    far = tuple(dict(map_o=0)) + PASSED
    names = [*SMALL, *far, *outs, *direct, *scratch, "load", "store"]
    results = pl.pallas_call(
        partial(tail_kernel, rows_per_slot(n, width, inner, units), names),
        out_shape=[jax.ShapeDtypeStruct(*v) for v in (outs | direct).values()],
        in_specs=[VMEM] * len(SMALL) + [ANY] * len(far),
        out_specs=[VMEM] * len(outs) + [ANY] * len(direct),
        scratch_shapes=[pltpu.VMEM(*v) for v in scratch.values()] + [pltpu.SemaphoreType.DMA((len(far) + 1,))] * 2,
        compiler_params=pltpu.CompilerParams(vmem_limit_bytes=BIG_VMEM),
        name="tail",
    )(*[made[k] for k in SMALL + far])
    return Refs(outs | direct, results)


def fast_einsum(pattern, left_side, right_side):
    return jnp.einsum(pattern, left_side, right_side, preferred_element_type=jnp.float32)


def in_parts(
    n, pixels, band_count, wavelengths, size_class, token_keep, hyp_attn, hyp_mlp_in, hyp_mlp_out, hyp_gain, hyp_shift, bias_token,
    kern_weight, kern_bias, patch_w, norm_gain, norm_shift, attn_in, attn_in_bias, attn_out, attn_out_bias, mlp_in, mlp_in_bias,
    mlp_out, mlp_out_bias, cotangent, frequency,
):
    mp = lax.axis_index("mp")
    _, bands, tokens, pix_size = pixels.shape
    hyper_width = hyp_attn.shape[1]
    half = pix_size // 2
    low = jnp.bfloat16
    inner = attn_in.shape[2]
    band_valid = jnp.arange(SPAN) < band_count[0]
    facts_own = wave_rows([wavelengths[0, b] for b in range(bands)], band_count[0])

    attn_shard = jnp.concatenate([attn_in[0], attn_in[1], attn_in[2], attn_out], axis=1).astype(low)
    mlp_shard = jnp.concatenate([mlp_in, mlp_out], axis=1).astype(low)
    weights = (hyp_attn, hyp_mlp_in, hyp_mlp_out, hyp_gain, hyp_shift)
    kernel, attn_all, mlp_all, facts, patch_bias, codes, *_ = front(
        n, bands, facts_own, frequency, bias_token, *weights, patch_w, kern_weight, kern_bias, attn_shard, mlp_shard
    )
    live_rows = jnp.where(
        size_class[0] == 0, tokens * 49 // 256, jnp.where(size_class[0] == 1, tokens * 196 // 256, tokens)
    )
    position = jnp.arange(tokens)
    row_valid = position < live_rows
    key_valid = row_valid & ((token_keep[0] == 1) | (position == 0))
    input_bias = jnp.concatenate([attn_in_bias[0], jnp.zeros_like(attn_in_bias[0]), attn_in_bias[1]])
    layer_ins = (
        lax.dynamic_slice_in_dim(pixels[0], mp * half, half, 2),
        kernel,
        attn_all,
        mlp_all,
        cotangent[0],
        jnp.broadcast_to(band_valid.astype(jnp.float32)[:, None], (SPAN, half)),
        key_valid.astype(jnp.float32)[None],
        row_valid.astype(jnp.float32)[:, None],
        patch_bias,
        norm_gain,
        norm_shift,
        input_bias[None],
        attn_out_bias[None],
        mlp_in_bias[None],
        mlp_out_bias[None],
    )
    generator = dict(
        codes=codes, facts=facts, frequency=frequency, token=bias_token, w_attn=hyp_attn, w_in=hyp_mlp_in, w_out=hyp_mlp_out,
        gain=hyp_gain, shift=hyp_shift,
    )
    return layer_and_back(n, inner, kern_weight, patch_w, layer_ins, generator)


def per_device(
    n,
    pixels,
    band_count,
    wavelengths,
    size_class,
    token_keep,
    hyp_attn,
    hyp_mlp_in,
    hyp_mlp_out,
    hyp_gain,
    hyp_shift,
    bias_token,
    kern_weight,
    kern_bias,
    patch_bias_weight,
    norm_gain,
    norm_shift,
    attn_in,
    attn_in_bias,
    attn_out,
    attn_out_bias,
    mlp_in,
    mlp_in_bias,
    mlp_out,
    mlp_out_bias,
    cotangent,
):
    slot_count, bands = pixels.shape[:2]
    assert slot_count == 1 and n % GROUP == 0 and bands + 1 <= SPAN
    arguments = dict(
        pixels=pixels, band_count=band_count, wavelengths=wavelengths, size_class=size_class, token_keep=token_keep,
        hyp_attn=hyp_attn, hyp_mlp_in=hyp_mlp_in, hyp_mlp_out=hyp_mlp_out, hyp_gain=hyp_gain, hyp_shift=hyp_shift,
        bias_token=bias_token, kern_weight=kern_weight, kern_bias=kern_bias, patch_w=patch_bias_weight, norm_gain=norm_gain,
        norm_shift=norm_shift, attn_in=attn_in, attn_in_bias=attn_in_bias, attn_out=attn_out, attn_out_bias=attn_out_bias,
        mlp_in=mlp_in, mlp_in_bias=mlp_in_bias, mlp_out=mlp_out, mlp_out_bias=mlp_out_bias, cotangent=cotangent,
    )
    half_width = hyp_attn.shape[1] // 2
    frequency = 10000.0 ** (-np.arange(half_width, dtype=np.float32) * 2.0 / (2 * half_width))
    frequency = jnp.asarray(np.concatenate([frequency, frequency])[None].astype(np.float32))
    make = whole if kern_weight.shape[1] % 16 == 0 else in_parts
    done = tail(make(n, frequency=frequency, **arguments))
    return (
        done.out_p[None],
        done.pixel_p[None],
        done.w_attn_p,
        done.w_in_p,
        done.w_out_p,
        done.gain_p,
        done.shift_p,
        done.token_p,
        done.map_p,
        done.bias_p,
        done.patch_p,
        done.n_gain,
        done.n_shift,
        done.in_p,
        done.in_bias,
        done.proj_p,
        done.out_bias,
        done.up_p,
        done.up_bias,
        done.down_p,
        done.down_bias,
    )


def solution(mesh):
    return jax.shard_map(
        partial(per_device, mesh.shape["dp"]),
        mesh=mesh,
        in_specs=(
            P("dp", None, None, None),
            P("dp"),
            P("dp", None),
            P("dp"),
            P("dp", None),
            P(),
            P(),
            P(),
            P(),
            P(),
            P(),
            P(None, "dp", None),
            P("dp", None),
            P(),
            P(),
            P(),
            P(None, "dp", "mp"),
            P(None, "mp"),
            P("dp", "mp"),
            P(),
            P("dp", "mp"),
            P("mp"),
            P("dp", "mp"),
            P(),
            P("dp", None, None),
        ),
        out_specs=(
            P("dp", None, None),
            P("dp", None, None, None),
            P(),
            P(),
            P(),
            P(),
            P(),
            P(),
            P(None, "dp", None),
            P("dp", None),
            P(),
            P(),
            P(),
            P(None, "dp", "mp"),
            P(None, "mp"),
            P("dp", "mp"),
            P(),
            P("dp", "mp"),
            P("mp"),
            P("dp", "mp"),
            P(),
        ),
        check_vma=False,
    )
```

```python
from functools import partial
import math

import jax
import jax.numpy as jnp
import numpy as np
from jax import lax
from jax.experimental import pallas as pl
from jax.experimental.pallas import tpu as pltpu
from jax.sharding import PartitionSpec as P

HEAD_DIM = 64
HYP_HEADS = 4
MESH = pl.DeviceIdType.MESH
ANY = pl.BlockSpec(memory_space=pl.ANY)
VMEM = pl.BlockSpec(memory_space=pltpu.VMEM)
BIG_VMEM = 61 * 1024 * 1024

vit_epsilon = 1e-06
hyper_epsilon = 1e-05


def factors_of(n):
    return {16: (2, 2, 2, 2), 128: (2, 2, 8, 4)}.get(n, (n,))


def coords(me, grid):
    out = []
    for size in reversed(grid):
        out.append(lax.rem(me, size))
        me = me // size
    return out[::-1]


def device_at(position, grid, offset):
    index = 0
    for place, size, step in zip(position, grid, offset):
        index = index * size + (lax.rem(place + step, size) if step else place)
    return index


def offsets_in(grid, dims):
    out = [()]
    for dim, size in enumerate(grid):
        out = [o + (i,) for o in out for i in range(size if dim in dims else 1)]
    return out


def along(grid, dim, step):
    return tuple(step if d == dim else 0 for d in range(len(grid)))


def minus(a, b, grid):
    return tuple((i - j) % size for i, j, size in zip(a, b, grid))


def orders_of(grid):
    dims = tuple(range(len(grid)))
    if len(grid) != 4:
        return [dims]
    return [(0, 1, 2, 3), (0, 2, 3, 1), (0, 1, 3, 2), (0, 3, 2, 1)]


def parts_of(lanes, grid):
    shares = (5, 1, 5, 1) if len(grid) == 4 else (1,)
    unit = lanes // sum(shares)
    assert unit % 128 == 0
    return [(sum(shares[:i]) * unit, share * unit) for i, share in enumerate(shares)]


def greet(n, me, mp, both):
    sem = pltpu.get_barrier_semaphore()
    for k in range(1, n):
        pl.semaphore_signal(sem, inc=1, device_id=(lax.rem(me + k, n), mp), device_id_type=MESH)
    if both:
        for k in range(n):
            pl.semaphore_signal(sem, inc=1, device_id=(lax.rem(me + k, n), 1 - mp), device_id_type=MESH)
    pl.semaphore_wait(sem, 2 * n - 1 if both else n - 1)


def remote(src, dst, send, recv, device):
    copy = pltpu.make_async_remote_copy(
        src_ref=src, dst_ref=dst, send_sem=send, recv_sem=recv, device_id=device, device_id_type=MESH
    )
    copy.start()
    return copy


def params(collective, limit=None):
    return pltpu.CompilerParams(collective_id=collective, has_side_effects=True, vmem_limit_bytes=limit)


NN, NT, TN = ((1,), (0,)), ((1,), (1,)), ((0,), (0,))
GROUP = 16
SPAN = 16


def dot(a, b, contract):
    return lax.dot_general(a, b, (contract, ((), ())), preferred_element_type=jnp.float32)


def exact(a, b, contract=NN):
    return lax.dot_general(
        a, b, (contract, ((), ())), precision=lax.Precision.HIGH, preferred_element_type=jnp.float32
    )


def lanes_at(i, width):
    return pl.ds(pl.multiple_of(i * width, width), width)


def row_mean(x):
    return jnp.mean(x, axis=-1, keepdims=True)


def row_sum(x):
    return jnp.sum(x, axis=-1, keepdims=True)


def all_rows(x):
    return jnp.sum(x, axis=0, keepdims=True)


def column_sums(x):
    return dot(jnp.ones((8, x.shape[0]), x.dtype), x, NN)[:1]


def normal_parts(x):
    return 0.5 + 0.5 * lax.erf(x * math.sqrt(0.5)), jnp.exp(-0.5 * x * x) * (1.0 / math.sqrt(2.0 * math.pi))


def normed(x, epsilon):
    center = x - row_mean(x)
    r = lax.rsqrt(row_mean(center * center) + epsilon)
    return center * r, r


def norm_back(hat, r, d_y, gain_row):
    u = d_y * gain_row
    return r * (u - row_mean(u) - hat * row_mean(u * hat)), all_rows(d_y * hat), all_rows(d_y)


def tiled(rows):
    return -(-rows // 8) * 8


def first_rows(ref, rows):
    return ref if ref.shape[-2] == rows else ref.at[:, pl.ds(0, rows)]


def arrived(block, sem):
    pltpu.make_async_copy(block, block, sem).wait()


class Refs:
    def __init__(self, names, refs):
        for name, ref in zip(names, refs, strict=True):
            setattr(self, name, ref)


SEQ, QUERY, KEY, VALUE, MIXED, HAT_A, FIRST, HAT_B, SECOND, SCALE_A, SCALE_B = range(11)


def head_masks(width):
    lane = lax.broadcasted_iota(jnp.int32, (1, width), 1)
    size = width // HYP_HEADS
    return [((lane >= h * size) & (lane < (h + 1) * size)).astype(jnp.float32) for h in range(HYP_HEADS)]


def wave_rows(waves, count):
    bands = len(waves)
    row = lax.broadcasted_iota(jnp.int32, (SPAN, 128), 0)
    values = jnp.zeros((SPAN, 128), jnp.float32)
    for b, wave in enumerate(waves):
        values = jnp.where(row == b, wave.astype(jnp.float32), values)
    return jnp.where(row < jnp.minimum(count, bands), values, -values).astype(jnp.bfloat16)


def generator_forward(bands, facts, frequency, token, g, w_attn, w_in, w_out, gain, shift, rows, wide, prob):
    count, width = GROUP * SPAN, facts.shape[-1]
    waves = facts[pl.ds(g * GROUP, GROUP)].astype(jnp.float32).reshape(count, width)
    angles = jnp.abs(waves) * frequency[...]
    lane = lax.broadcasted_iota(jnp.int32, (count, width), 1)
    row = lax.rem(lax.broadcasted_iota(jnp.int32, (count, width), 0), SPAN)
    embedding = jnp.where(lane < width // 2, jnp.sin(angles), jnp.cos(angles))
    last = jnp.where(row == bands, token[...].reshape(1, width), 0.0)
    seq = jnp.where(row < bands, embedding, last)
    valid = ((waves > 0.0) | (row == bands)).astype(jnp.float32)
    columns = dot(jnp.ones((8, width), jnp.bfloat16), valid.astype(jnp.bfloat16), NT)[:1]
    slot = [lax.shift_right_logical(lax.broadcasted_iota(jnp.int32, (count, count), d), 4) for d in range(2)]
    allowed = (slot[0] == slot[1]) & (columns > 0.5)
    rows[SEQ] = seq
    for i in range(3):
        rows[QUERY + i] = exact(seq, w_attn[i])
    scale = 1.0 / math.sqrt(width // HYP_HEADS)
    mixed = jnp.zeros((count, width), jnp.float32)
    for h, mask in enumerate(head_masks(width)):
        scores = jnp.where(allowed, exact(rows[QUERY] * mask, rows[KEY], NT) * scale, -1e30)
        raised = jnp.exp(scores - jnp.max(scores, axis=-1, keepdims=True))
        weights = raised / row_sum(raised)
        prob[h] = weights
        mixed = mixed + exact(weights, rows[VALUE] * mask)
    rows[MIXED] = mixed
    hat, r = normed(seq + exact(mixed, w_attn[3]), hyper_epsilon)
    rows[HAT_A] = hat
    rows[SCALE_A] = jnp.broadcast_to(r, (count, width))
    rows[FIRST] = hat * gain[0:1] + shift[0:1]
    tile = 512

    @pl.loop(0, w_in.shape[1] // tile)
    def _(j):
        cols = lanes_at(j, tile)
        pre = exact(rows[FIRST], w_in[:, cols])
        phi, density = normal_parts(pre)
        wide[0, :, cols] = pre * phi
        wide[1, :, cols] = phi + pre * density

    rows[SECOND] = rows[FIRST]

    @pl.loop(0, w_in.shape[1] // tile)
    def _(j):
        cols = lanes_at(j, tile)
        rows[SECOND] = rows[SECOND] + exact(wide[0, :, cols], w_out[cols])

    hat, r = normed(rows[SECOND], hyper_epsilon)
    rows[HAT_B] = hat
    rows[SCALE_B] = jnp.broadcast_to(r, (count, width))
    rows[SECOND] = hat * gain[1:2] + shift[1:2]


def generator_backward(d_second, put, w_attn, w_in, w_out, gain, rows, wide, prob, d_mlp, outs):
    g_attn, g_in, g_out, g_gain, g_shift = outs
    width = d_second.shape[1]
    d_sum, gain_b, shift_b = norm_back(rows[HAT_B], rows[SCALE_B], d_second, gain[1:2])
    put(g_gain, slice(1, 2), gain_b)
    put(g_shift, slice(1, 2), shift_b)
    d_mlp[0] = d_sum
    d_mlp[1] = d_sum
    tile = 512

    @pl.loop(0, w_in.shape[1] // tile)
    def _(j):
        cols = lanes_at(j, tile)
        put(g_out, cols, exact(wide[0, :, cols], d_mlp[0], TN))
        d_pre = exact(d_mlp[0], w_out[cols], NT) * wide[1, :, cols]
        put(g_in, (slice(None), cols), exact(rows[FIRST], d_pre, TN))
        d_mlp[1] = d_mlp[1] + exact(d_pre, w_in[:, cols], NT)

    d_res, gain_a, shift_a = norm_back(rows[HAT_A], rows[SCALE_A], d_mlp[1], gain[0:1])
    put(g_gain, slice(0, 1), gain_a)
    put(g_shift, slice(0, 1), shift_a)
    put(g_attn, 3, exact(rows[MIXED], d_res, TN))
    d_mixed = exact(d_res, w_attn[3], NT)
    scale = 1.0 / math.sqrt(width // HYP_HEADS)
    d_q = jnp.zeros_like(d_res)
    d_k, d_v = d_q, d_q
    for h, mask in enumerate(head_masks(width)):
        p, d_m = prob[h], d_mixed * mask
        d_p = exact(d_m, rows[VALUE], NT)
        d_s = p * (d_p - row_sum(p * d_p)) * scale
        d_q = d_q + exact(d_s, rows[KEY] * mask)
        d_k = d_k + exact(d_s, rows[QUERY] * mask, TN)
        d_v = d_v + exact(p, d_m, TN)
    d_seq = d_res
    for i, grad in enumerate((d_q, d_k, d_v)):
        put(g_attn, i, exact(rows[SEQ], grad, TN))
        d_seq = d_seq + exact(grad, w_attn[i], NT)
    d_mlp[0] = d_seq


def generator_scratch(width, units):
    f32, count = jnp.float32, GROUP * SPAN
    return [(11, count, width), (2, count, units), (HYP_HEADS, count, count)], f32


def shard_of(ref, owner, rows, cols):
    if len(ref.shape) == 2:
        return ref.at[pl.ds(pl.multiple_of(rows * owner, 16), rows), cols]
    return ref.at[owner, :, cols]


class Gather:
    def __init__(self, grid, rows, arrays, send, recv):
        self.me, self.mp = lax.axis_index("dp"), lax.axis_index("mp")
        self.grid, self.rows, self.here = grid, rows, coords(self.me, grid)
        self.send_sem, self.recv_sem, self.sends = send, recv, {}
        self.pieces = []
        orders = orders_of(grid)
        for array in arrays:
            for (first, width), order in zip(parts_of(array.shape[-1], grid), orders):
                self.sends[len(self.pieces)] = []
                self.pieces.append((array, pl.ds(first, width), order, len(self.pieces)))

    def pass_on(self, piece, owner, number):
        array, cols, order, p = piece
        block = shard_of(array, owner, self.rows, cols)
        for dim in order[number:]:
            for k in range(1, self.grid[dim]):
                there = device_at(self.here, self.grid, along(self.grid, dim, k))
                sem = self.send_sem.at[p, len(self.sends[p])]
                self.sends[p].append(remote(block, block, sem, self.recv_sem.at[p, owner], (there, self.mp)))

    def begin(self, piece):
        self.pass_on(piece, self.me, 0)

    def step(self, piece, number):
        array, cols, order, p = piece
        for offset in offsets_in(self.grid, order[:number]):
            if offset[order[number - 1]]:
                owner = device_at(self.here, self.grid, offset)
                arrived(shard_of(array, owner, self.rows, cols), self.recv_sem.at[p, owner])
                self.pass_on(piece, owner, number)

    def sent(self, pieces):
        for piece in pieces:
            for copy in self.sends[piece[3]]:
                copy.wait_send()


class Exchange:
    def __init__(self, n, grid, blocks, slot, send, recv, own_sem):
        self.me, self.mp = lax.axis_index("dp"), lax.axis_index("mp")
        self.blocks, self.slot, self.sends = blocks, slot, []
        self.send_sem, self.recv_sem, self.own_sem = send, recv, own_sem
        self.grid, self.here = grid, coords(self.me, grid)
        self.near_first = sorted(offsets_in(grid, range(len(grid)))[1:], key=sum)

    def start(self):
        for i, away in enumerate(reversed(self.near_first)):
            there = device_at(self.here, self.grid, away)
            block = self.blocks.at[there]
            self.sends.append(
                remote(block, self.slot(self.me), self.send_sem.at[i], self.recv_sem.at[self.me], (there, self.mp))
            )
        self.own = pltpu.make_async_copy(self.blocks.at[self.me], self.slot(self.me), self.own_sem)
        self.own.start()

    def sources(self):
        for away in self.near_first:
            yield device_at(self.here, self.grid, away)

    def arrive(self, source):
        arrived(self.slot(source), self.recv_sem.at[source])

    def sent(self):
        for copy in self.sends:
            copy.wait_send()


def exchange_sems(n):
    dma = pltpu.SemaphoreType.DMA
    return [dma((n - 1,)), dma((n,)), dma]


class Front:
    def __init__(self, n, grid, bands, facts, frequency, token, w_half, b_half, k32, k16):
        self.n, self.grid, self.bands, self.facts = n, grid, bands, facts
        self.frequency, self.token = frequency, token
        self.w_half, self.b_half, self.k32, self.k16 = w_half, b_half, k32, k16
        self.me, self.mp = lax.axis_index("dp"), lax.axis_index("mp")
        self.shares = []

    def share(self, facts_own, send, recv):
        for k in range(1, self.n):
            there = (lax.rem(self.me + k, self.n), self.mp)
            self.shares.append(remote(facts_own, self.facts.at[self.me], send.at[k - 1], recv.at[k - 1], there))
        self.facts[self.me] = facts_own[...]

    def generate(self, weights, patch_w, second, codes, patch, kept):
        for copy in self.shares:
            copy.wait_recv()
        count = GROUP * SPAN
        position = lax.broadcasted_iota(jnp.int32, (count, self.facts.shape[-1]), 0)
        is_band = lax.rem(position, SPAN) < self.bands
        for g in range(self.n // GROUP):
            generator_forward(self.bands, self.facts, self.frequency, self.token, g, *weights, *kept)
            group = pl.ds(g * count, count)
            second[group] = kept[0][SECOND]
            codes[group] = jnp.where(is_band, kept[0][SECOND] + kept[0][SEQ], 0.0).astype(codes.dtype)
        own = second[pl.ds(pl.multiple_of(self.me * SPAN, SPAN), SPAN)]
        patch[...] = exact(own, patch_w[...])[self.bands : self.bands + 1]

    def make(self, codes, rows):
        n, half, low = self.n, self.w_half.shape[2], jnp.bfloat16
        step = tiled(rows)
        w_rows = self.w_half.reshape(self.w_half.shape[0] * step, half)
        k_rows = self.k32.reshape(n * SPAN * step, half)

        @pl.loop(0, rows // 2)
        def _(j):
            both = [w_rows[pl.ds(2 * j + i, self.w_half.shape[0], stride=step), :].astype(low) for i in range(2)]
            made = dot(codes[...], jnp.concatenate(both, axis=1), NN)
            for i in range(2):
                c = 2 * j + i
                bias = self.b_half[pl.ds(c, 1)]
                k_rows[pl.ds(c, n * SPAN, stride=step), :] = made[:, i * half : (i + 1) * half] + bias

    def ready(self, rows):
        @pl.loop(0, self.n)
        def _(t):
            self.k16[t] = self.k32[t, : self.bands, :rows].astype(self.k16.dtype)

    def sent(self):
        for copy in self.shares:
            copy.wait_send()


def front_kernel(
    n, grid, bands,
    facts_own, frequency, token, w_attn, w_in, w_out, gain, shift, patch_w, kern_w, kern_b, attn, mlp,
    kern_o, attn_o, mlp_o, facts, patch_o, codes_o, rows_o, wide_o, prob_o,
    second, w_half, b_half, k32, k16, local, f_send, f_recv, g_send, g_recv, *a_sems,
):
    me, mp = lax.axis_index("dp"), lax.axis_index("mp")
    rows, half = kern_w.shape[1], kern_w.shape[2] // 2
    load = weight_load(kern_w, w_half, local.at[0], mp)
    own = [
        pltpu.make_async_copy(attn, attn_o.at[me], local.at[1]),
        pltpu.make_async_copy(mlp, mlp_o.at[me], local.at[2]),
    ]
    for copy in own:
        copy.start()
    greet(n, me, mp, False)
    for copy in own:
        copy.wait()
    work = Front(n, grid, bands, facts, frequency, token, w_half, b_half, k32, k16)
    work.share(facts_own, f_send, f_recv)
    gather = Gather(grid, rows, (attn_o, mlp_o), g_send, g_recv)
    for piece in gather.pieces:
        gather.begin(piece)
    work.generate((w_attn, w_in, w_out, gain, shift), patch_w, second, codes_o, patch_o, (rows_o, wide_o, prob_o))
    load.wait()
    b_half[...] = kern_b[:, lanes_at(mp, half)]
    work.make(codes_o, rows)
    work.ready(rows)
    exchange = Exchange(n, grid, k16, lambda source: kern_o.at[source], *a_sems)
    exchange.start()
    for number in range(1, len(grid) + 1):
        for piece in gather.pieces:
            gather.step(piece, number)
    gather.sent(gather.pieces)
    for source in exchange.sources():
        exchange.arrive(source)
    exchange.own.wait()
    exchange.sent()
    work.sent()


def front(n, bands, facts_own, frequency, token, w_attn, w_in, w_out, gain, shift, patch_w, kern_w, kern_b, attn, mlp):
    grid = factors_of(n)
    hyper_width, rows, pixels = kern_w.shape
    half = pixels // 2
    pieces = 2 * len(orders_of(grid))
    f32, low = jnp.float32, jnp.bfloat16
    kept, _ = generator_scratch(hyper_width, w_in.shape[1])
    shapes = [
        ((n, bands, rows, half), low),
        ((n,) + attn.shape, low),
        ((n,) + mlp.shape, low),
        ((n,) + facts_own.shape, low),
        ((1, patch_w.shape[1]), f32),
        ((n * SPAN, hyper_width), low),
    ] + [(k, f32) for k in kept]
    out = pl.pallas_call(
        partial(front_kernel, n, grid, bands),
        out_shape=[jax.ShapeDtypeStruct(*s) for s in shapes],
        in_specs=[VMEM] * 9 + [ANY, VMEM, ANY, ANY],
        out_specs=[ANY] * 3 + [VMEM] * 6,
        scratch_shapes=[
            pltpu.VMEM((n * SPAN, hyper_width), f32),
            pltpu.VMEM((hyper_width, tiled(rows), half), f32),
            pltpu.VMEM((rows, half), f32),
            pltpu.VMEM((n, SPAN, tiled(rows), half), f32),
            pltpu.VMEM((n, bands, rows, half), low),
            pltpu.SemaphoreType.DMA((3,)),
            pltpu.SemaphoreType.DMA((n - 1,)),
            pltpu.SemaphoreType.DMA((n - 1,)),
            pltpu.SemaphoreType.DMA((pieces, n - 1)),
            pltpu.SemaphoreType.DMA((pieces, n)),
        ]
        + exchange_sems(n),
        compiler_params=params(1, BIG_VMEM),
        name="front",
    )(facts_own, frequency, token, w_attn, w_in, w_out, gain, shift, patch_w, kern_w, kern_b, attn, mlp)
    kernel = out[0].transpose(1, 0, 2, 3).reshape(bands, rows * n, half)
    return [kernel, out[1].reshape(n * rows, -1), out[2].reshape(n * rows, -1)] + list(out[3:])


def layer_body(
    inner, hook,
    pix, kern, attn, mlp, cot, band_mask, key_mask, row_scale, patch_bias, gains, shifts, in_bias, out_bias, up_bias, down_bias,
    out_o, emb_grad_o, attn_grad, mlp_grad, small_o, small_up_o, small_in_o,
    emb, mid, part, inbox, norm_a, norm_b, qkv, prob, ctx, act, slope, d_out, d_pre, d_mid, d_att, d_ctx, d_qkv, turned, send, recv,
):
    me, mp = lax.axis_index("dp"), lax.axis_index("mp")
    partner = (me, 1 - mp)
    low = jnp.bfloat16
    bands, tokens, _ = pix.shape
    width = emb.shape[1]
    units = act.shape[1]
    halves = 2
    span = tokens // halves
    tile = 256
    copies = {}

    def swap(i, compute):
        for h in range(halves):
            r = pl.ds(h * span, span)
            if i >= 3:
                copies[i - 3, h].wait_send()

            @pl.loop(0, width // tile)
            def _(j):
                part[i % 3, r, lanes_at(j, tile)] = compute(r, j)

            copies[i, h] = remote(part.at[i % 3, r], inbox.at[i % 3, r], send.at[i, h], recv.at[i, h], partner)

    def swapped(i, h):
        copies[i, h].wait_recv()
        r = pl.ds(h * span, span)
        return part[i % 3, r] + inbox[i % 3, r]

    def embed_terms(r, j):
        total = jnp.zeros((span, tile), jnp.float32)
        for b in range(0, bands, 2):
            both = range(b, min(b + 2, bands))
            left = jnp.concatenate([pix[i, r] * band_mask[i : i + 1].astype(low) for i in both], axis=1)
            right = jnp.concatenate([kern[i, lanes_at(j, tile)] for i in both], axis=1)
            total = total + dot(left, right, NT)
        return total

    hook("start")
    swap(0, embed_terms)
    hook("embedded")
    d_out[...] = (cot[...].astype(jnp.float32) * row_scale[...]).astype(low)
    turned[0] = d_out[...].T
    for h in range(halves):
        r = pl.ds(h * span, span)
        emb[r] = swapped(0, h) + patch_bias[...]
        hat, _ = normed(emb[r], vit_epsilon)
        norm_a[r] = (hat * gains[0:1] + shifts[0:1]).astype(low)

    @pl.loop(0, 3 * inner // 384)
    def _(j):
        cols = lanes_at(j, 384)
        qkv[:, cols] = (dot(norm_a[...], attn[:, cols], NN) + in_bias[:, cols]).astype(low)

    hook("projected")
    wide = 2 * HEAD_DIM
    lane = lax.broadcasted_iota(jnp.int32, (1, wide), 1)
    in_head = [(lane < HEAD_DIM).astype(low), (lane >= HEAD_DIM).astype(low)]
    scale = 1.0 / math.sqrt(HEAD_DIM)
    pairs = inner // wide

    def head_lanes(j, which):
        return pl.ds(pl.multiple_of(which * inner + j * wide, wide), wide)

    @pl.loop(0, pairs)
    def _(j):
        q, k, v = (qkv[:, head_lanes(j, w)] for w in range(3))
        total = jnp.zeros((tokens, wide), jnp.float32)
        for h in range(2):
            scores = jnp.where(key_mask[...] > 0.0, dot(q * in_head[h], k, NT) * scale, -1e30)
            raised = jnp.exp(scores - jnp.max(scores, axis=-1, keepdims=True))
            p = raised / row_sum(raised)
            prob[2 * j + h] = p
            total = total + dot(p.astype(low), v * in_head[h], NN)
        ctx[:, lanes_at(j, wide)] = total.astype(low)

    def out_terms(r, j):
        return dot(ctx[r], attn[lanes_at(j, tile), pl.ds(3 * inner, inner)], NT)

    swap(1, out_terms)
    hook("attended")
    turned[1] = norm_a[...].T
    for h in range(halves):
        r = pl.ds(h * span, span)
        mid[r] = emb[r] + swapped(1, h) + out_bias[...]
        hat, _ = normed(mid[r], vit_epsilon)
        norm_b[r] = (hat * gains[1:2] + shifts[1:2]).astype(low)

    @pl.loop(0, units // tile)
    def _(j):
        cols = lanes_at(j, tile)
        pre = dot(norm_b[...], mlp[:, cols], NN) + up_bias[:, cols]
        phi, density = normal_parts(pre)
        act[:, cols] = (pre * phi).astype(low)
        slope[:, cols] = phi + pre * density

    def down_terms(r, j):
        return dot(act[r], mlp[lanes_at(j, tile), pl.ds(units, units)], NT)

    @pl.loop(0, units // tile)
    def _(j):
        cols = lanes_at(j, tile)
        d_act = dot(d_out[...], mlp[:, pl.ds(pl.multiple_of(units + j * tile, tile), tile)], NN).astype(low)
        d_pre[:, cols] = (d_act.astype(jnp.float32) * slope[:, cols]).astype(low)

    def up_terms(r, j):
        return dot(d_pre[r], mlp[lanes_at(j, tile), pl.ds(0, units)], NT)

    def weight_grad(turned_ref, x, out, start):
        @pl.loop(0, width // tile)
        def _(i):
            for j in range(x.shape[1] // 384):
                out[lanes_at(i, tile), pl.ds(start + j * 384, 384)] = dot(
                    turned_ref[lanes_at(i, tile)], x[:, j * 384 : (j + 1) * 384], NN
                ).astype(low)

    swap(2, up_terms)
    swap(3, down_terms)
    turned[2] = norm_b[...].T
    hook("before feed")
    weight_grad(turned.at[2], d_pre, mlp_grad, 0)
    weight_grad(turned.at[0], act, mlp_grad, units)
    hook("fed")
    small_up_o[...] = column_sums(d_pre[...])
    small_o[5:6] = column_sums(d_out[...])

    def back_through(x, i, h, which):
        hat, r = normed(x, vit_epsilon)
        return norm_back(hat, r, swapped(i, h), gains[which : which + 1])

    sums = []
    for h in range(halves):
        r = pl.ds(h * span, span)
        d_x, gain, shift = back_through(mid[r], 2, h, 1)
        d_x = d_x + d_out[r].astype(jnp.float32)
        d_mid[r] = d_x
        d_att[r] = d_x.astype(low)
        sums.append((gain, shift))
    small_o[1:2] = sums[0][0] + sums[1][0]
    small_o[3:4] = sums[0][1] + sums[1][1]
    small_o[4:5] = column_sums(d_att[...])

    @pl.loop(0, inner // 384)
    def _(j):
        d_ctx[:, lanes_at(j, 384)] = dot(
            d_att[...], attn[:, pl.ds(pl.multiple_of(3 * inner + j * 384, 384), 384)], NN
        ).astype(low)

    @pl.loop(0, pairs)
    def _(j):
        q, k, v = (qkv[:, head_lanes(j, w)] for w in range(3))
        d_c = d_ctx[:, lanes_at(j, wide)]
        d_q = jnp.zeros((tokens, wide), jnp.float32)
        d_k, d_v = d_q, d_q
        for h in range(2):
            p = prob[2 * j + h]
            d_p = dot(d_c * in_head[h], v, NT)
            d_s = (p * (d_p - row_sum(p * d_p))).astype(low)
            d_q = d_q + dot(d_s, k * in_head[h], NN)
            d_k = d_k + dot(d_s, q * in_head[h], TN)
            d_v = d_v + dot(p.astype(low), d_c * in_head[h], TN)
        d_qkv[:, head_lanes(j, 0)] = (d_q * scale).astype(low)
        d_qkv[:, head_lanes(j, 1)] = (d_k * scale).astype(low)
        d_qkv[:, head_lanes(j, 2)] = d_v.astype(low)

    def in_terms(r, j):
        return dot(d_qkv[r], attn[lanes_at(j, tile), pl.ds(0, 3 * inner)], NT)

    swap(4, in_terms)
    hook("before attention")
    weight_grad(turned.at[1], d_qkv, attn_grad, 0)
    turned[2] = d_att[...].T
    weight_grad(turned.at[2], ctx, attn_grad, 3 * inner)
    hook("attention")
    sums = []
    for h in range(halves):
        r = pl.ds(h * span, span)
        d_x, gain, shift = back_through(emb[r], 4, h, 0)
        emb_grad_o[r] = (d_x + d_mid[r]).astype(low)
        sums.append((gain, shift))
    small_o[0:1] = sums[0][0] + sums[1][0]
    small_o[2:3] = sums[0][1] + sums[1][1]
    small_o[6:7] = column_sums(emb_grad_o[...])
    small_o[7:8] = jnp.zeros((1, width), jnp.float32)
    small_in_o[...] = column_sums(d_qkv[...])

    def finish():
        for h in range(halves):
            r = pl.ds(h * span, span)
            out_o[r] = ((mid[r] + swapped(3, h) + down_bias[...]) * row_scale[r]).astype(low)
        for i in range(2, 5):
            for h in range(halves):
                copies[i, h].wait_send()

    return finish


def layer_buffers(inner, units, tokens, width):
    f32, low = jnp.float32, jnp.bfloat16
    return [
        pltpu.VMEM((tokens, width), f32),
        pltpu.VMEM((tokens, width), f32),
        pltpu.VMEM((3, tokens, width), f32),
        pltpu.VMEM((3, tokens, width), f32),
        pltpu.VMEM((tokens, width), low),
        pltpu.VMEM((tokens, width), low),
        pltpu.VMEM((tokens, 3 * inner), low),
        pltpu.VMEM((inner // HEAD_DIM, tokens, tokens), f32),
        pltpu.VMEM((tokens, inner), low),
        pltpu.VMEM((tokens, units), low),
        pltpu.VMEM((tokens, units), f32),
        pltpu.VMEM((tokens, width), low),
        pltpu.VMEM((tokens, units), low),
        pltpu.VMEM((tokens, width), f32),
        pltpu.VMEM((tokens, width), low),
        pltpu.VMEM((tokens, inner), low),
        pltpu.VMEM((tokens, 3 * inner), low),
        pltpu.VMEM((3, width, tokens), low),
        pltpu.SemaphoreType.DMA((5, 2)),
        pltpu.SemaphoreType.DMA((5, 2)),
    ]


LAYER_INS, LAYER_BUFFERS, TURNED = 15, 20, 17


class Scatter:
    def __init__(self, n, grid, rows, attn, mlp, attn_box, mlp_box, outs, send, recv):
        self.me, self.mp = lax.axis_index("dp"), lax.axis_index("mp")
        self.here, self.grid, self.rows = coords(self.me, grid), grid, rows
        self.orders = [order[::-1] for order in orders_of(grid)]
        self.stages = len(grid)
        self.send_sem, self.recv_sem, self.sends = send, recv, []
        self.pieces = []
        for terms, box, out in ((attn, attn_box, outs[:4]), (mlp, mlp_box, outs[4:])):
            for (first, width), order in zip(parts_of(terms.shape[-1], grid), self.orders):
                start, to = 0, []
                for ref in out:
                    low, high = max(start, first), min(start + ref.shape[1], first + width)
                    if low < high:
                        to.append((ref, low - start, low - first, high - low))
                    start += ref.shape[1]
                self.pieces.append((terms, box, to, pl.ds(first, width), order, len(self.pieces)))
        self.slots = {}
        for which, order in enumerate(self.orders):
            number = 0
            for t in range(self.stages):
                for shard in self.rest(order, t):
                    for k in range(1, grid[order[t]]):
                        self.slots[which, t, shard, k] = number
                        number += 1

    def rest(self, order, t):
        return sorted(offsets_in(self.grid, order[t + 1 :]), key=sum, reverse=True)

    def start(self, t, pieces):
        for terms, box, _, cols, order, p in pieces:
            for shard in self.rest(order, t):
                for k in range(1, self.grid[order[t]]):
                    step = along(self.grid, order[t], k)
                    owner = device_at(self.here, self.grid, tuple(i + j for i, j in zip(shard, step)))
                    slot = self.slots[p % len(self.orders), t, shard, self.grid[order[t]] - k]
                    there = (device_at(self.here, self.grid, step), self.mp)
                    block = shard_of(terms, owner, self.rows, cols)
                    self.sends.append(
                        remote(block, box.at[slot, :, cols], self.send_sem.at[p, slot], self.recv_sem.at[p, slot], there)
                    )

    def add(self, t, pieces):
        for terms, box, outs, cols, order, p in pieces:
            for shard in self.rest(order, t):
                block = shard_of(terms, device_at(self.here, self.grid, shard), self.rows, cols)
                total = block[...].astype(jnp.float32)
                for k in range(1, self.grid[order[t]]):
                    slot = self.slots[p % len(self.orders), t, shard, k]
                    arrived(box.at[slot, :, cols], self.recv_sem.at[p, slot])
                    total = total + box[slot, :, cols].astype(jnp.float32)
                if t < self.stages - 1:
                    block[...] = total.astype(terms.dtype)
                else:
                    for ref, to, first, width in outs:
                        ref[:, to : to + width] = total[:, first : first + width]

    def go_on(self, t, pieces):
        if t < self.stages:
            self.add(t, pieces)
            if t + 1 < self.stages:
                self.start(t + 1, pieces)


def generator_gradients(n, bands, recompute, blocks, patch_at, w_attn, w_in, w_out, gain, shift, kept, d_mlp, tails, outs):
    g_attn, g_in, g_out, g_gain, g_shift, g_token, g_patch = outs
    groups = n // GROUP

    def put(ref, where, value):
        ref[where] = value if groups == 1 else ref[where] + value

    if groups > 1:
        for ref in (g_attn, g_in, g_out, g_gain, g_shift):
            ref[...] = jnp.zeros_like(ref)
    width = blocks.shape[2]
    token = jnp.zeros((1, width), jnp.float32)
    for g in range(groups):
        recompute(g)
        d_second = blocks[pl.ds(g * GROUP, GROUP), :SPAN].reshape(GROUP * SPAN, width)
        generator_backward(
            d_second, put, w_attn, w_in, w_out, gain, *kept, d_mlp, (g_attn, g_in, g_out, g_gain, g_shift)
        )
        tails[pl.ds(g * GROUP, GROUP)] = kept[0].at[SECOND][pl.ds(bands, GROUP, stride=SPAN), :]
        token = token + all_rows(d_mlp.at[0][pl.ds(bands, GROUP, stride=SPAN), :])
    g_token[...] = token
    lane = 128
    for i in range(g_patch.shape[1] // lane):
        g_patch[:, i * lane : (i + 1) * lane] = exact(tails[...], blocks[:, patch_at + i, :], TN)


def back_body(
    n, grid, scatter, ordered, finish, gradients, exchange,
    pix, kern, band_mask, emb_grad, small, small_up, small_in, patch_w, codes,
    pixel_o, map_o, blocks_o, bias_o,
    w_half, d_pix, got, got32, code, codes_turned, terms, term_box, vectors, vector_box, bias_half, load, local, f_send, f_recv,
    c_send, c_recv, b_send, b_recv, v_send, v_recv, u_send, u_recv,
):
    me, mp = lax.axis_index("dp"), lax.axis_index("mp")
    partner = (me, 1 - mp)
    low = jnp.bfloat16
    bands, tokens, half = pix.shape
    rows = got.shape[2]
    lanes = lanes_at(mp, half)
    own, to_partner = [], []
    mine, rest = ordered

    exchange.start()
    scatter.start(0, rest)
    scatter.go_on(0, mine)
    finish()

    def pixel_gradients(b, count):
        made = dot(emb_grad[...], jnp.concatenate([kern[b + i] for i in range(count)], axis=1), NN)
        for i in range(count):
            d_pix[b + i] = (made[:, i * half : (i + 1) * half] * band_mask[pl.ds(b + i, 1)]).astype(low)

    pl.loop(0, bands // 2)(lambda j: pixel_gradients(2 * j, 2))
    if bands % 2:
        pixel_gradients(bands - 1, 1)

    own.append(pltpu.make_async_copy(d_pix, pixel_o.at[:, :, lanes], local.at[0]))
    own[-1].start()
    to_partner.append(remote(d_pix, pixel_o.at[:, :, lanes], f_send.at[0], f_recv.at[0], partner))

    lane = 128
    per_slot = vectors.shape[1]
    vectors[...] = jnp.zeros_like(vectors)
    chunks = []
    for r in range(4):
        chunks += [small[r : r + 1, i * lane : (i + 1) * lane] for i in range(small.shape[1] // lane)]
    inner = small_in.shape[1] // 3
    for start in (0, 2 * inner):
        chunks += [small_in[:, start + i * lane : start + (i + 1) * lane] for i in range(inner // lane)]
    chunks += [small[4:5, i * lane : (i + 1) * lane] for i in range(small.shape[1] // lane)]
    chunks += [small_up[:, i * lane : (i + 1) * lane] for i in range(small_up.shape[1] // lane)]
    chunks += [small[5:6, i * lane : (i + 1) * lane] for i in range(small.shape[1] // lane)]
    each = -(-len(chunks) // n)
    for i, chunk in enumerate(chunks):
        vectors[i // each, i % each : i % each + 1] = chunk
    patch_grad = small[6:7]
    d_tail = exact(jnp.broadcast_to(patch_grad, (8, patch_grad.shape[1])), patch_w[...], NT)[:1]
    adding = []
    for k in range(1, n):
        there = lax.rem(me + k, n)
        adding.append(remote(vectors.at[there], vector_box.at[n - k], v_send.at[k], v_recv.at[n - k], (there, mp)))
    codes_turned[...] = codes[...].T

    scatter.go_on(1, mine)
    scatter.go_on(0, rest)
    scatter.go_on(1, rest)

    for copy in adding:
        copy.wait_recv()
    total = vectors[me]
    for k in range(1, n):
        total = total + vector_box[k]
    blocks_o[me, SPAN : SPAN + per_slot] = total
    for i in range(patch_grad.shape[1] // lane):
        r = SPAN + per_slot + i
        blocks_o[me, r : r + 1] = patch_grad[:, i * lane : (i + 1) * lane]
    back = []
    beyond = pl.ds(SPAN, blocks_o.shape[1] - SPAN)
    for k in range(1, n):
        there = lax.rem(me + k, n)
        block = blocks_o.at[me, beyond]
        back.append(remote(block, block, u_send.at[k - 1], u_recv.at[k - 1], (there, mp)))

    bias_half[...] = jnp.zeros_like(bias_half)

    def take(source):
        block = got[source].astype(jnp.float32)
        got32[source, :bands, :rows] = block
        got32[source, bands:, :rows] = jnp.zeros((SPAN - bands,) + block.shape[1:], jnp.float32)
        bias_half[...] = bias_half[...] + jnp.sum(block, axis=0)

    exchange.own.wait()
    take(me)
    for source in exchange.sources():
        exchange.arrive(source)
        take(source)

    if load is not None:
        load.wait()
    step = tiled(rows)
    w_rows = w_half.reshape(w_half.shape[0] * step, half)
    g_rows = got32.reshape(n * SPAN * step, half)
    code[...] = jnp.zeros_like(code)

    @pl.loop(0, rows // 2)
    def _(j):
        taken = [g_rows[pl.ds(2 * j + i, n * SPAN, stride=step), :].astype(low) for i in range(2)]
        weights = [w_rows[pl.ds(2 * j + i, w_half.shape[0], stride=step), :].astype(low) for i in range(2)]
        code[...] = code[...] + dot(jnp.concatenate(taken, axis=1), jnp.concatenate(weights, axis=1), NT)

    terms[...] = code[...].reshape(n, SPAN, code.shape[1]).astype(low)
    sums = []
    for k in range(1, n):
        there = lax.rem(me + k, n)
        slot = n - k
        sums.append(remote(terms.at[there], term_box.at[mp, slot], c_send.at[k], c_recv.at[slot], (there, mp)))
    for k in range(n):
        there = lax.rem(me + k, n)
        slot = (n - k) % n
        sums.append(
            remote(terms.at[there], term_box.at[mp, slot], c_send.at[n + k], c_recv.at[n + slot], (there, 1 - mp))
        )
    term_box[mp, 0] = terms[me]
    bias_o[:, lanes] = bias_half[...]
    to_partner.append(remote(bias_half, bias_o.at[:, lanes], f_send.at[2], f_recv.at[2], partner))

    scatter.go_on(2, mine)
    scatter.go_on(2, rest)
    @pl.loop(0, rows // 2)
    def _(j):
        taken = [g_rows[pl.ds(2 * j + c, n * SPAN, stride=step), :].astype(low) for c in range(2)]
        both = dot(codes_turned[...], jnp.concatenate(taken, axis=1), NN)
        for c in range(2):
            w_rows[pl.ds(2 * j + c, w_half.shape[0], stride=step), :] = both[:, c * half : (c + 1) * half]

    filled = first_rows(w_half, rows)
    to_partner.append(remote(filled, map_o.at[mp], f_send.at[1], f_recv.at[1], partner))
    own.append(pltpu.make_async_copy(filled, map_o.at[mp], local.at[1]))
    own[-1].start()

    for copy in sums:
        copy.wait_recv()
    total = term_box[0, 0].astype(jnp.float32)
    for i in range(1, 2 * n):
        total = total + term_box[i // n, i % n].astype(jnp.float32)
    is_tail = lax.broadcasted_iota(jnp.int32, total.shape, 0) == bands
    blocks_o[me, :SPAN] = jnp.where(is_tail, d_tail, total)
    for k in range(1, n):
        there = lax.rem(me + k, n)
        block = blocks_o.at[me, pl.ds(0, SPAN)]
        back.append(remote(block, block, b_send.at[k - 1], b_recv.at[k - 1], (there, mp)))
    for copy in back:
        copy.wait_recv()
    gradients(blocks_o, SPAN + per_slot)
    for t in range(3, scatter.stages):
        scatter.go_on(t, mine + rest)
    for copy in to_partner:
        copy.wait()
    for copy in sums + adding + back + scatter.sends:
        copy.wait_send()
    exchange.sent()
    for copy in own:
        copy.wait()


GENERATOR_OUTS = tuple(dict(
    g_attn=0, g_in=0, g_out=0, g_gain=0, g_shift=0, g_token=0, g_patch=0,
))


def rows_per_slot(n, width, inner, units):
    chunks = (6 * width + 2 * inner + units) // 128
    return -(-(-(-chunks // n)) // 8) * 8


def back_shapes(n, bands, tokens, rows, half, width, inner, units, hyper_width, hyper_units):
    f32, low = jnp.float32, jnp.bfloat16
    per_slot = rows_per_slot(n, width, inner, units)
    block = SPAN + per_slot + width // 128 + -(width // 128) % 8
    part, whole_row = ((rows, inner), f32), ((rows, units), f32)
    outs = dict(
        g_q=part, g_k=part, g_v=part, g_proj=part, g_up=whole_row, g_down=whole_row, pixel_o=((bands, tokens, 2 * half), low),
        map_o=((2, hyper_width, rows, half), f32), blocks_o=((n, block, 128), f32), bias_o=((rows, 2 * half), f32),
    )
    square = (2, hyper_width)
    shapes = [(4, hyper_width, hyper_width), (hyper_width, hyper_units), (hyper_units, hyper_width), square, square]
    shapes += [(1, hyper_width), (hyper_width, width)]
    outs.update({k: (v, f32) for k, v in zip(GENERATOR_OUTS, shapes)})
    specs = [ANY if k in dict(pixel_o=0, map_o=0) else VMEM for k in outs]
    buffers = dict(
        w_half=pltpu.VMEM((hyper_width, tiled(rows), half), f32),
        d_pix=pltpu.VMEM((bands, tokens, half), low),
        got=pltpu.VMEM((n, bands, rows, half), low),
        got32=pltpu.VMEM((n, SPAN, tiled(rows), half), f32),
        code=pltpu.VMEM((n * SPAN, hyper_width), f32),
        codes_turned=pltpu.VMEM((hyper_width, n * SPAN), low),
        terms=pltpu.VMEM((n, SPAN, hyper_width), low),
        term_box=pltpu.VMEM((2, n, SPAN, hyper_width), low),
        vectors=pltpu.VMEM((n, per_slot, 128), f32),
        vector_box=pltpu.VMEM((n, per_slot, 128), f32),
        bias_half=pltpu.VMEM((rows, half), f32),
    )
    sems = dict(
        blocal=(2,), p_send=(3,), p_recv=(3,), c_send=(2 * n,), c_recv=(2 * n,), b_send=(n - 1,),
        b_recv=(n - 1,), v_send=(n,), v_recv=(n,), u_send=(n - 1,), u_recv=(n - 1,),
    )
    buffers.update({k: pltpu.SemaphoreType.DMA(v) for k, v in sems.items()})
    return outs, specs, buffers


BACK = tuple(dict(
    w_half=0, d_pix=0, got=0, got32=0, code=0, codes_turned=0, terms=0, term_box=0, vectors=0, vector_box=0,
    bias_half=0,
))
BACK_SEMS = tuple(dict(
    blocal=0, p_send=0, p_recv=0, c_send=0, c_recv=0, b_send=0, b_recv=0, v_send=0, v_recv=0, u_send=0, u_recv=0,
))


def scatter_buffers(n, grid, rows, attn_lanes, mlp_lanes):
    low, pieces = jnp.bfloat16, 2 * len(orders_of(grid))
    slots = n - 1
    return [
        pltpu.VMEM((slots, rows, attn_lanes), low),
        pltpu.VMEM((slots, rows, mlp_lanes), low),
        pltpu.SemaphoreType.DMA((pieces, slots)),
        pltpu.SemaphoreType.DMA((pieces, slots)),
    ]


def weight_load(kern_w, w_half, sem, mp):
    half = w_half.shape[2]
    copy = pltpu.make_async_copy(kern_w.at[:, :, lanes_at(mp, half)], first_rows(w_half, kern_w.shape[1]), sem)
    copy.start()
    return copy


def whole_kernel(n, grid, names, *refs):
    r = Refs(names, refs)
    me, mp = lax.axis_index("dp"), lax.axis_index("mp")
    low, f32 = jnp.bfloat16, jnp.float32
    bands, tokens, half = r.pix.shape
    rows, inner = r.attn_out.shape
    units = r.mlp_in.shape[1]
    load = weight_load(r.kern_weight, r.w_half, r.local.at[0], mp)
    lanes = lanes_at(mp, half)
    pix_load = pltpu.make_async_copy(r.pixels.at[0, :, :, lanes], r.pix, r.local.at[1])
    pix_load.start()

    mine = pl.ds(pl.multiple_of(me * rows, 16), rows)
    for i in range(3):
        r.attn[mine, i * inner : (i + 1) * inner] = r.attn_in[i].astype(low)
    r.attn[mine, 3 * inner :] = r.attn_out[...].astype(low)
    r.mlp[mine, :units] = r.mlp_in[...].astype(low)
    r.mlp[mine, units:] = r.mlp_out[...].astype(low)
    count = r.band_count[0]
    r.facts_own[...] = wave_rows([r.wavelengths[0, b] for b in range(bands)], count)

    greet(n, me, mp, True)
    work = Front(n, grid, bands, r.facts, r.frequency, r.bias_token, r.w_half, r.b_half, r.k32, r.k16)
    work.share(r.facts_own, r.f_send, r.f_recv)
    gather = Gather(grid, rows, (r.attn, r.mlp), r.w_send, r.w_recv)
    split = len(gather.pieces) // 2
    attn_pieces, mlp_pieces = gather.pieces[:split], gather.pieces[split:]
    for piece in gather.pieces:
        gather.begin(piece)

    r.in_bias[...] = jnp.zeros_like(r.in_bias)
    r.in_bias[:, :inner] = r.attn_in_bias[0:1]
    r.in_bias[:, 2 * inner :] = r.attn_in_bias[1:2]
    r.out_bias[...] = r.attn_out_bias[...].reshape(r.out_bias.shape)
    r.up_bias[...] = r.mlp_in_bias[...].reshape(r.up_bias.shape)
    r.down_bias[...] = r.mlp_out_bias[...].reshape(r.down_bias.shape)
    r.b_half[...] = r.kern_bias[:, lanes]
    size = r.size_class[0]
    live = jnp.where(size == 0, tokens * 49 // 256, jnp.where(size == 1, tokens * 196 // 256, tokens))
    column = lax.broadcasted_iota(jnp.int32, (1, tokens), 1)
    r.key_mask[...] = ((column < live) & ((r.token_keep[...] == 1) | (column == 0))).astype(f32)
    r.row_scale[...] = (lax.broadcasted_iota(jnp.int32, (tokens, 1), 0) < live).astype(f32)
    r.band_mask[...] = (lax.broadcasted_iota(jnp.int32, r.band_mask.shape, 0) < count).astype(f32)

    kept = (r.rows, r.wide, r.prob.at[pl.ds(0, HYP_HEADS)])
    weights = (r.hyp_attn, r.hyp_mlp_in, r.hyp_mlp_out, r.hyp_gain, r.hyp_shift)
    work.generate(weights, r.patch_w, r.second, r.codes, r.patch_bias, kept)
    saves = []
    for i, (src, dst) in enumerate(zip(kept[1:], (r.wide_o, r.prob_o))):
        saves.append(pltpu.make_async_copy(src, dst, r.local.at[2 + i]))
        saves[-1].start()
    for piece in attn_pieces:
        gather.step(piece, 1)
    for piece in mlp_pieces:
        gather.step(piece, 1)
    load.wait()
    work.make(r.codes, rows)
    work.ready(rows)

    def kern_of(source):
        return r.kern.at[:, pl.ds(pl.multiple_of(rows * source, 16), rows)]

    fetch = Exchange(n, grid, r.k16, kern_of, r.k_send, r.k_recv, r.k_own)
    fetch.start()
    for number in range(2, len(grid) + 1):
        for piece in attn_pieces:
            gather.step(piece, number)
    pix_load.wait()
    for copy in saves:
        copy.wait()
    fetch.own.wait()
    for source in fetch.sources():
        fetch.arrive(source)

    scatter = Scatter(
        n, grid, rows, r.attn, r.mlp, r.attn_box, r.mlp_box,
        (r.g_q, r.g_k, r.g_v, r.g_proj, r.g_up, r.g_down), r.g_send, r.g_recv,
    )
    scatter_attn, scatter_mlp = scatter.pieces[:split], scatter.pieces[split:]

    def hook(at):
        if at in ("start", "embedded", "attended"):
            number = ("start", "embedded", "attended").index(at) + 2
            for number in range(number, number + 1 if at != "attended" else len(grid) + 1):
                for piece in mlp_pieces:
                    gather.step(piece, number)
        if at == "before feed":
            gather.sent(mlp_pieces)
        if at == "fed":
            scatter.start(0, scatter_mlp)
        if at == "before attention":
            gather.sent(attn_pieces)

    model = r.emb.shape[1]
    slope, mid, d_mid = r.wide.at[0, :, pl.ds(0, units)], r.wide.at[1, :, pl.ds(0, model)], r.wide.at[1, :, pl.ds(model, model)]
    finish = layer_body(
        inner, hook,
        r.pix, r.kern, r.attn, r.mlp, r.cotangent.at[0], r.band_mask, r.key_mask, r.row_scale, r.patch_bias, r.norm_gain,
        r.norm_shift, r.in_bias, r.out_bias, r.up_bias, r.down_bias,
        r.out_o, r.emb_grad, r.attn, r.mlp, r.small, r.small_up, r.small_in,
        r.emb, mid, r.part, r.inbox, r.norm_a, r.norm_b, r.qkv, r.prob, r.ctx, r.act, slope, r.d_out, r.d_pre, d_mid, r.d_att,
        r.d_ctx, r.d_qkv, r.turned, r.s_send, r.s_recv,
    )
    work.sent()
    fetch.sent()
    r.turned[2] = r.emb_grad[...].T
    tile = 2 * rows * (256 // (2 * rows)) if model % (2 * rows * (256 // (2 * rows))) == 0 else rows

    def kernel_gradients(b, bands_here):
        masked = [r.pix[b + i] * r.band_mask[pl.ds(b + i, 1)].astype(low) for i in range(bands_here)]
        masked = jnp.concatenate(masked, axis=1)
        for i in range(model // tile):
            made = dot(r.turned[2, i * tile : (i + 1) * tile], masked, NN).astype(low)
            for t in range(tile // rows):
                for c in range(bands_here):
                    part = made[t * rows : (t + 1) * rows, c * half : (c + 1) * half]
                    r.k16[i * (tile // rows) + t, b + c] = part

    pl.loop(0, bands // 2)(lambda j: kernel_gradients(2 * j, 2))
    if bands % 2:
        kernel_gradients(bands - 1, 1)

    exchange = Exchange(n, grid, r.k16, lambda source: r.got.at[source], r.a_send, r.a_recv, r.a_own)
    loads = []

    def finish_layer():
        finish()
        for i, (src, dst) in enumerate(zip((r.wide_o, r.prob_o), kept[1:])):
            loads.append(pltpu.make_async_copy(src, dst, r.local.at[2 + i]))
            loads[-1].start()

    def gradients(blocks, patch_at):
        for copy in loads:
            copy.wait()
        outs = [getattr(r, k) for k in GENERATOR_OUTS]
        generator_gradients(n, bands, recompute, blocks, patch_at, *weights, kept, r.d_mlp, r.tails, outs)

    def recompute(g):
        if n > GROUP:
            generator_forward(bands, r.facts, r.frequency, r.bias_token, g, *weights, *kept)

    back_body(
        n, grid, scatter, (scatter_mlp, scatter_attn), finish_layer, gradients, exchange,
        r.pix, r.kern, r.band_mask, r.emb_grad, r.small, r.small_up, r.small_in, r.patch_w, r.codes,
        r.pixel_o, r.map_o, r.blocks_o, r.bias_o,
        r.w_half, r.pix, r.got, r.k32, *[getattr(r, k) for k in BACK[4:]], None, *[getattr(r, k) for k in BACK_SEMS],
    )


def whole(n, **arguments):
    a = Refs(arguments, arguments.values())
    f32, low, dma = jnp.float32, jnp.bfloat16, pltpu.SemaphoreType.DMA
    grid = factors_of(n)
    _, bands, tokens, pixels = a.pixels.shape
    half = pixels // 2
    rows, inner = a.attn_out.shape
    units = a.mlp_in.shape[1]
    width = a.norm_gain.shape[1]
    hyper_width, hyper_units = a.hyp_mlp_in.shape
    outs, specs, buffers = back_shapes(n, bands, tokens, rows, half, width, inner, units, hyper_width, hyper_units)
    kept, _ = generator_scratch(hyper_width, hyper_units)
    outs = dict(out_o=((tokens, width), low)) | outs | dict(wide_o=(kept[1], f32), prob_o=(kept[2], f32))
    specs = [VMEM] + specs + [ANY, ANY]
    pieces = 2 * len(orders_of(grid))
    slots = n - 1
    scratch = dict(
        pix=((bands, tokens, half), low),
        attn=((width, 4 * inner), low),
        mlp=((width, 2 * units), low),
        kern=((bands, width, half), low),
        facts_own=((SPAN, hyper_width), low),
        facts=((n, SPAN, hyper_width), low),
        b_half=((rows, half), f32),
        k32=((n, SPAN, rows, half), f32),
        k16=((n, bands, rows, half), low),
        rows=(kept[0], f32),
        wide=(kept[1], f32),
        prob=((max(HYP_HEADS, inner // HEAD_DIM), tokens, tokens), f32),
        second=((n * SPAN, hyper_width), f32),
        codes=((n * SPAN, hyper_width), low),
        d_mlp=((2, GROUP * SPAN, hyper_width), f32),
        tails=((n, hyper_width), f32),
        patch_bias=((1, width), f32),
        in_bias=((1, 3 * inner), f32),
        out_bias=((1, width), f32),
        up_bias=((1, units), f32),
        down_bias=((1, width), f32),
        key_mask=((1, tokens), f32),
        row_scale=((tokens, 1), f32),
        band_mask=((SPAN, half), f32),
        emb=((tokens, width), f32),
        part=((3, tokens, width), f32),
        inbox=((3, tokens, width), f32),
        norm_a=((tokens, width), low),
        norm_b=((tokens, width), low),
        qkv=((tokens, 3 * inner), low),
        ctx=((tokens, inner), low),
        act=((tokens, units), low),
        d_out=((tokens, width), low),
        d_pre=((tokens, units), low),
        d_att=((tokens, width), low),
        d_ctx=((tokens, inner), low),
        d_qkv=((tokens, 3 * inner), low),
        turned=((3, width, tokens), low),
        emb_grad=((tokens, width), low),
        small=((8, width), f32),
        small_up=((1, units), f32),
        small_in=((1, 3 * inner), f32),
        attn_box=((slots, rows, 4 * inner), low),
        mlp_box=((slots, rows, 2 * units), low),
    )
    scratch = {k: pltpu.VMEM(*v) for k, v in scratch.items()}
    shared = dict(d_pix=0, got32=0)
    scratch.update({k: v for k, v in buffers.items() if k not in shared})
    scratch.update(zip(dict(k_send=0, k_recv=0, k_own=0), exchange_sems(n)))
    scratch.update(zip(dict(a_send=0, a_recv=0, a_own=0), exchange_sems(n)))
    sems = dict(
        local=(4,), f_send=(n - 1,), f_recv=(n - 1,), w_send=(pieces, n - 1), w_recv=(pieces, n),
        s_send=(5, 2), s_recv=(5, 2), g_send=(pieces, slots), g_recv=(pieces, slots),
    )
    names = [*arguments, *outs, *scratch, *sems]
    smem = pl.BlockSpec(memory_space=pltpu.SMEM)
    places = dict(pixels=ANY, kern_weight=ANY, band_count=smem, wavelengths=smem, size_class=smem)
    flops = 2 * tokens * width * (3 * bands * half + 9 * inner * 2 + 9 * units)
    out = pl.pallas_call(
        partial(whole_kernel, n, grid, names),
        out_shape=[jax.ShapeDtypeStruct(*o) for o in outs.values()],
        in_specs=[places.get(k, VMEM) for k in arguments],
        out_specs=specs,
        scratch_shapes=list(scratch.values()) + [dma(v) for v in sems.values()],
        compiler_params=params(6, BIG_VMEM),
        cost_estimate=pl.CostEstimate(flops=flops, bytes_accessed=3 * 10**7, transcendentals=10**6),
        name="whole",
    )(*arguments.values())
    return dict(zip(outs, out))


def layer_kernel(inner, *refs):
    me, mp = lax.axis_index("dp"), lax.axis_index("mp")
    sem = pltpu.get_barrier_semaphore()
    pl.semaphore_signal(sem, inc=1, device_id=(me, 1 - mp), device_id_type=MESH)
    pl.semaphore_wait(sem, 1)
    layer_body(inner, lambda at: None, *refs)()


BACK_INS = tuple(dict(
    pix=0, kern=0, band_mask=0, emb_grad=0, small=0, small_up=0, small_in=0, patch_w=0, codes=0, facts=0,
    frequency=0, token=0, w_attn=0, w_in=0, w_out=0, gain=0, shift=0, attn=0, mlp=0, d_kern=0, kern_w=0,
))


def back_kernel(n, grid, names, *refs):
    r = Refs(names, refs)
    me, mp = lax.axis_index("dp"), lax.axis_index("mp")
    load = weight_load(r.kern_w, r.w_half, r.load_sem.at[0], mp)
    terms = []
    for i, (src, dst) in enumerate(((r.attn, r.attn_acc), (r.mlp, r.mlp_acc))):
        terms.append(pltpu.make_async_copy(src, dst, r.load_sem.at[1 + i]))
        terms[-1].start()
    greet(n, me, mp, True)
    outs = (r.g_q, r.g_k, r.g_v, r.g_proj, r.g_up, r.g_down)
    for copy in terms:
        copy.wait()
    scatter = Scatter(
        n, grid, r.attn.shape[1], r.attn_acc, r.mlp_acc, r.attn_box, r.mlp_box, outs, r.g_send, r.g_recv
    )
    scatter.start(0, scatter.pieces)
    exchange = Exchange(n, grid, r.d_kern, lambda source: r.got.at[source], r.a_send, r.a_recv, r.a_own)
    weights = (r.w_attn, r.w_in, r.w_out, r.gain, r.shift)
    kept = (r.rows, r.wide, r.prob)
    bands = r.pix.shape[0]

    def recompute(g):
        generator_forward(bands, r.facts, r.frequency, r.token, g, *weights, *kept)

    def gradients(blocks, patch_at):
        outs = [getattr(r, k) for k in GENERATOR_OUTS]
        generator_gradients(n, bands, recompute, blocks, patch_at, *weights, kept, r.d_mlp, r.tails, outs)

    back_body(
        n, grid, scatter, (scatter.pieces, []), lambda: None, gradients, exchange,
        r.pix, r.kern, r.band_mask, r.emb_grad, r.small, r.small_up, r.small_in, r.patch_w, r.codes,
        r.pixel_o, r.map_o, r.blocks_o, r.bias_o, *[getattr(r, k) for k in BACK], load, *[getattr(r, k) for k in BACK_SEMS],
    )


def layer_and_back(n, inner, kern_w, patch_w, layer_ins, generator):
    pix, kern, attn, mlp, _, band_mask = layer_ins[:6]
    grid = factors_of(n)
    bands, tokens, half = pix.shape
    width, units = attn.shape[0], mlp.shape[1] // 2
    hyper_width, rows, _ = kern_w.shape
    hyper_units = generator["w_in"].shape[1]
    f32, low = jnp.float32, jnp.bfloat16
    shape, dma = jax.ShapeDtypeStruct, pltpu.SemaphoreType.DMA
    outs, specs, buffers = back_shapes(n, bands, tokens, rows, half, width, inner, units, hyper_width, hyper_units)
    layer_outs = [
        ((tokens, width), low),
        (attn.shape, low),
        (mlp.shape, low),
        ((8, width), f32),
        ((1, units), f32),
        ((1, 3 * inner), f32),
    ]
    layer_out, emb_grad, attn_grad, mlp_grad, small, small_up, small_in = pl.pallas_call(
        partial(layer_kernel, inner),
        out_shape=[shape((tokens, width), low)] + [shape(*o) for o in layer_outs],
        in_specs=[VMEM] * LAYER_INS,
        out_specs=[VMEM] * 7,
        scratch_shapes=layer_buffers(inner, units, tokens, width),
        compiler_params=params(3, BIG_VMEM),
        name="layer",
    )(*layer_ins)
    d_kern = fast_einsum("tc,btp->bcp", emb_grad, pix * band_mask[:bands, None].astype(low)).astype(low)
    d_kern = d_kern.reshape(bands, n, rows, half).transpose(1, 0, 2, 3)
    attn_grad, mlp_grad = attn_grad.reshape(n, rows, -1), mlp_grad.reshape(n, rows, -1)
    ins = dict(
        pix=pix, kern=kern, band_mask=band_mask, emb_grad=emb_grad, small=small, small_up=small_up, small_in=small_in,
        attn=attn_grad, mlp=mlp_grad, patch_w=patch_w, d_kern=d_kern, kern_w=kern_w, **generator,
    )
    kept, _ = generator_scratch(hyper_width, hyper_units)
    scratch = dict(attn_acc=pltpu.VMEM(attn_grad.shape, low), mlp_acc=pltpu.VMEM(mlp_grad.shape, low))
    scratch.update(
        zip(dict(attn_box=0, mlp_box=0, g_send=0, g_recv=0), scatter_buffers(n, grid, rows, attn.shape[1], mlp.shape[1]))
    )
    scratch.update(zip(dict(a_send=0, a_recv=0, a_own=0), exchange_sems(n)))
    scratch.update({k: pltpu.VMEM(v, f32) for k, v in zip(dict(rows=0, wide=0, prob=0), kept)})
    scratch.update(
        d_mlp=pltpu.VMEM((2, GROUP * SPAN, hyper_width), f32), tails=pltpu.VMEM((n, hyper_width), f32), load_sem=dma((3,))
    )
    scratch.update(buffers)
    out = pl.pallas_call(
        partial(back_kernel, n, grid, [*BACK_INS, *outs, *scratch]),
        out_shape=[shape(*o) for o in outs.values()],
        in_specs=[VMEM] * (len(BACK_INS) - 4) + [ANY] * 4,
        out_specs=specs,
        scratch_shapes=list(scratch.values()),
        compiler_params=params(2, BIG_VMEM),
        name="back",
    )(*[ins[k] for k in BACK_INS])
    return dict(out_o=layer_out) | dict(zip(outs, out))


PASSED = tuple(dict(
    out_o=0, pixel_o=0, g_q=0, g_k=0, g_v=0, g_proj=0, g_up=0, g_down=0, bias_o=0, g_in=0, g_out=0, g_attn=0,
    g_patch=0,
))
SMALL = tuple(dict(
    blocks_o=0, g_gain=0, g_shift=0, g_token=0,
))


def tail_kernel(per_slot, names, *refs):
    r = Refs(names, refs)
    loads, stores = [], []
    for i in range(2):
        loads.append(pltpu.make_async_copy(r.map_o.at[i], r.via_map.at[i], r.load.at[i]))
    for i, name in enumerate(PASSED):
        loads.append(pltpu.make_async_copy(getattr(r, name), getattr(r, "via_" + name), r.load.at[2 + i]))
    for copy in loads:
        copy.start()
    r.gain_p[...] = r.g_gain[...]
    r.shift_p[...] = r.g_shift[...]
    r.token_p[...] = r.g_token[...].reshape(r.token_p.shape)
    lane = 128
    chunks = []
    for ref, which in ((r.n_gain, 0), (r.n_gain, 1), (r.n_shift, 0), (r.n_shift, 1), (r.in_bias, 0), (r.in_bias, 1)):
        chunks += [(ref, which, i) for i in range(ref.shape[1] // lane)]
    for ref in (r.out_bias, r.up_bias, r.down_bias):
        chunks += [(ref, None, i) for i in range(ref.shape[0] // lane)]
    each = -(-len(chunks) // r.blocks_o.shape[0])
    for k, (ref, which, i) in enumerate(chunks):
        at = SPAN + k % each
        if which is None:
            ref[pl.ds(i * lane, lane)] = r.blocks_o[k // each, at]
        else:
            ref[which : which + 1, i * lane : (i + 1) * lane] = r.blocks_o[k // each, at : at + 1]
    half = r.map_p.shape[2] // 2
    sources = [r.via_map.at[0], r.via_map.at[1]] + [getattr(r, "via_" + k) for k in PASSED]
    targets = [r.map_p.at[:, :, pl.ds(i * half, half)] for i in range(2)]
    targets += [r.out_p, r.pixel_p, r.in_p.at[0], r.in_p.at[1], r.in_p.at[2], r.proj_p, r.up_p, r.down_p, r.bias_p]
    targets += [r.w_in_p, r.w_out_p, r.w_attn_p, r.patch_p]
    for i, (load, src, dst) in enumerate(zip(loads, sources, targets, strict=True)):
        load.wait()
        stores.append(pltpu.make_async_copy(src, dst, r.store.at[i]))
        stores[-1].start()
    for copy in stores:
        copy.wait()


def tail(made):
    m = Refs(made, made.values())
    f32, low = jnp.float32, jnp.bfloat16
    n = m.blocks_o.shape[0]
    (rows, inner), units = m.g_proj.shape, m.g_up.shape[1]
    hyper_width, width = m.g_patch.shape
    half = m.map_o.shape[3]
    outs = dict(
        gain_p=m.g_gain.shape, shift_p=m.g_shift.shape, token_p=(hyper_width,), n_gain=(2, width),
        n_shift=(2, width), in_bias=(2, inner), out_bias=(width,), up_bias=(units,), down_bias=(width,),
    )
    outs = {k: (v, f32) for k, v in outs.items()}
    direct = dict(
        map_p=((hyper_width, rows, 2 * half), f32), out_p=(m.out_o.shape, low),
        pixel_p=(m.pixel_o.shape, low), in_p=((3, rows, inner), f32), proj_p=((rows, inner), f32),
        up_p=((rows, units), f32), down_p=((rows, units), f32), bias_p=((rows, 2 * half), f32),
        w_in_p=(m.g_in.shape, f32), w_out_p=(m.g_out.shape, f32), w_attn_p=(m.g_attn.shape, f32),
        patch_p=(m.g_patch.shape, f32),
    )
    scratch = {"via_" + k: (made[k].shape, made[k].dtype) for k in PASSED}
    scratch.update(via_map=(m.map_o.shape, f32))
    far = tuple(dict(map_o=0)) + PASSED
    names = [*SMALL, *far, *outs, *direct, *scratch, "load", "store"]
    results = pl.pallas_call(
        partial(tail_kernel, rows_per_slot(n, width, inner, units), names),
        out_shape=[jax.ShapeDtypeStruct(*v) for v in (outs | direct).values()],
        in_specs=[VMEM] * len(SMALL) + [ANY] * len(far),
        out_specs=[VMEM] * len(outs) + [ANY] * len(direct),
        scratch_shapes=[pltpu.VMEM(*v) for v in scratch.values()] + [pltpu.SemaphoreType.DMA((len(far) + 1,))] * 2,
        compiler_params=pltpu.CompilerParams(vmem_limit_bytes=BIG_VMEM),
        name="tail",
    )(*[made[k] for k in SMALL + far])
    return Refs(outs | direct, results)


def fast_einsum(pattern, left_side, right_side):
    return jnp.einsum(pattern, left_side, right_side, preferred_element_type=jnp.float32)


def in_parts(
    n, pixels, band_count, wavelengths, size_class, token_keep, hyp_attn, hyp_mlp_in, hyp_mlp_out, hyp_gain, hyp_shift, bias_token,
    kern_weight, kern_bias, patch_w, norm_gain, norm_shift, attn_in, attn_in_bias, attn_out, attn_out_bias, mlp_in, mlp_in_bias,
    mlp_out, mlp_out_bias, cotangent, frequency,
):
    mp = lax.axis_index("mp")
    _, bands, tokens, pix_size = pixels.shape
    hyper_width = hyp_attn.shape[1]
    half = pix_size // 2
    low = jnp.bfloat16
    inner = attn_in.shape[2]
    band_valid = jnp.arange(SPAN) < band_count[0]
    facts_own = wave_rows([wavelengths[0, b] for b in range(bands)], band_count[0])

    attn_shard = jnp.concatenate([attn_in[0], attn_in[1], attn_in[2], attn_out], axis=1).astype(low)
    mlp_shard = jnp.concatenate([mlp_in, mlp_out], axis=1).astype(low)
    weights = (hyp_attn, hyp_mlp_in, hyp_mlp_out, hyp_gain, hyp_shift)
    kernel, attn_all, mlp_all, facts, patch_bias, codes, *_ = front(
        n, bands, facts_own, frequency, bias_token, *weights, patch_w, kern_weight, kern_bias, attn_shard, mlp_shard
    )
    live_rows = jnp.where(
        size_class[0] == 0, tokens * 49 // 256, jnp.where(size_class[0] == 1, tokens * 196 // 256, tokens)
    )
    position = jnp.arange(tokens)
    row_valid = position < live_rows
    key_valid = row_valid & ((token_keep[0] == 1) | (position == 0))
    input_bias = jnp.concatenate([attn_in_bias[0], jnp.zeros_like(attn_in_bias[0]), attn_in_bias[1]])
    layer_ins = (
        lax.dynamic_slice_in_dim(pixels[0], mp * half, half, 2),
        kernel,
        attn_all,
        mlp_all,
        cotangent[0],
        jnp.broadcast_to(band_valid.astype(jnp.float32)[:, None], (SPAN, half)),
        key_valid.astype(jnp.float32)[None],
        row_valid.astype(jnp.float32)[:, None],
        patch_bias,
        norm_gain,
        norm_shift,
        input_bias[None],
        attn_out_bias[None],
        mlp_in_bias[None],
        mlp_out_bias[None],
    )
    generator = dict(
        codes=codes, facts=facts, frequency=frequency, token=bias_token, w_attn=hyp_attn, w_in=hyp_mlp_in, w_out=hyp_mlp_out,
        gain=hyp_gain, shift=hyp_shift,
    )
    return layer_and_back(n, inner, kern_weight, patch_w, layer_ins, generator)


def per_device(
    n,
    pixels,
    band_count,
    wavelengths,
    size_class,
    token_keep,
    hyp_attn,
    hyp_mlp_in,
    hyp_mlp_out,
    hyp_gain,
    hyp_shift,
    bias_token,
    kern_weight,
    kern_bias,
    patch_bias_weight,
    norm_gain,
    norm_shift,
    attn_in,
    attn_in_bias,
    attn_out,
    attn_out_bias,
    mlp_in,
    mlp_in_bias,
    mlp_out,
    mlp_out_bias,
    cotangent,
):
    slot_count, bands = pixels.shape[:2]
    assert slot_count == 1 and n % GROUP == 0 and bands + 1 <= SPAN
    arguments = dict(
        pixels=pixels, band_count=band_count, wavelengths=wavelengths, size_class=size_class, token_keep=token_keep,
        hyp_attn=hyp_attn, hyp_mlp_in=hyp_mlp_in, hyp_mlp_out=hyp_mlp_out, hyp_gain=hyp_gain, hyp_shift=hyp_shift,
        bias_token=bias_token, kern_weight=kern_weight, kern_bias=kern_bias, patch_w=patch_bias_weight, norm_gain=norm_gain,
        norm_shift=norm_shift, attn_in=attn_in, attn_in_bias=attn_in_bias, attn_out=attn_out, attn_out_bias=attn_out_bias,
        mlp_in=mlp_in, mlp_in_bias=mlp_in_bias, mlp_out=mlp_out, mlp_out_bias=mlp_out_bias, cotangent=cotangent,
    )
    half_width = hyp_attn.shape[1] // 2
    frequency = 10000.0 ** (-np.arange(half_width, dtype=np.float32) * 2.0 / (2 * half_width))
    frequency = jnp.asarray(np.concatenate([frequency, frequency])[None].astype(np.float32))
    make = whole if kern_weight.shape[1] % 16 == 0 else in_parts
    done = tail(make(n, frequency=frequency, **arguments))
    return (
        done.out_p[None],
        done.pixel_p[None],
        done.w_attn_p,
        done.w_in_p,
        done.w_out_p,
        done.gain_p,
        done.shift_p,
        done.token_p,
        done.map_p,
        done.bias_p,
        done.patch_p,
        done.n_gain,
        done.n_shift,
        done.in_p,
        done.in_bias,
        done.proj_p,
        done.out_bias,
        done.up_p,
        done.up_bias,
        done.down_p,
        done.down_bias,
    )


def solution(mesh):
    return jax.shard_map(
        partial(per_device, mesh.shape["dp"]),
        mesh=mesh,
        in_specs=(
            P("dp", None, None, None),
            P("dp"),
            P("dp", None),
            P("dp"),
            P("dp", None),
            P(),
            P(),
            P(),
            P(),
            P(),
            P(),
            P(None, "dp", None),
            P("dp", None),
            P(),
            P(),
            P(),
            P(None, "dp", "mp"),
            P(None, "mp"),
            P("dp", "mp"),
            P(),
            P("dp", "mp"),
            P("mp"),
            P("dp", "mp"),
            P(),
            P("dp", None, None),
        ),
        out_specs=(
            P("dp", None, None),
            P("dp", None, None, None),
            P(),
            P(),
            P(),
            P(),
            P(),
            P(),
            P(None, "dp", None),
            P("dp", None),
            P(),
            P(),
            P(),
            P(None, "dp", "mp"),
            P(None, "mp"),
            P("dp", "mp"),
            P(),
            P("dp", "mp"),
            P("mp"),
            P("dp", "mp"),
            P(),
        ),
        check_vma=False,
    )
```
